512 devices in a mesh: ctx: 16 (over y, core), exp: 32 (over z, x).
Axes of the slice: x: 4, y: 8, z: 8, core: 2. Of those that a mesh axis runs over, the one named last changes fastest.
Arguments:
- queries: bfloat16 [4096, 8192], P('exp', 'ctx'), may hold values from -180 to 180
- key_proj: bfloat16 [4096, 512], P('exp'), may hold values from -7 to 7
- value_matrix_rows: bfloat16 [4096, 512], P('exp'), may hold values from -6 to 6
- attn_grad: bfloat16 [4096, 8192], P('exp', 'ctx'), may hold values from -6 to 6
- moe_input: bfloat16 [4096, 4096], P('exp', 'ctx'), may hold values from -6 to 6
- moe_grad: bfloat16 [4096, 4096], P('exp', 'ctx'), may hold values from -6 to 6
- expert_ids: int32 [4096, 2], P('exp'), may hold values from 0 to 63, as said below
- route_weights: float32 [4096, 2], P('exp'), may hold values from 0.1 to 1
- gate_proj: bfloat16 [64, 4096, 768], P('exp', 'ctx'), may hold values from -0.09375 to 0.09375
- up_proj: bfloat16 [64, 4096, 768], P('exp', 'ctx'), may hold values from -0.09375 to 0.09375
- down_proj: bfloat16 [64, 768, 4096], P('exp', None, 'ctx'), may hold values from -0.21875 to 0.21875
Outputs:
- attn_out: bfloat16 [4096, 8192], P('exp', 'ctx')
- query_grad: bfloat16 [4096, 8192], P('exp', 'ctx')
- key_grad: bfloat16 [4096, 512], P('exp')
- value_grad: bfloat16 [4096, 512], P('exp')
- moe_out: bfloat16 [4096, 4096], P('exp', 'ctx')
- input_grad: bfloat16 [4096, 4096], P('exp', 'ctx')
The draws below stay inside these ranges and needn't reach their ends.
Inputs may be any that keep to these rules, and one draw needn't show every extreme that they name: `expert_ids`: each row names 2 different experts. In each aligned block of 128 rows no expert is named more than 6 times, and one expert, the same in every block, is named exactly 6 times in every block.
All inputs are finite; a program needn't handle non-finite values.
Results may differ from the reference program's by a relative error of at most 0.019.
Values may be sent and summed in bfloat16 or wider, within the bound.
A program may use at most 64 MiB of HBM per device.

```python
import jax
import jax.numpy as jnp
from jax import lax

D = 4096
QUERY_HEAD_COUNT = 64
KEY_VALUE_HEADS = 4
HEAD_SIZE = 128
FF = 768
TOP = 2
TOK_DEV = 128
SEQUENCE_TOKENS = 4096
EXPERTS = 64
SLOT = 6
CAP = 192


def drawn_pair(key):
    query = jnp.clip(jax.random.normal(jax.random.fold_in(key, 101), (SEQUENCE_TOKENS, QUERY_HEAD_COUNT * HEAD_SIZE), jnp.float32), -6.0, 6.0)
    key_row_block = jnp.clip(jax.random.normal(jax.random.fold_in(key, 102), (SEQUENCE_TOKENS, KEY_VALUE_HEADS * HEAD_SIZE), jnp.float32), -6.0, 6.0)
    return (query, key_row_block)


def draw_queries(key, part):
    return drawn_pair(key)[0].astype(jnp.bfloat16)


def draw_key_proj(key, part):
    return drawn_pair(key)[1].astype(jnp.bfloat16)


def draw_expert_ids(key, part):
    others = EXPERTS - 1
    busiest = jax.random.randint(jax.random.fold_in(key, 201), (), 0, EXPERTS).astype(jnp.int32)
    block_count = SEQUENCE_TOKENS // TOK_DEV

    def one_block(block_index):
        block_key = jax.random.fold_in(jax.random.fold_in(key, 301), block_index)
        ranking = jax.random.permutation(jax.random.fold_in(block_key, 1), others).astype(jnp.int32)
        ranking = ranking + (ranking >= busiest).astype(jnp.int32)
        spots = jnp.arange(2 * TOK_DEV, dtype=jnp.int32)
        rest = jnp.maximum(spots - SLOT, 0) // SLOT
        rest = jnp.minimum(rest, others - 1)
        labels = jnp.where(spots < SLOT, busiest, ranking[rest]).astype(jnp.int32)
        first = labels[:TOK_DEV]
        second = labels[TOK_DEV:]
        flip = jax.random.randint(jax.random.fold_in(block_key, 3), (TOK_DEV,), 0, 2).astype(jnp.int32)
        left = jnp.where(flip == 1, second, first)
        right = jnp.where(flip == 1, first, second)
        order = jax.random.permutation(jax.random.fold_in(block_key, 2), TOK_DEV).astype(jnp.int32)
        return jnp.stack([left[order], right[order]], axis=1)
    table = jax.vmap(one_block)(jnp.arange(block_count, dtype=jnp.int32))
    return table.reshape(SEQUENCE_TOKENS, 2).astype(jnp.int32)


def steps_of(stream_key, shape, split, low, top_value):
    level = 1.0
    for dim, blocks in split:
        steps = jax.random.uniform(jax.random.fold_in(jax.random.fold_in(stream_key, 6), dim), (blocks,), jnp.float32, low / len(split), top_value / len(split))
        level = level * jnp.repeat(jnp.exp(steps), shape[dim] // blocks).reshape((-1,) + (1,) * (len(shape) - 1 - dim))
    return level


def normal_values(key, dims, width, reach, split=(), kind=jnp.bfloat16):
    gain = steps_of(key, dims, split, -0.22, 0.18) if split else 1.0
    values = jax.random.normal(key, dims, jnp.float32) * width * gain
    return jnp.minimum(jnp.maximum(values, -reach), reach).astype(kind)


def setup_inputs(seed: int = 0) -> dict:
    key_of = jax.random.split(jax.random.key(seed), 12)
    queries = draw_queries(jax.random.fold_in(key_of[11], 71), 0)
    key_proj = draw_key_proj(jax.random.fold_in(key_of[11], 71), 0)
    value_matrix_rows = normal_values(key_of[2], (SEQUENCE_TOKENS, KEY_VALUE_HEADS * HEAD_SIZE), 1.0, 6.0, ((0, 32),))
    attn_grad = normal_values(key_of[3], (SEQUENCE_TOKENS, QUERY_HEAD_COUNT * HEAD_SIZE), 1.0, 6.0, ((0, 32), (1, 16)))
    moe_input = normal_values(key_of[4], (SEQUENCE_TOKENS, D), 1.0, 6.0, ((0, 32), (1, 16)))
    moe_grad = normal_values(key_of[5], (SEQUENCE_TOKENS, D), 1.0, 6.0, ((0, 32), (1, 16)))
    expert_ids = draw_expert_ids(jax.random.fold_in(key_of[11], 71), 0)
    route_weights = jnp.clip(0.1 + 0.9 * jax.random.uniform(key_of[7], (SEQUENCE_TOKENS, TOP), jnp.float32) ** steps_of(key_of[7], (SEQUENCE_TOKENS, TOP), ((0, 32),), -0.2, 0.2), 0.1, 1.0)
    gate_proj = normal_values(key_of[8], (EXPERTS, D, FF), D ** -0.5, 0.09375, ((0, 32), (1, 16)))
    up_proj = normal_values(key_of[9], (EXPERTS, D, FF), D ** -0.5, 0.09375, ((0, 32), (1, 16)))
    down_proj = normal_values(key_of[10], (EXPERTS, FF, D), FF ** -0.5, 0.21875, ((0, 32), (2, 16)))
    return dict(queries=queries, key_proj=key_proj, value_matrix_rows=value_matrix_rows, attn_grad=attn_grad, moe_input=moe_input, moe_grad=moe_grad, expert_ids=expert_ids, route_weights=route_weights, gate_proj=gate_proj, up_proj=up_proj, down_proj=down_proj)


def head_pass(query_head, cotan_head, key_head, value_head, positions):
    score_scale = HEAD_SIZE ** -0.5
    scores = jnp.dot(query_head, key_head.T, preferred_element_type=jnp.float32) * score_scale
    scores = jnp.where(positions[None, :] <= positions[:, None], scores, -jnp.inf)
    log_total = jax.nn.logsumexp(scores, axis=1, keepdims=True)
    attn_probs = jnp.exp(scores - log_total).astype(jnp.bfloat16)
    attended = jnp.dot(attn_probs, value_head, preferred_element_type=jnp.float32).astype(jnp.bfloat16)
    row_dot = jnp.sum(cotan_head.astype(jnp.float32) * attended.astype(jnp.float32), axis=1, keepdims=True)
    prob_grad = jnp.dot(cotan_head, value_head.T, preferred_element_type=jnp.float32)
    score_grad = (attn_probs.astype(jnp.float32) * (prob_grad - row_dot)).astype(jnp.bfloat16)
    query_back = (jnp.dot(score_grad, key_head, preferred_element_type=jnp.float32) * score_scale).astype(jnp.bfloat16)
    key_term = jnp.dot(score_grad.T, query_head, preferred_element_type=jnp.float32)
    value_term = jnp.dot(attn_probs.T, cotan_head, preferred_element_type=jnp.float32)
    return attended, query_back, key_term, value_term


def reference(queries, key_proj, value_matrix_rows, attn_grad, moe_input, moe_grad, expert_ids, route_weights, gate_proj, up_proj, down_proj):
    positions = jnp.arange(SEQUENCE_TOKENS, dtype=jnp.int32)
    query_group_width = QUERY_HEAD_COUNT // KEY_VALUE_HEADS
    query_heads = queries.reshape(SEQUENCE_TOKENS, QUERY_HEAD_COUNT, HEAD_SIZE).transpose(1, 0, 2)
    cotan_heads = attn_grad.reshape(SEQUENCE_TOKENS, QUERY_HEAD_COUNT, HEAD_SIZE).transpose(1, 0, 2)
    out_list = []
    qgrad_list = []
    kgrad_list = []
    vgrad_list = []
    for key_value_index in range(KEY_VALUE_HEADS):
        key_head = key_proj[:, key_value_index * HEAD_SIZE:(key_value_index + 1) * HEAD_SIZE]
        value_head = value_matrix_rows[:, key_value_index * HEAD_SIZE:(key_value_index + 1) * HEAD_SIZE]

        def one_head(pair, key_head=key_head, value_head=value_head):
            return head_pass(pair[0], pair[1], key_head, value_head, positions)

        attended, query_back, key_term, value_term = lax.map(
            one_head,
            (query_heads[key_value_index * query_group_width:(key_value_index + 1) * query_group_width],
             cotan_heads[key_value_index * query_group_width:(key_value_index + 1) * query_group_width]))
        out_list.append(attended)
        qgrad_list.append(query_back)
        kgrad_list.append((jnp.sum(key_term, axis=0) * (HEAD_SIZE ** -0.5)).astype(jnp.bfloat16))
        vgrad_list.append(jnp.sum(value_term, axis=0).astype(jnp.bfloat16))
    attn_out = jnp.concatenate(out_list, axis=0).transpose(1, 0, 2).reshape(SEQUENCE_TOKENS, QUERY_HEAD_COUNT * HEAD_SIZE)
    query_grad = jnp.concatenate(qgrad_list, axis=0).transpose(1, 0, 2).reshape(SEQUENCE_TOKENS, QUERY_HEAD_COUNT * HEAD_SIZE)
    key_grad = jnp.concatenate(kgrad_list, axis=1)
    value_grad = jnp.concatenate(vgrad_list, axis=1)

    flat_ids = expert_ids.reshape(-1)
    flat_gain = route_weights.reshape(-1)

    def expert_step(carry, inputs):
        out_acc, grad_acc = carry
        expert_index, gate_w, up_w, down_w = inputs
        chosen = flat_ids == expert_index
        places = jnp.nonzero(chosen, size=CAP, fill_value=0)[0]
        filled = jnp.arange(CAP) < jnp.sum(chosen)
        token_of = (places // TOP).astype(jnp.int32)
        picked_gain = flat_gain[places]
        route_gain = jnp.where(filled, picked_gain, jnp.zeros_like(picked_gain))
        rows_in = moe_input[token_of]
        gate = jnp.dot(rows_in, gate_w, preferred_element_type=jnp.float32)
        up_term = jnp.dot(rows_in, up_w, preferred_element_type=jnp.float32)
        sigmoid_gate = jax.nn.sigmoid(gate)
        activated = gate * sigmoid_gate
        hidden = (activated * up_term).astype(jnp.bfloat16)
        route_out = jnp.dot(hidden, down_w, preferred_element_type=jnp.float32).astype(jnp.bfloat16)
        scaled = (moe_grad[token_of].astype(jnp.float32) * route_gain[:, None]).astype(jnp.bfloat16)
        hidden_grad = jnp.dot(scaled, down_w.T, preferred_element_type=jnp.float32)
        gate_back = (hidden_grad * up_term * sigmoid_gate * (1.0 + gate * (1.0 - sigmoid_gate))).astype(jnp.bfloat16)
        up_back = (hidden_grad * activated).astype(jnp.bfloat16)
        route_in = (jnp.dot(gate_back, gate_w.T, preferred_element_type=jnp.float32)
                    + jnp.dot(up_back, up_w.T, preferred_element_type=jnp.float32)).astype(jnp.bfloat16)
        out_terms = route_out.astype(jnp.float32) * route_gain[:, None]
        in_terms = jnp.where(filled[:, None], route_in.astype(jnp.float32), jnp.zeros_like(route_in, dtype=jnp.float32))
        out_acc = out_acc + jax.ops.segment_sum(out_terms, token_of, num_segments=SEQUENCE_TOKENS)
        grad_acc = grad_acc + jax.ops.segment_sum(in_terms, token_of, num_segments=SEQUENCE_TOKENS)
        return (out_acc, grad_acc), None

    start = (jnp.zeros((SEQUENCE_TOKENS, D), jnp.float32), jnp.zeros((SEQUENCE_TOKENS, D), jnp.float32))
    (out_acc, grad_acc), unused = lax.scan(
        expert_step, start, (jnp.arange(EXPERTS, dtype=jnp.int32), gate_proj, up_proj, down_proj))
    moe_out = out_acc.astype(jnp.bfloat16)
    input_grad = grad_acc.astype(jnp.bfloat16)
    return (attn_out, query_grad, key_grad, value_grad, moe_out, input_grad)
```

```python
import functools

import jax
import jax.numpy as jnp
from jax import lax
from jax.experimental import pallas as pl
from jax.experimental.pallas import tpu as pltpu
from jax.sharding import PartitionSpec as P

MESH = pl.DeviceIdType.MESH
F32 = jnp.float32
BF16 = jnp.bfloat16
HEAD = 128
NX, NZ, NY = 4, 8, 8
NE = NX * NZ
TOK = 128
LOCAL = 2
EXPERTS = LOCAL * NE
SLOT = 6
GROUP = LOCAL * SLOT
SLAB = 4 * GROUP
ROWS = NE * GROUP
FF = 768
HALF = FF // 2
YROWS = ROWS // NY
SCALE = HEAD ** (-0.5)
VMEM_LIMIT = 60 * 1024 * 1024


def dot(a, b):
    return jnp.dot(a, b, preferred_element_type=F32)


def dot_t(a, b):
    return lax.dot_general(a, b, (((1,), (1,)), ((), ())), preferred_element_type=F32)


def t_dot(a, b):
    return lax.dot_general(a, b, (((0,), (0,)), ((), ())), preferred_element_type=F32)


def fdiv(a, n):
    return jnp.floor((a + 0.5) * (1.0 / n))


def fiota(shape, dim):
    return lax.broadcasted_iota(jnp.int32, shape, dim).astype(F32)


def route_tables(ids):
    lane = lax.broadcasted_iota(jnp.int32, (TOK, EXPERTS), 1)
    first = jnp.where(ids[:, 0:1] == lane, 1.0, 0.0)
    second = jnp.where(ids[:, 1:2] == lane, 1.0, 0.0)
    row = lax.broadcasted_iota(jnp.int32, (TOK, TOK), 0)
    col = lax.broadcasted_iota(jnp.int32, (TOK, TOK), 1)
    before = jnp.where(col < row, 1.0, 0.0).astype(BF16)
    place = dot(before, (first + second).astype(BF16)) + 1.0
    return (first * place).astype(BF16), (second * place).astype(BF16)


def slab_index(p):
    dest = fdiv(p, SLAB)
    inner = p - dest * SLAB
    quarter = fdiv(inner, GROUP)
    inner = inner - quarter * GROUP
    local = fdiv(inner, SLOT)
    slot = inner - local * SLOT
    return dest * LOCAL + local, quarter, slot


def prep_kernel(ids_ref, gain_ref, x_ref, g_ref, out_ref):
    v0, v1 = route_tables(ids_ref[...])
    total = NE * SLAB
    expert, quarter, slot = slab_index(fiota((total, 1), 0))
    pick = jnp.where(expert == fiota((total, EXPERTS), 1), 1.0, 0.0).astype(BF16)
    y0 = dot_t(pick, v0)
    y1 = dot_t(pick, v1)
    want = slot + 1.0
    hit0 = jnp.where(y0 == want, 1.0, 0.0)
    hit1 = jnp.where(y1 == want, 1.0, 0.0)
    both = hit0 + hit1
    q = [jnp.where(quarter == float(i), 1.0, 0.0) for i in range(4)]
    table = jnp.concatenate(
        [both * q[0], both * q[1], hit0 * q[2], hit0 * q[3], hit1 * q[2], hit1 * q[3]], axis=1
    ).astype(BF16)
    x = x_ref[...]
    g = g_ref[...].astype(F32)
    gain = gain_ref[...]
    s0 = (g * gain[:, 0:1]).astype(BF16)
    s1 = (g * gain[:, 1:2]).astype(BF16)
    rows = jnp.concatenate(
        [x[:, :128], x[:, 128:], s0[:, :128], s0[:, 128:], s1[:, :128], s1[:, 128:]], axis=0
    )
    out_ref[...] = dot(table, rows).astype(BF16)


def combine_kernel(ids_ref, gain_ref, back_ref, kvg_ref, out_ref, in_ref, kg_ref, vg_ref):
    v0, v1 = route_tables(ids_ref[...])
    total = NE * SLAB
    expert, quarter, slot = slab_index(fiota((1, total), 1))
    pick = jnp.where(expert == fiota((EXPERTS, total), 0), 1.0, 0.0).astype(BF16)
    y0 = dot(v0, pick)
    y1 = dot(v1, pick)
    want = slot + 1.0
    hit0 = jnp.where(y0 == want, 1.0, 0.0)
    hit1 = jnp.where(y1 == want, 1.0, 0.0)
    both = hit0 + hit1
    q = [jnp.where(quarter == float(i), 1.0, 0.0) for i in range(4)]
    back = back_ref[...]
    gain = gain_ref[...]
    for i in range(2):
        part0 = dot((hit0 * q[i]).astype(BF16), back)
        part1 = dot((hit1 * q[i]).astype(BF16), back)
        out_ref[:, i * 128 : (i + 1) * 128] = (
            part0 * gain[:, 0:1] + part1 * gain[:, 1:2]
        ).astype(BF16)
        in_ref[:, i * 128 : (i + 1) * 128] = dot((both * q[2 + i]).astype(BF16), back).astype(BF16)
    kg_ref[...] = kvg_ref[0]
    vg_ref[...] = kvg_ref[1]


PACK = 8 * GROUP


def pack_table(transposed):
    n = 4 * PACK
    shape = (n, n)
    r = fiota((1, n) if transposed else (n, 1), 1 if transposed else 0)
    quarter = fdiv(r, PACK)
    inner = r - quarter * PACK
    source = fdiv(inner, GROUP)
    p = source * SLAB + quarter * GROUP + (inner - source * GROUP)
    return jnp.where(p == fiota(shape, 0 if transposed else 1), 1.0, 0.0).astype(BF16)


def first_local(rows):
    r = fiota((rows, 1), 0)
    inner = r - fdiv(r, GROUP) * GROUP
    return inner < float(SLOT)


def moe_in_kernel(recv_ref, gate_ref, up_ref, down_ref, out_ref):
    table = pack_table(False)
    parts = [[], [], [], []]
    n = 4 * PACK
    for g in range(NE // 8):
        packed = dot(table, recv_ref[g * n : (g + 1) * n, :]).astype(BF16)
        for i in range(4):
            parts[i].append(packed[i * PACK : (i + 1) * PACK, :])
    cols = [jnp.concatenate(p, axis=0) for p in parts]
    rows = jnp.concatenate(cols[:2], axis=1)
    scaled = jnp.concatenate(cols[2:], axis=1)
    first = first_local(ROWS)
    for m in range(3):
        if m < 2:
            w_ref = gate_ref if m == 0 else up_ref
            full = jnp.where(first, dot(rows, w_ref[0]), dot(rows, w_ref[1]))
        else:
            full = jnp.where(first, dot_t(scaled, down_ref[0]), dot_t(scaled, down_ref[1]))
        full = full.astype(BF16)
        for k in range(2):
            for y in range(NY):
                out_ref[k, y, m] = full[y * YROWS : (y + 1) * YROWS, k * HALF : (k + 1) * HALF]


def moe_out_kernel(full_ref, gate_ref, up_ref, down_ref, out_ref):
    first = first_local(ROWS)

    def both(m, weight, transposed):
        halves = [full_ref[k, :, m].reshape(ROWS, HALF) for k in range(2)]
        whole = jnp.concatenate(halves, axis=1)
        f = dot_t if transposed else dot
        return jnp.where(first, f(whole, weight[0]), f(whole, weight[1]))

    route_out = both(0, down_ref, False).astype(BF16)
    route_in = (both(1, gate_ref, True) + both(2, up_ref, True)).astype(BF16)
    quarters = [route_out[:, :128], route_out[:, 128:], route_in[:, :128], route_in[:, 128:]]
    table = pack_table(True)
    n = 4 * PACK
    for g in range(NE // 8):
        stack = jnp.concatenate([q[g * PACK : (g + 1) * PACK] for q in quarters], axis=0)
        out_ref[g * n : (g + 1) * n, :] = dot(table, stack).astype(BF16)


CHUNK = 512


def attn_kernel(q_ref, kv_ref, do_ref, out_ref, dq_ref, dkv_ref, s_ref, e_ref):
    heads = q_ref.shape[1] // HEAD
    width = heads * TOK
    per = CHUNK // (NX * TOK)
    chunks = NZ // per
    base = lax.axis_index("exp") * TOK
    q = jnp.concatenate([q_ref[:, h * HEAD : (h + 1) * HEAD] for h in range(heads)], axis=0)
    do = jnp.concatenate([do_ref[:, h * HEAD : (h + 1) * HEAD] for h in range(heads)], axis=0)
    lane = lax.broadcasted_iota(jnp.int32, (1, width), 1)
    q_pos = base + jnp.bitwise_and(lane, TOK - 1)
    row = lax.broadcasted_iota(jnp.int32, (CHUNK, 1), 0)

    def load(which, j):
        return kv_ref[which, pl.ds(j * per, per)].reshape(CHUNK, HEAD)

    def scores(j, m):
        s = dot_t(load(0, j), q) * SCALE
        s = jnp.where(row + j * CHUNK <= q_pos, s, -jnp.inf)
        s_ref[j] = s
        return jnp.maximum(m, jnp.max(s, axis=0, keepdims=True))

    m = lax.fori_loop(0, chunks, scores, jnp.full((1, width), -jnp.inf, F32))

    def values(j, carry):
        l, o = carry
        e = jnp.exp(s_ref[j] - m)
        e16 = e.astype(BF16)
        e_ref[j] = e16
        return l + jnp.sum(e, axis=0, keepdims=True), o + t_dot(load(1, j), e16)

    l, o = lax.fori_loop(
        0, chunks, values, (jnp.zeros((1, width), F32), jnp.zeros((HEAD, width), F32))
    )
    inv = 1.0 / l
    o16 = (o * inv).astype(BF16)
    o_r = o16.astype(F32).T
    delta_parts = []
    for h in range(heads):
        piece = o_r[h * TOK : (h + 1) * TOK, :]
        out_ref[:, h * HEAD : (h + 1) * HEAD] = piece.astype(BF16)
    do_t = do.astype(F32).T
    delta = jnp.sum(do_t * o16.astype(F32), axis=0, keepdims=True)

    def back(j, dq):
        k = load(0, j)
        dp = dot_t(load(1, j), do)
        p = e_ref[j].astype(F32) * inv
        ds = (p * (dp - delta)).astype(BF16)
        p16 = p.astype(BF16)
        dk = (dot(ds, q) * SCALE).astype(BF16)
        dv = dot(p16, do).astype(BF16)
        dkv_ref[0, pl.ds(j * per, per)] = dk.reshape(per, NX, TOK, HEAD)
        dkv_ref[1, pl.ds(j * per, per)] = dv.reshape(per, NX, TOK, HEAD)
        return dq + t_dot(k, ds)

    dq = lax.fori_loop(0, chunks, back, jnp.zeros((HEAD, width), F32))
    dq_r = (dq * SCALE).T
    for h in range(heads):
        dq_ref[:, h * HEAD : (h + 1) * HEAD] = dq_r[h * TOK : (h + 1) * TOK, :].astype(BF16)


class Place:
    def __init__(self):
        self.e = lax.axis_index("exp")
        self.c = lax.axis_index("ctx")
        self.z, self.x = self.e // NX, self.e % NX
        self.y, self.k = self.c // 2, self.c % 2
        self.sgn = 1 - 2 * self.k
        self.mate = {"exp": self.e, "ctx": self.y * 2 + 1 - self.k}
        self.twin = {"exp": self.e, "ctx": (self.y + 1 - 2 * (self.y % 2)) * 2 + self.k}

    def at_z(self, step):
        return (self.z + self.sgn * step + 2 * NZ) % NZ

    def at_x(self, step):
        return (self.x + self.sgn * step + 2 * NX) % NX

    def at_y(self, step):
        return (self.y + self.sgn * step + 2 * NY) % NY

    def dev_z(self, step):
        return {"exp": self.at_z(step) * NX + self.x, "ctx": self.c}

    def dev_x(self, step):
        return {"exp": self.z * NX + self.at_x(step), "ctx": self.c}

    def dev_y(self, step):
        return {"exp": self.e, "ctx": self.at_y(step) * 2 + self.k}


def remote(src, dst, send, recv, device):
    return pltpu.make_async_remote_copy(
        src_ref=src, dst_ref=dst, send_sem=send, recv_sem=recv, device_id=device,
        device_id_type=MESH,
    )


def greet(devices, far):
    barrier = pltpu.get_barrier_semaphore()
    for device in devices:
        pl.semaphore_signal(barrier, inc=1, device_id=device, device_id_type=MESH)
    count = len(devices)
    if far is not None:

        def one(o, carry):
            peer = (far.e + o) % NE
            pl.semaphore_signal(
                barrier, inc=1, device_id={"exp": peer, "ctx": far.c}, device_id_type=MESH
            )
            return carry

        lax.fori_loop(1, NE, one, 0)
        count += NE - 1
    pl.semaphore_wait(barrier, count)


def exchange(here, send_ref, recv_ref, send_sem, recv_sem):
    def desc(o):
        dest = (here.e + o) % NE
        return remote(
            send_ref.at[dest], recv_ref.at[here.e], send_sem.at[o], recv_sem.at[o],
            {"exp": dest, "ctx": here.c},
        )

    def incoming(o):
        source = (here.e + NE - o) % NE
        return remote(
            send_ref.at[source], recv_ref.at[source], send_sem.at[o], recv_sem.at[o],
            {"exp": source, "ctx": here.c},
        )

    def begin(first, last):
        def go(o, carry):
            desc(o).start()
            return carry

        lax.fori_loop(first, last, go, 0)

    def finish():
        def go(o, carry):
            desc(o).wait_send()
            incoming(o).wait_recv()
            return carry

        lax.fori_loop(1, NE, go, 0)

    return begin, finish


def drive(*chains):
    live = list(chains)
    while live:
        for chain in list(live):
            try:
                next(chain)
            except StopIteration:
                live.remove(chain)


def spread_kernel(
    send_ref, key_ref, val_ref, kv_ref, recv_ref, s_far, r_far, s_x, r_x, s_z, r_z, s_m, r_m, s_l
):
    here = Place()
    greet([here.mate], here)
    begin, finish = exchange(here, send_ref, recv_ref, s_far, r_far)
    k, z, x = here.k, here.z, here.x
    cols = pl.ds(pl.multiple_of((here.y // 2) * HEAD, HEAD), HEAD)
    own = kv_ref.at[k, z, x]

    @pl.when(k == 0)
    def _():
        c = pltpu.make_async_copy(key_ref.at[:, cols], own, s_l.at[0])
        c.start()
        c.wait()

    @pl.when(k == 1)
    def _():
        c = pltpu.make_async_copy(val_ref.at[:, cols], own, s_l.at[0])
        c.start()
        c.wait()

    local = pltpu.make_async_copy(send_ref.at[here.e], recv_ref.at[here.e], s_l.at[1])
    local.start()

    def block(step):
        return kv_ref.at[k, z, here.at_x(step)]

    def slab(step):
        return kv_ref.at[k, here.at_z(step)]

    def xcopy(i, origin, to):
        return remote(block(origin), block(origin), s_x.at[i], r_x.at[i], here.dev_x(to))

    sends = [xcopy(0, 0, 1), xcopy(2, 0, -1)]
    sends[0].start()
    sends[1].start()
    begin(1, 9)
    xcopy(0, -1, 1).wait_recv()
    c = xcopy(1, -1, 1)
    c.start()
    sends.append(c)
    xcopy(2, 1, -1).wait_recv()
    xcopy(1, -2, 1).wait_recv()

    def zcopy(i, origin, to):
        return remote(slab(origin), slab(origin), s_z.at[i], r_z.at[i], here.dev_z(to))

    def mcopy(i, origin):
        return remote(slab(origin), slab(origin), s_m.at[i], r_m.at[i], here.mate)

    half = NZ // 2
    a = zcopy(0, 0, 1)
    a.start()
    b = zcopy(half, 0, -1)
    b.start()
    m = mcopy(0, 0)
    m.start()
    sends += [a, b, m]
    bounds = [9, 17, 25, 32, 32]
    for s in range(1, half + 1):
        begin(bounds[s - 1], bounds[s])
        zcopy(s - 1, -s, 1).wait_recv()
        if s < half:
            c = zcopy(s, -s, 1)
            c.start()
            sends.append(c)
        m = mcopy(s, -s)
        m.start()
        sends.append(m)
        if s < half:
            zcopy(half + s - 1, s, -1).wait_recv()
            if s < half - 1:
                c = zcopy(half + s, s, -1)
                c.start()
                sends.append(c)
            m = mcopy(half + s, s)
            m.start()
            sends.append(m)
    other = 1 - k

    def from_mate(i, step):
        spot = kv_ref.at[other, here.at_z(-step)]
        return remote(spot, spot, s_m.at[i], r_m.at[i], here.mate)

    for s in range(0, half + 1):
        from_mate(s, -s).wait_recv()
        if 0 < s < half:
            from_mate(half + s, s).wait_recv()
    for c in sends:
        c.wait_send()
    finish()
    local.wait()


def add16(*refs):
    total = refs[0].astype(F32)
    for r in refs[1:]:
        total = total + r.astype(F32)
    return total


def reduce_kernel(
    part_ref, dkv_ref, full_ref, kg_ref,
    pmate, ysend, yrecv, dmate, zsend, zrecv, own4, xsend, xrecv, tsend, trecv,
    s_pm, r_pm, s_y, r_y, s_g, r_g, s_gm, r_gm, s_dm, r_dm, s_z, r_z, s_x, r_x, s_t, r_t,
):
    here = Place()
    k = here.k
    greet(
        [here.mate, here.twin, here.dev_z(1), here.dev_z(-1), here.dev_x(1), here.dev_x(-1),
         here.dev_y(1), here.dev_y(-1)],
        None,
    )
    half = NY // 2
    sends = []

    def go(c):
        c.start()
        sends.append(c)

    order = [4, -3, 3, -2, 2, -1, 1, 0]
    for i, step in enumerate(order):
        d = here.at_y(-step)
        go(remote(part_ref.at[1 - k, d], pmate.at[d], s_pm.at[i], r_pm.at[i], here.mate))
        d = here.at_z(-step)
        go(remote(dkv_ref.at[1 - k, d], dmate.at[d], s_dm.at[i], r_dm.at[i], here.mate))

    def part_in(i):
        d = here.at_y(order[i])
        remote(part_ref.at[k, d], pmate.at[d], s_pm.at[i], r_pm.at[i], here.mate).wait_recv()
        return d

    def dkv_in(i):
        d = here.at_z(order[i])
        remote(dkv_ref.at[k, d], dmate.at[d], s_dm.at[i], r_dm.at[i], here.mate).wait_recv()
        return d

    def yslot(i, to):
        return remote(ysend.at[i], yrecv.at[i], s_y.at[i], r_y.at[i], here.dev_y(to))

    def zslot(i, to):
        return remote(zsend.at[i], zrecv.at[i], s_z.at[i], r_z.at[i], here.dev_z(to))

    def chain_y():
        for s in range(half):
            d = part_in(order.index(half - s))
            if s == 0:
                ysend[0] = add16(part_ref[k, d], pmate[d]).astype(BF16)
            else:
                yslot(s - 1, 1).wait_recv()
                ysend[s] = add16(part_ref[k, d], pmate[d], yrecv[s - 1]).astype(BF16)
            go(yslot(s, 1))
            yield
            if s < half - 1:
                d = part_in(order.index(-(half - 1 - s)))
                if s == 0:
                    ysend[half] = add16(part_ref[k, d], pmate[d]).astype(BF16)
                else:
                    yslot(half + s - 1, -1).wait_recv()
                    ysend[half + s] = add16(
                        part_ref[k, d], pmate[d], yrecv[half + s - 1]
                    ).astype(BF16)
                go(yslot(half + s, -1))
                yield
        d = part_in(order.index(0))
        yslot(2 * half - 2, -1).wait_recv()
        yslot(half - 1, 1).wait_recv()
        total = add16(part_ref[k, d], pmate[d], yrecv[2 * half - 2], yrecv[half - 1])
        gate, up, hidden_grad = total[0], total[1], total[2]
        sig = 1.0 / (1.0 + jnp.exp(-gate))
        act = gate * sig
        full_ref[k, here.y, 0] = (act * up).astype(BF16)
        full_ref[k, here.y, 1] = (hidden_grad * up * sig * (1.0 + gate * (1.0 - sig))).astype(BF16)
        full_ref[k, here.y, 2] = (hidden_grad * act).astype(BF16)

        def gcopy(i, origin, to):
            spot = full_ref.at[k, here.at_y(origin)]
            return remote(spot, spot, s_g.at[i], r_g.at[i], here.dev_y(to))

        def mcopy(i, origin):
            spot = full_ref.at[k, here.at_y(origin)]
            return remote(spot, spot, s_gm.at[i], r_gm.at[i], here.mate)

        go(gcopy(0, 0, 1))
        go(gcopy(half, 0, -1))
        go(mcopy(0, 0))
        yield
        for s in range(1, half + 1):
            gcopy(s - 1, -s, 1).wait_recv()
            if s < half:
                go(gcopy(s, -s, 1))
            go(mcopy(s, -s))
            if s < half:
                gcopy(half + s - 1, s, -1).wait_recv()
                if s < half - 1:
                    go(gcopy(half + s, s, -1))
                go(mcopy(half + s, s))
            yield

        def from_mate(i, step):
            spot = full_ref.at[1 - k, here.at_y(step)]
            remote(spot, spot, s_gm.at[i], r_gm.at[i], here.mate).wait_recv()

        for s in range(0, half + 1):
            from_mate(s, s)
            if 0 < s < half:
                from_mate(half + s, -s)

    def chain_z():
        for s in range(half):
            d = dkv_in(order.index(half - s))
            if s == 0:
                zsend[0] = add16(dkv_ref[k, d], dmate[d]).astype(BF16)
            else:
                zslot(s - 1, 1).wait_recv()
                zsend[s] = add16(dkv_ref[k, d], dmate[d], zrecv[s - 1]).astype(BF16)
            go(zslot(s, 1))
            yield
            if s < half - 1:
                d = dkv_in(order.index(-(half - 1 - s)))
                if s == 0:
                    zsend[half] = add16(dkv_ref[k, d], dmate[d]).astype(BF16)
                else:
                    zslot(half + s - 1, -1).wait_recv()
                    zsend[half + s] = add16(
                        dkv_ref[k, d], dmate[d], zrecv[half + s - 1]
                    ).astype(BF16)
                go(zslot(half + s, -1))
                yield
        d = dkv_in(order.index(0))
        zslot(2 * half - 2, -1).wait_recv()
        zslot(half - 1, 1).wait_recv()
        own4[...] = add16(dkv_ref[k, d], dmate[d], zrecv[2 * half - 2], zrecv[half - 1])

        def xslot(i, to):
            return remote(xsend.at[i], xrecv.at[i], s_x.at[i], r_x.at[i], here.dev_x(to))

        xsend[0] = own4[here.at_x(2)].astype(BF16)
        go(xslot(0, 1))
        xsend[2] = own4[here.at_x(-1)].astype(BF16)
        go(xslot(2, -1))
        yield
        xslot(0, 1).wait_recv()
        xsend[1] = add16(own4[here.at_x(1)], xrecv[0]).astype(BF16)
        go(xslot(1, 1))
        yield
        xslot(2, -1).wait_recv()
        xslot(1, 1).wait_recv()
        tsend[...] = add16(own4[here.x], xrecv[2], xrecv[1]).astype(BF16)
        t = remote(tsend, trecv, s_t.at[0], r_t.at[0], here.twin)
        go(t)
        yield
        t.wait_recv()
        kg_ref[...] = add16(tsend[...], trecv[...]).astype(BF16)

    drive(chain_z(), chain_y())
    for c in sends:
        c.wait_send()


def return_kernel(
    send_ref, kg_ref, recv_ref, kvg_ref, s_far, r_far, s_y, r_y, s_m, r_m, s_l
):
    here = Place()
    k = here.k
    greet([here.mate] + [here.dev_y(s) for s in (2, 4, 6)], here)
    begin, finish = exchange(here, send_ref, recv_ref, s_far, r_far)

    def cols(step):
        head = here.at_y(step) // 2
        return pl.ds(pl.multiple_of(head * HEAD, HEAD), HEAD)

    def spot(which, step):
        return kvg_ref.at[which, :, cols(step)]

    sends = []

    def go(c):
        c.start()
        sends.append(c)

    for i, step in enumerate((2, 4, 6)):
        go(remote(kg_ref, spot(k, 0), s_y.at[i], r_y.at[i], here.dev_y(step)))
    go(remote(kg_ref, spot(k, 0), s_m.at[3], r_m.at[3], here.mate))
    mine = pltpu.make_async_copy(kg_ref, spot(k, 0), s_l.at[0])
    mine.start()
    local = pltpu.make_async_copy(send_ref.at[here.e], recv_ref.at[here.e], s_l.at[1])
    local.start()
    begin(1, NE)
    for i, step in enumerate((2, 4, 6)):
        remote(kg_ref, spot(k, -step), s_y.at[i], r_y.at[i], here.dev_y(-step)).wait_recv()
        go(remote(spot(k, -step), spot(k, -step), s_m.at[i], r_m.at[i], here.mate))
    for i, step in enumerate((2, 4, 6)):
        remote(
            spot(1 - k, step), spot(1 - k, step), s_m.at[i], r_m.at[i], here.mate
        ).wait_recv()
    remote(kg_ref, spot(1 - k, 0), s_m.at[3], r_m.at[3], here.mate).wait_recv()
    for c in sends:
        c.wait_send()
    finish()
    mine.wait()
    local.wait()


def vmem():
    return pl.BlockSpec(memory_space=pltpu.VMEM)


def dma(n):
    return pltpu.SemaphoreType.DMA((n,))


def call(kernel, outs, scratch, *args, specs=None, collective=None, name=None, flops=0):
    params = {"vmem_limit_bytes": VMEM_LIMIT}
    if collective is not None:
        params.update(collective_id=collective, has_side_effects=True)
    return pl.pallas_call(
        kernel,
        out_shape=outs,
        in_specs=specs or [vmem()] * len(args),
        out_specs=jax.tree.map(lambda o: vmem(), outs),
        scratch_shapes=scratch,
        compiler_params=pltpu.CompilerParams(**params),
        name=name,
    )(*args)


def shape(*dims, dtype=BF16):
    return jax.ShapeDtypeStruct(dims, dtype)


def body(q, key, val, do, x, g, ids, gain, gate, up, down):
    send = call(prep_kernel, shape(NE * SLAB, 128), [], ids, gain, x, g, name="prep")
    hbm = pl.BlockSpec(memory_space=pl.ANY)
    kv, recv = call(
        spread_kernel,
        (shape(2, NZ, NX, TOK, HEAD), shape(NE, SLAB, 128)),
        [dma(NE), dma(NE), dma(3), dma(3), dma(8), dma(8), dma(8), dma(8), dma(2)],
        send.reshape(NE, SLAB, 128), key, val,
        specs=[vmem(), hbm, hbm], collective=0, name="spread",
    )
    part = call(
        moe_in_kernel, shape(2, NY, 3, YROWS, HALF), [],
        recv.reshape(NE * SLAB, 128), gate, up, down, name="moe_in",
    )
    heads = q.shape[1] // HEAD
    steps = NE * TOK // CHUNK
    attn_out, dq, dkv = call(
        attn_kernel,
        (shape(TOK, q.shape[1]), shape(TOK, q.shape[1]), shape(2, NZ, NX, TOK, HEAD)),
        [pltpu.VMEM((steps, CHUNK, heads * TOK), F32), pltpu.VMEM((steps, CHUNK, heads * TOK), BF16)],
        q, kv, do, name="attn",
    )
    yslab = (3, YROWS, HALF)
    zslab = (NX, TOK, HEAD)
    block = (TOK, HEAD)
    full, kg = call(
        reduce_kernel,
        (shape(2, NY, *yslab), shape(*block)),
        [
            pltpu.VMEM((NY, *yslab), BF16), pltpu.VMEM((7, *yslab), BF16),
            pltpu.VMEM((7, *yslab), BF16),
            pltpu.VMEM((NZ, *zslab), BF16), pltpu.VMEM((7, *zslab), BF16),
            pltpu.VMEM((7, *zslab), BF16), pltpu.VMEM(zslab, F32),
            pltpu.VMEM((3, *block), BF16), pltpu.VMEM((3, *block), BF16),
            pltpu.VMEM(block, BF16), pltpu.VMEM(block, BF16),
            dma(8), dma(8), dma(7), dma(7), dma(7), dma(7), dma(8), dma(8),
            dma(8), dma(8), dma(7), dma(7), dma(3), dma(3), dma(1), dma(1),
        ],
        part, dkv, collective=1, name="reduce",
    )
    back = call(
        moe_out_kernel, shape(NE * SLAB, 128), [], full, gate, up, down, name="moe_out"
    )
    returned, kvg = call(
        return_kernel,
        (shape(NE, SLAB, 128), shape(2, TOK, 4 * HEAD)),
        [dma(NE), dma(NE), dma(3), dma(3), dma(4), dma(4), dma(2)],
        back.reshape(NE, SLAB, 128), kg, collective=2, name="return",
    )
    moe_out, input_grad, key_grad, value_grad = call(
        combine_kernel,
        (shape(TOK, 256), shape(TOK, 256), shape(TOK, 512), shape(TOK, 512)), [],
        ids, gain, returned.reshape(NE * SLAB, 128), kvg, name="combine",
    )
    return attn_out, dq, key_grad, value_grad, moe_out, input_grad


def solution(mesh):
    rows, both = P("exp", None), P("exp", "ctx")
    return jax.shard_map(
        body,
        mesh=mesh,
        in_specs=(
            both, rows, rows, both, both, both, rows, rows,
            P("exp", "ctx", None), P("exp", "ctx", None), P("exp", None, "ctx"),
        ),
        out_specs=(both, both, rows, rows, both, both),
        check_vma=False,
    )
```

```python
import functools

import jax
import jax.numpy as jnp
from jax import lax
from jax.experimental import pallas as pl
from jax.experimental.pallas import tpu as pltpu
from jax.sharding import PartitionSpec as P

MESH = pl.DeviceIdType.MESH
F32 = jnp.float32
BF16 = jnp.bfloat16
HEAD = 128
NX, NZ, NY = 4, 8, 8
NE = NX * NZ
TOK = 128
LOCAL = 2
EXPERTS = LOCAL * NE
SLOT = 6
GROUP = LOCAL * SLOT
SLAB = 4 * GROUP
ROWS = NE * GROUP
FF = 768
HALF = FF // 2
YROWS = ROWS // NY
SCALE = HEAD ** (-0.5)
VMEM_LIMIT = 60 * 1024 * 1024


def dot(a, b):
    return jnp.dot(a, b, preferred_element_type=F32)


def dot_t(a, b):
    return lax.dot_general(a, b, (((1,), (1,)), ((), ())), preferred_element_type=F32)


def t_dot(a, b):
    return lax.dot_general(a, b, (((0,), (0,)), ((), ())), preferred_element_type=F32)


def fdiv(a, n):
    return jnp.floor((a + 0.5) * (1.0 / n))


def fiota(shape, dim):
    return lax.broadcasted_iota(jnp.int32, shape, dim).astype(F32)


def column(row):
    return jnp.broadcast_to(row, (TOK, TOK)).T


def route_tables(ids):
    lane = fiota((TOK, EXPERTS), 1)
    ids = ids.astype(F32)
    first = jnp.where(column(ids[0:1])[:, :EXPERTS] == lane, 1.0, 0.0)
    second = jnp.where(column(ids[1:2])[:, :EXPERTS] == lane, 1.0, 0.0)
    row = lax.broadcasted_iota(jnp.int32, (TOK, TOK), 0)
    col = lax.broadcasted_iota(jnp.int32, (TOK, TOK), 1)
    before = jnp.where(col < row, 1.0, 0.0).astype(BF16)
    place = dot(before, (first + second).astype(BF16)) + 1.0
    return (first * place).astype(BF16), (second * place).astype(BF16)


def slab_index(p):
    dest = fdiv(p, SLAB)
    inner = p - dest * SLAB
    quarter = fdiv(inner, GROUP)
    inner = inner - quarter * GROUP
    local = fdiv(inner, SLOT)
    slot = inner - local * SLOT
    return dest * LOCAL + local, quarter, slot


def prepare(ids_ref, gain_ref, x_ref, g_ref, out_ref):
    v0, v1 = route_tables(ids_ref[...])
    total = NE * SLAB
    expert, quarter, slot = slab_index(fiota((total, 1), 0))
    pick = jnp.where(expert == fiota((total, EXPERTS), 1), 1.0, 0.0).astype(BF16)
    y0 = dot_t(pick, v0)
    y1 = dot_t(pick, v1)
    want = slot + 1.0
    hit0 = jnp.where(y0 == want, 1.0, 0.0)
    hit1 = jnp.where(y1 == want, 1.0, 0.0)
    both = hit0 + hit1
    q = [jnp.where(quarter == float(i), 1.0, 0.0) for i in range(4)]
    table = jnp.concatenate(
        [both * q[0], both * q[1], hit0 * q[2], hit0 * q[3], hit1 * q[2], hit1 * q[3]], axis=1
    ).astype(BF16)
    x = x_ref[...]
    g = g_ref[...].astype(F32)
    gain = gain_ref[...]
    w0, w1 = column(gain[0:1]), column(gain[1:2])
    lo, hi = g[:, :128], g[:, 128:]
    scaled = [(a * w).astype(BF16) for w in (w0, w1) for a in (lo, hi)]
    rows = jnp.concatenate([x[:, :128], x[:, 128:]] + scaled, axis=0)
    out_ref[...] = dot(table, rows).astype(BF16).reshape(NE, SLAB, 128)


def combine_kernel(
    ids_ref, gain_ref, back_ref, kvg_ref, ao_ref, dq_ref,
    out_ref, in_ref, kg_ref, vg_ref, ao_out, dq_out,
):
    v0, v1 = route_tables(ids_ref[...])
    total = NE * SLAB
    expert, quarter, slot = slab_index(fiota((1, total), 1))
    pick = jnp.where(expert == fiota((EXPERTS, total), 0), 1.0, 0.0).astype(BF16)
    y0 = dot(v0, pick)
    y1 = dot(v1, pick)
    want = slot + 1.0
    hit0 = jnp.where(y0 == want, 1.0, 0.0)
    hit1 = jnp.where(y1 == want, 1.0, 0.0)
    both = hit0 + hit1
    q = [jnp.where(quarter == float(i), 1.0, 0.0) for i in range(4)]
    back = back_ref[...]
    gain = gain_ref[...]
    w0, w1 = column(gain[0:1]), column(gain[1:2])
    for i in range(2):
        part0 = dot((hit0 * q[i]).astype(BF16), back)
        part1 = dot((hit1 * q[i]).astype(BF16), back)
        out_ref[:, i * 128 : (i + 1) * 128] = (part0 * w0 + part1 * w1).astype(BF16)
        in_ref[:, i * 128 : (i + 1) * 128] = dot((both * q[2 + i]).astype(BF16), back).astype(BF16)
    kg_ref[...] = kvg_ref[0]
    vg_ref[...] = kvg_ref[1]
    ao_out[...] = ao_ref[...]
    dq_out[...] = dq_ref[...]


PACK = 8 * GROUP


def pack_table(transposed):
    n = 4 * PACK
    shape = (n, n)
    r = fiota((1, n) if transposed else (n, 1), 1 if transposed else 0)
    quarter = fdiv(r, PACK)
    inner = r - quarter * PACK
    source = fdiv(inner, GROUP)
    p = source * SLAB + quarter * GROUP + (inner - source * GROUP)
    return jnp.where(p == fiota(shape, 0 if transposed else 1), 1.0, 0.0).astype(BF16)


def first_local(rows):
    r = fiota((rows, 1), 0)
    inner = r - fdiv(r, GROUP) * GROUP
    return inner < float(SLOT)


class Place:
    def __init__(self):
        self.e = lax.axis_index("exp")
        self.c = lax.axis_index("ctx")
        self.z, self.x = self.e // NX, self.e % NX
        self.y, self.k = self.c // 2, self.c % 2
        self.sgn = 1 - 2 * self.k
        self.mate = {"exp": self.e, "ctx": self.y * 2 + 1 - self.k}
        self.twin = {"exp": self.e, "ctx": (self.y + 1 - 2 * (self.y % 2)) * 2 + self.k}

    def at_z(self, step):
        return (self.z + self.sgn * step + 2 * NZ) % NZ

    def at_x(self, step):
        return (self.x + self.sgn * step + 2 * NX) % NX

    def at_y(self, step):
        return (self.y + self.sgn * step + 2 * NY) % NY

    def dev_z(self, step):
        return {"exp": self.at_z(step) * NX + self.x, "ctx": self.c}

    def dev_x(self, step):
        return {"exp": self.z * NX + self.at_x(step), "ctx": self.c}

    def dev_y(self, step):
        return {"exp": self.e, "ctx": self.at_y(step) * 2 + self.k}


def remote(src, dst, send, recv, device):
    return pltpu.make_async_remote_copy(
        src_ref=src, dst_ref=dst, send_sem=send, recv_sem=recv, device_id=device,
        device_id_type=MESH,
    )


def exchange(here, send_ref, recv_ref, send_sem, recv_sem):
    def desc(o):
        dest = (here.e + o) % NE
        return remote(
            send_ref.at[dest], recv_ref.at[here.e], send_sem.at[o], recv_sem.at[o],
            {"exp": dest, "ctx": here.c},
        )

    def incoming(o):
        source = (here.e + NE - o) % NE
        return remote(
            send_ref.at[source], recv_ref.at[source], send_sem.at[o], recv_sem.at[o],
            {"exp": source, "ctx": here.c},
        )

    def begin(first, last):
        def go(o, carry):
            desc(o).start()
            return carry

        lax.fori_loop(first, last, go, 0)

    def finish():
        def go(o, carry):
            desc(o).wait_send()
            incoming(o).wait_recv()
            return carry

        lax.fori_loop(1, NE, go, 0)

    return begin, finish


def add16(*refs):
    total = refs[0].astype(F32)
    for r in refs[1:]:
        total = total + r.astype(F32)
    return total


ORDER = [4, -3, 3, -2, 2, -1, 1, 0]
DEEP = NZ // 2
KEYS = NX * TOK


def layer_kernel(
    ids_ref, gain_ref, x_ref, g_ref, key_ref, val_ref, q_hbm, do_hbm, gate_hbm, up_hbm, down_hbm,
    ao_ref, dq_ref, ret_ref, kvg_ref,
    q_ref, do_ref, gate_ref, up_ref, down_ref,
    send, recv, rows_ref, part, pmate, ysend, yrecv, full,
    kv, qs, dos, e_ref, mj, m_ref, l_ref, o_ref, d_ref, dq_acc,
    dkv, dmate, zsend, zrecv, own4, xsend, xrecv, tsend, trecv, kg, back,
    s_in, s_l, s_far, r_far, s_kx, r_kx, s_kz, r_kz, s_km, r_km,
    s_pm, r_pm, s_y, r_y, s_g, r_g, s_gm, r_gm,
    s_dm, r_dm, s_z, r_z, s_x, r_x, s_t, r_t, s_c, r_c, s_cm, r_cm, s_ret, r_ret,
):
    here = Place()
    k, z, x, e = here.k, here.z, here.x, here.e
    barrier = pltpu.get_barrier_semaphore()

    def greet(device):
        pl.semaphore_signal(barrier, inc=1, device_id=device, device_id_type=MESH)

    near = [here.mate] + [here.dev_y(s) for s in (1, -1, 2, -2, 4)]
    for device in near:
        greet(device)

    def greet_far(o, carry):
        greet({"exp": (e + o) % NE, "ctx": here.c})
        return carry

    lax.fori_loop(1, NE, greet_far, 0)

    loads = [
        pltpu.make_async_copy(a, b, s_in.at[i])
        for i, (a, b) in enumerate(
            [(gate_hbm, gate_ref), (up_hbm, up_ref), (down_hbm, down_ref), (q_hbm, q_ref), (do_hbm, do_ref)]
        )
    ]
    for c in loads:
        c.start()
    cols = pl.ds(pl.multiple_of((here.y // 2) * HEAD, HEAD), HEAD)
    own = kv.at[k, z, x]

    @pl.when(k == 0)
    def _():
        pltpu.make_async_copy(key_ref.at[:, cols], own, s_l.at[0]).start()

    @pl.when(k == 1)
    def _():
        pltpu.make_async_copy(val_ref.at[:, cols], own, s_l.at[0]).start()

    prepare(ids_ref, gain_ref, x_ref, g_ref, send)
    pltpu.make_async_copy(key_ref.at[:, cols], own, s_l.at[0]).wait()
    pl.semaphore_wait(barrier, len(near) + NE - 1)

    sends = []

    def go(c):
        c.start()
        sends.append(c)

    begin, finish = exchange(here, send, recv, s_far, r_far)
    begin(1, NE)
    local = pltpu.make_async_copy(send.at[e], recv.at[e], s_l.at[1])
    local.start()

    def block(step):
        return kv.at[k, z, here.at_x(step)]

    def slab(step):
        return kv.at[k, here.at_z(step)]

    def xcopy(i, origin, to):
        return remote(block(origin), block(origin), s_kx.at[i], r_kx.at[i], here.dev_x(to))

    def zcopy(i, origin, to):
        return remote(slab(origin), slab(origin), s_kz.at[i], r_kz.at[i], here.dev_z(to))

    def kv_mate(i, origin):
        return remote(slab(origin), slab(origin), s_km.at[i], r_km.at[i], here.mate)

    go(xcopy(0, 0, 1))
    go(xcopy(2, 0, -1))
    xcopy(0, -1, 1).wait_recv()
    go(xcopy(1, -1, 1))
    xcopy(2, 1, -1).wait_recv()
    xcopy(1, -2, 1).wait_recv()
    go(zcopy(0, 0, 1))
    go(zcopy(DEEP, 0, -1))
    go(kv_mate(0, 0))

    def kv_step(s):
        zcopy(s - 1, -s, 1).wait_recv()
        if s < DEEP:
            go(zcopy(s, -s, 1))
        go(kv_mate(s, -s))
        if s < DEEP:
            zcopy(DEEP + s - 1, s, -1).wait_recv()
            if s < DEEP - 1:
                go(zcopy(DEEP + s, s, -1))
            go(kv_mate(DEEP + s, s))

    def kv_from_mate(i, step):
        spot = kv.at[1 - k, here.at_z(step)]
        remote(spot, spot, s_km.at[i], r_km.at[i], here.mate).wait_recv()

    def kv_ready(d):
        kv_from_mate(d, d)
        if 0 < d < DEEP:
            kv_from_mate(DEEP + d, -d)

    for c in loads:
        c.wait()
    local.wait()
    finish()

    table = pack_table(False)
    n = 4 * PACK
    for g in range(NE // 8):
        slabs = recv[g * 8 : (g + 1) * 8].reshape(n, 128)
        packed = dot(table, slabs).astype(BF16)
        for i in range(4):
            rows_ref[i // 2, g * PACK : (g + 1) * PACK, (i % 2) * 128 : (i % 2 + 1) * 128] = packed[
                i * PACK : (i + 1) * PACK, :
            ]
    first = first_local(ROWS)

    def product(m):
        if m < 2:
            w_ref = (gate_ref, up_ref)[m]
            rows = rows_ref[0]
            whole = jnp.where(first, dot(rows, w_ref[0]), dot(rows, w_ref[1]))
        else:
            rows = rows_ref[1]
            whole = jnp.where(first, dot_t(rows, down_ref[0]), dot_t(rows, down_ref[1]))
        whole = whole.astype(BF16)
        for c in range(2):
            for y in range(NY):
                part[c, y, m] = whole[y * YROWS : (y + 1) * YROWS, c * HALF : (c + 1) * HALF]
        for i, step in enumerate(ORDER):
            d = here.at_y(-step)
            j = m * 8 + i
            go(remote(part.at[1 - k, d, m], pmate.at[d, m], s_pm.at[j], r_pm.at[j], here.mate))

    def part_in(i, m):
        d = here.at_y(ORDER[i])
        j = m * 8 + i
        remote(part.at[k, d, m], pmate.at[d, m], s_pm.at[j], r_pm.at[j], here.mate).wait_recv()
        return d

    def yslot(i, m, to):
        j = m * 7 + i
        return remote(ysend.at[j], yrecv.at[j], s_y.at[j], r_y.at[j], here.dev_y(to))

    def y_step(s, m):
        d = part_in(ORDER.index(DEEP - s), m)
        j = m * 7 + s
        if s == 0:
            ysend[j] = add16(part[k, d, m], pmate[d, m]).astype(BF16)
        else:
            yslot(s - 1, m, 1).wait_recv()
            ysend[j] = add16(part[k, d, m], pmate[d, m], yrecv[j - 1]).astype(BF16)
        go(yslot(s, m, 1))
        if s < DEEP - 1:
            d = part_in(ORDER.index(s + 1 - DEEP), m)
            j = m * 7 + DEEP + s
            if s == 0:
                ysend[j] = add16(part[k, d, m], pmate[d, m]).astype(BF16)
            else:
                yslot(DEEP + s - 1, m, -1).wait_recv()
                ysend[j] = add16(part[k, d, m], pmate[d, m], yrecv[j - 1]).astype(BF16)
            go(yslot(DEEP + s, m, -1))

    def gcopy(i, m, origin, to):
        spot = full.at[k, here.at_y(origin), m]
        j = m * 7 + i
        return remote(spot, spot, s_g.at[j], r_g.at[j], here.dev_y(to))

    def g_mate(i, m, origin):
        spot = full.at[k, here.at_y(origin), m]
        j = m * 8 + i
        return remote(spot, spot, s_gm.at[j], r_gm.at[j], here.mate)

    def activate():
        total = []
        for m in range(3):
            d = part_in(ORDER.index(0), m)
            yslot(2 * DEEP - 2, m, -1).wait_recv()
            yslot(DEEP - 1, m, 1).wait_recv()
            total.append(
                add16(part[k, d, m], pmate[d, m], yrecv[m * 7 + 2 * DEEP - 2], yrecv[m * 7 + DEEP - 1])
            )
        gate, up, hidden_grad = total
        sig = 1.0 / (1.0 + jnp.exp(-gate))
        act = gate * sig
        full[k, here.y, 0] = (act * up).astype(BF16)
        full[k, here.y, 1] = (hidden_grad * up * sig * (1.0 + gate * (1.0 - sig))).astype(BF16)
        full[k, here.y, 2] = (hidden_grad * act).astype(BF16)
        for m in range(3):
            go(gcopy(0, m, 0, 1))
            go(gcopy(DEEP, m, 0, -1))
        for m in range(3):
            go(g_mate(0, m, 0))

    def gather_step(s):
        for m in range(3):
            gcopy(s - 1, m, -s, 1).wait_recv()
            if s < DEEP:
                go(gcopy(s, m, -s, 1))
            go(g_mate(s, m, -s))
            if s < DEEP:
                gcopy(DEEP + s - 1, m, s, -1).wait_recv()
                if s < DEEP - 1:
                    go(gcopy(DEEP + s, m, s, -1))
                go(g_mate(DEEP + s, m, s))

    def gather_from_mate():
        for m in range(3):
            pairs = [(s, s) for s in range(DEEP + 1)] + [(DEEP + s, -s) for s in range(1, DEEP)]
            for i, step in pairs:
                spot = full.at[1 - k, here.at_y(step), m]
                j = m * 8 + i
                remote(spot, spot, s_gm.at[j], r_gm.at[j], here.mate).wait_recv()

    heads = q_ref.shape[1] // HEAD
    width = heads * TOK

    def stack():
        for h in range(heads):
            qs[h * TOK : (h + 1) * TOK, :] = q_ref[:, h * HEAD : (h + 1) * HEAD]
            dos[h * TOK : (h + 1) * TOK, :] = do_ref[:, h * HEAD : (h + 1) * HEAD]
        m_ref[...] = jnp.full((1, width), -jnp.inf, F32)
        l_ref[...] = jnp.zeros((1, width), F32)
        o_ref[...] = jnp.zeros((HEAD, width), F32)
        dq_acc[...] = jnp.zeros((HEAD, width), F32)

    def forward(step):
        j = here.at_z(step)
        lane = lax.broadcasted_iota(jnp.int32, (1, width), 1)
        q_pos = e * TOK + jnp.bitwise_and(lane, TOK - 1)
        row = lax.broadcasted_iota(jnp.int32, (KEYS, 1), 0) + j * KEYS
        s = dot_t(kv[0, j].reshape(KEYS, HEAD), qs[...]) * SCALE
        s = jnp.where(row <= q_pos, s, -jnp.inf)
        old = m_ref[...]
        m = jnp.maximum(old, jnp.max(s, axis=0, keepdims=True))
        p = jnp.exp(s - m)
        p16 = p.astype(BF16)
        e_ref[j] = p16
        mj[j] = m
        m_ref[...] = m
        fade = jnp.exp(old - m)
        l_ref[...] = l_ref[...] * fade + jnp.sum(p, axis=0, keepdims=True)
        o_ref[...] = o_ref[...] * fade + t_dot(kv[1, j].reshape(KEYS, HEAD), p16)

    def normalize():
        inv = 1.0 / l_ref[...]
        l_ref[...] = inv
        o16 = (o_ref[...] * inv).astype(BF16)
        turned = o16.astype(F32).T
        for h in range(heads):
            ao_ref[:, h * HEAD : (h + 1) * HEAD] = turned[h * TOK : (h + 1) * TOK, :].astype(BF16)
        do_t = dos[...].astype(F32).T
        d_ref[...] = jnp.sum(do_t * o16.astype(F32), axis=0, keepdims=True)

    def backward(step):
        j = here.at_z(step)
        keys = kv[0, j].reshape(KEYS, HEAD)
        dp = dot_t(kv[1, j].reshape(KEYS, HEAD), dos[...])
        p = e_ref[j].astype(F32) * (jnp.exp(mj[j] - m_ref[...]) * l_ref[...])
        ds = (p * (dp - d_ref[...])).astype(BF16)
        dkv[0, j] = (dot(ds, qs[...]) * SCALE).astype(BF16).reshape(NX, TOK, HEAD)
        dkv[1, j] = dot(p.astype(BF16), dos[...]).astype(BF16).reshape(NX, TOK, HEAD)
        dq_acc[...] += t_dot(keys, ds)
        i = ORDER.index(step if step == DEEP else -step)
        go(remote(dkv.at[1 - k, j], dmate.at[j], s_dm.at[i], r_dm.at[i], here.mate))

    def query_grad():
        turned = (dq_acc[...] * SCALE).T
        for h in range(heads):
            dq_ref[:, h * HEAD : (h + 1) * HEAD] = turned[h * TOK : (h + 1) * TOK, :].astype(BF16)

    def dkv_in(i):
        d = here.at_z(ORDER[i])
        remote(dkv.at[k, d], dmate.at[d], s_dm.at[i], r_dm.at[i], here.mate).wait_recv()
        return d

    def zslot(i, to):
        return remote(zsend.at[i], zrecv.at[i], s_z.at[i], r_z.at[i], here.dev_z(to))

    def z_step(s):
        d = dkv_in(ORDER.index(DEEP - s))
        if s == 0:
            zsend[0] = add16(dkv[k, d], dmate[d]).astype(BF16)
        else:
            zslot(s - 1, 1).wait_recv()
            zsend[s] = add16(dkv[k, d], dmate[d], zrecv[s - 1]).astype(BF16)
        go(zslot(s, 1))
        if s < DEEP - 1:
            d = dkv_in(ORDER.index(s + 1 - DEEP))
            i = DEEP + s
            if s == 0:
                zsend[i] = add16(dkv[k, d], dmate[d]).astype(BF16)
            else:
                zslot(i - 1, -1).wait_recv()
                zsend[i] = add16(dkv[k, d], dmate[d], zrecv[i - 1]).astype(BF16)
            go(zslot(i, -1))

    def xslot(i, to):
        return remote(xsend.at[i], xrecv.at[i], s_x.at[i], r_x.at[i], here.dev_x(to))

    def x_first():
        d = dkv_in(ORDER.index(0))
        zslot(2 * DEEP - 2, -1).wait_recv()
        zslot(DEEP - 1, 1).wait_recv()
        own4[...] = add16(dkv[k, d], dmate[d], zrecv[2 * DEEP - 2], zrecv[DEEP - 1])
        xsend[0] = own4[here.at_x(2)].astype(BF16)
        go(xslot(0, 1))
        xsend[2] = own4[here.at_x(-1)].astype(BF16)
        go(xslot(2, -1))

    def x_second():
        xslot(0, 1).wait_recv()
        xsend[1] = add16(own4[here.at_x(1)], xrecv[0]).astype(BF16)
        go(xslot(1, 1))

    twin = remote(tsend, trecv, s_t.at[0], r_t.at[0], here.twin)

    def x_third():
        xslot(2, -1).wait_recv()
        xslot(1, 1).wait_recv()
        tsend[...] = add16(own4[x], xrecv[2], xrecv[1]).astype(BF16)
        go(twin)

    def spot(which, step):
        head = here.at_y(step) // 2
        return kvg_ref.at[which, :, pl.ds(pl.multiple_of(head * HEAD, HEAD), HEAD)]

    mine = pltpu.make_async_copy(kg, spot(k, 0), s_l.at[2])

    def spread():
        twin.wait_recv()
        kg[...] = add16(tsend[...], trecv[...]).astype(BF16)
        for i, step in enumerate((2, 4, 6)):
            go(remote(kg, spot(k, 0), s_c.at[i], r_c.at[i], here.dev_y(step)))
        go(remote(kg, spot(k, 0), s_cm.at[3], r_cm.at[3], here.mate))
        mine.start()

    def spread_end():
        for i, step in enumerate((2, 4, 6)):
            remote(kg, spot(k, -step), s_c.at[i], r_c.at[i], here.dev_y(-step)).wait_recv()
            go(remote(spot(k, -step), spot(k, -step), s_cm.at[i], r_cm.at[i], here.mate))
        for i, step in enumerate((2, 4, 6)):
            there = spot(1 - k, step)
            remote(there, there, s_cm.at[i], r_cm.at[i], here.mate).wait_recv()
        remote(kg, spot(1 - k, 0), s_cm.at[3], r_cm.at[3], here.mate).wait_recv()
        mine.wait()

    ret_begin, ret_finish = exchange(here, back, ret_ref, s_ret, r_ret)
    ret_local = pltpu.make_async_copy(back.at[e], ret_ref.at[e], s_l.at[3])

    def experts_out():
        def both(m, weight, transposed):
            halves = [full[c, :, m].reshape(ROWS, HALF) for c in range(2)]
            whole = jnp.concatenate(halves, axis=1)
            f = dot_t if transposed else dot
            return jnp.where(first, f(whole, weight[0]), f(whole, weight[1]))

        route_out = both(0, down_ref, False).astype(BF16)
        route_in = (both(1, gate_ref, True) + both(2, up_ref, True)).astype(BF16)
        quarters = [route_out[:, :128], route_out[:, 128:], route_in[:, :128], route_in[:, 128:]]
        unpack = pack_table(True)
        for g in range(NE // 8):
            stacked = jnp.concatenate([q[g * PACK : (g + 1) * PACK] for q in quarters], axis=0)
            back[g * 8 : (g + 1) * 8] = dot(unpack, stacked).astype(BF16).reshape(8, SLAB, 128)
        ret_begin(1, NE)
        ret_local.start()

    product(0)
    kv_step(1)
    product(1)
    y_step(0, 0)
    product(2)
    y_step(0, 1)
    kv_step(2)
    y_step(0, 2)
    stack()
    kv_ready(0)
    forward(0)
    for m in range(3):
        y_step(1, m)
    kv_step(3)
    kv_ready(1)
    forward(-1)
    forward(1)
    for m in range(3):
        y_step(2, m)
    kv_step(4)
    kv_ready(2)
    forward(-2)
    forward(2)
    for m in range(3):
        y_step(3, m)
    kv_ready(3)
    forward(-3)
    forward(3)
    activate()
    kv_ready(4)
    forward(4)
    normalize()
    gather_step(1)
    backward(4)
    backward(-3)
    gather_step(2)
    backward(3)
    z_step(0)
    backward(-2)
    gather_step(3)
    backward(2)
    z_step(1)
    backward(-1)
    gather_step(4)
    gather_from_mate()
    experts_out()
    backward(1)
    z_step(2)
    backward(0)
    z_step(3)
    query_grad()
    x_first()
    x_second()
    x_third()
    spread()
    spread_end()
    ret_finish()
    ret_local.wait()
    for c in sends:
        c.wait_send()


def vmem():
    return pl.BlockSpec(memory_space=pltpu.VMEM)


def dma(n):
    return pltpu.SemaphoreType.DMA((n,))


def call(kernel, outs, scratch, *args, specs=None, collective=None, name=None, flops=0):
    params = {"vmem_limit_bytes": VMEM_LIMIT}
    if collective is not None:
        params.update(collective_id=collective, has_side_effects=True)
    return pl.pallas_call(
        kernel,
        out_shape=outs,
        in_specs=specs or [vmem()] * len(args),
        out_specs=jax.tree.map(lambda o: vmem(), outs),
        scratch_shapes=scratch,
        compiler_params=pltpu.CompilerParams(**params),
        name=name,
    )(*args)


def shape(*dims, dtype=BF16):
    return jax.ShapeDtypeStruct(dims, dtype)


def body(q, key, val, do, x, g, ids, gain, gate, up, down):
    ids, gain = ids.T, gain.T
    hbm = pl.BlockSpec(memory_space=pl.ANY)
    heads = q.shape[1] // HEAD
    width = heads * TOK
    yslab, zslab, block = (YROWS, HALF), (NX, TOK, HEAD), (TOK, HEAD)

    def f32(*dims):
        return pltpu.VMEM(dims, F32)

    def b16(*dims):
        return pltpu.VMEM(dims, BF16)

    sems = [5, 4, NE, NE, 3, 3, 8, 8, 8, 8, 24, 24, 21, 21, 21, 21, 24, 24]
    sems += [8, 8, 7, 7, 3, 3, 1, 1, 3, 3, 4, 4, NE, NE]
    attn_out, dq, returned, kvg = call(
        layer_kernel,
        (shape(*q.shape), shape(*q.shape), shape(NE, SLAB, 128), shape(2, TOK, 4 * HEAD)),
        [
            b16(*q.shape), b16(*do.shape), b16(*gate.shape), b16(*up.shape), b16(*down.shape),
            b16(NE, SLAB, 128), b16(NE, SLAB, 128), b16(2, ROWS, 256),
            b16(2, NY, 3, *yslab), b16(NY, 3, *yslab), b16(21, *yslab), b16(21, *yslab),
            b16(2, NY, 3, *yslab),
            b16(2, NZ, *zslab), b16(width, HEAD), b16(width, HEAD), b16(NZ, KEYS, width),
            f32(NZ, 1, width), f32(1, width), f32(1, width), f32(HEAD, width), f32(1, width),
            f32(HEAD, width),
            b16(2, NZ, *zslab), b16(NZ, *zslab), b16(7, *zslab), b16(7, *zslab), f32(*zslab),
            b16(3, *block), b16(3, *block), b16(*block), b16(*block), b16(*block),
            b16(NE, SLAB, 128),
        ]
        + [dma(n) for n in sems],
        ids, gain, x, g, key, val, q, do, gate, up, down,
        specs=[vmem()] * 4 + [hbm] * 7, collective=0, name="layer",
    )
    moe_out, input_grad, key_grad, value_grad, attn_out, dq = call(
        combine_kernel,
        (shape(TOK, 256), shape(TOK, 256), shape(TOK, 512), shape(TOK, 512),
         shape(*q.shape), shape(*q.shape)), [],
        ids, gain, returned.reshape(NE * SLAB, 128), kvg, attn_out, dq, name="combine",
    )
    return attn_out, dq, key_grad, value_grad, moe_out, input_grad


def solution(mesh):
    rows, both = P("exp", None), P("exp", "ctx")
    return jax.shard_map(
        body,
        mesh=mesh,
        in_specs=(
            both, rows, rows, both, both, both, rows, rows,
            P("exp", "ctx", None), P("exp", "ctx", None), P("exp", None, "ctx"),
        ),
        out_specs=(both, both, rows, rows, both, both),
        check_vma=False,
    )
```

```python
import functools

import jax
import jax.numpy as jnp
from jax import lax
from jax.experimental import pallas as pl
from jax.experimental.pallas import tpu as pltpu
from jax.sharding import PartitionSpec as P

MESH = pl.DeviceIdType.MESH
F32 = jnp.float32
BF16 = jnp.bfloat16
HEAD = 128
NX, NZ, NY = 4, 8, 8
NE = NX * NZ
TOK = 128
LOCAL = 2
EXPERTS = LOCAL * NE
SLOT = 6
GROUP = LOCAL * SLOT
SLAB = 4 * GROUP
ROWS = NE * GROUP
FF = 768
HALF = FF // 2
YROWS = ROWS // NY
SCALE = HEAD ** (-0.5)
VMEM_LIMIT = 60 * 1024 * 1024


def dot(a, b):
    return jnp.dot(a, b, preferred_element_type=F32)


def dot_t(a, b):
    return lax.dot_general(a, b, (((1,), (1,)), ((), ())), preferred_element_type=F32)


def t_dot(a, b):
    return lax.dot_general(a, b, (((0,), (0,)), ((), ())), preferred_element_type=F32)


def fdiv(a, n):
    return jnp.floor((a + 0.5) * (1.0 / n))


def fiota(shape, dim):
    return lax.broadcasted_iota(jnp.int32, shape, dim).astype(F32)


def column(row):
    return jnp.broadcast_to(row, (TOK, TOK)).T


def route_tables(ids):
    lane = fiota((TOK, EXPERTS), 1)
    ids = ids.astype(F32)
    first = jnp.where(column(ids[0:1])[:, :EXPERTS] == lane, 1.0, 0.0)
    second = jnp.where(column(ids[1:2])[:, :EXPERTS] == lane, 1.0, 0.0)
    row = lax.broadcasted_iota(jnp.int32, (TOK, TOK), 0)
    col = lax.broadcasted_iota(jnp.int32, (TOK, TOK), 1)
    before = jnp.where(col < row, 1.0, 0.0).astype(BF16)
    place = dot(before, (first + second).astype(BF16)) + 1.0
    return (first * place).astype(BF16), (second * place).astype(BF16)


def slab_index(p):
    dest = fdiv(p, SLAB)
    inner = p - dest * SLAB
    quarter = fdiv(inner, GROUP)
    inner = inner - quarter * GROUP
    local = fdiv(inner, SLOT)
    slot = inner - local * SLOT
    return dest * LOCAL + local, quarter, slot


def prepare(ids_ref, gain_ref, x_ref, g_ref, out_ref):
    v0, v1 = route_tables(ids_ref[...])
    total = NE * SLAB
    expert, quarter, slot = slab_index(fiota((total, 1), 0))
    pick = jnp.where(expert == fiota((total, EXPERTS), 1), 1.0, 0.0).astype(BF16)
    y0 = dot_t(pick, v0)
    y1 = dot_t(pick, v1)
    want = slot + 1.0
    hit0 = jnp.where(y0 == want, 1.0, 0.0)
    hit1 = jnp.where(y1 == want, 1.0, 0.0)
    both = hit0 + hit1
    q = [jnp.where(quarter == float(i), 1.0, 0.0) for i in range(4)]
    table = jnp.concatenate(
        [both * q[0], both * q[1], hit0 * q[2], hit0 * q[3], hit1 * q[2], hit1 * q[3]], axis=1
    ).astype(BF16)
    x = x_ref[...]
    g = g_ref[...].astype(F32)
    gain = gain_ref[...]
    w0, w1 = column(gain[0:1]), column(gain[1:2])
    lo, hi = g[:, :128], g[:, 128:]
    scaled = [(a * w).astype(BF16) for w in (w0, w1) for a in (lo, hi)]
    rows = jnp.concatenate([x[:, :128], x[:, 128:]] + scaled, axis=0)
    out_ref[...] = dot(table, rows).astype(BF16).reshape(NE, SLAB, 128)


def combine_kernel(
    ids_ref, gain_ref, back_ref, kvg_ref, ao_ref, dq_ref,
    out_ref, in_ref, kg_ref, vg_ref, ao_out, dq_out,
):
    v0, v1 = route_tables(ids_ref[...])
    total = NE * SLAB
    expert, quarter, slot = slab_index(fiota((1, total), 1))
    pick = jnp.where(expert == fiota((EXPERTS, total), 0), 1.0, 0.0).astype(BF16)
    y0 = dot(v0, pick)
    y1 = dot(v1, pick)
    want = slot + 1.0
    hit0 = jnp.where(y0 == want, 1.0, 0.0)
    hit1 = jnp.where(y1 == want, 1.0, 0.0)
    both = hit0 + hit1
    q = [jnp.where(quarter == float(i), 1.0, 0.0) for i in range(4)]
    back = back_ref[...]
    gain = gain_ref[...]
    w0, w1 = column(gain[0:1]), column(gain[1:2])
    for i in range(2):
        part0 = dot((hit0 * q[i]).astype(BF16), back)
        part1 = dot((hit1 * q[i]).astype(BF16), back)
        out_ref[:, i * 128 : (i + 1) * 128] = (part0 * w0 + part1 * w1).astype(BF16)
        in_ref[:, i * 128 : (i + 1) * 128] = dot((both * q[2 + i]).astype(BF16), back).astype(BF16)
    kg_ref[...] = kvg_ref[0]
    vg_ref[...] = kvg_ref[1]
    ao_out[...] = ao_ref[...]
    dq_out[...] = dq_ref[...]


PACK = 8 * GROUP


def pack_table(transposed, rows):
    n = 4 * rows
    r = fiota((1, n) if transposed else (n, 1), 1 if transposed else 0)
    quarter = fdiv(r, rows)
    inner = r - quarter * rows
    source = fdiv(inner, GROUP)
    p = source * SLAB + quarter * GROUP + (inner - source * GROUP)
    return jnp.where(p == fiota((n, n), 0 if transposed else 1), 1.0, 0.0).astype(BF16)


def first_local(rows):
    r = fiota((rows, 1), 0)
    inner = r - fdiv(r, GROUP) * GROUP
    return inner < float(SLOT)


def source(y, i):
    return ((y - 2 * i + 2 * NZ) % NZ) * NX + i


class Place:
    def __init__(self):
        self.e = lax.axis_index("exp")
        self.c = lax.axis_index("ctx")
        self.z, self.x = self.e // NX, self.e % NX
        self.y, self.k = self.c // 2, self.c % 2
        self.sgn = 1 - 2 * self.k
        self.mate = {"exp": self.e, "ctx": self.y * 2 + 1 - self.k}
        self.twin = {"exp": self.e, "ctx": (self.y + 1 - 2 * (self.y % 2)) * 2 + self.k}

    def at_z(self, step):
        return (self.z + self.sgn * step + 2 * NZ) % NZ

    def at_x(self, step):
        return (self.x + self.sgn * step + 2 * NX) % NX

    def at_y(self, step):
        return (self.y + self.sgn * step + 2 * NY) % NY

    def dev_z(self, step):
        return {"exp": self.at_z(step) * NX + self.x, "ctx": self.c}

    def dev_x(self, step):
        return {"exp": self.z * NX + self.at_x(step), "ctx": self.c}

    def dev_y(self, step):
        return {"exp": self.e, "ctx": self.at_y(step) * 2 + self.k}


def remote(src, dst, send, recv, device):
    return pltpu.make_async_remote_copy(
        src_ref=src, dst_ref=dst, send_sem=send, recv_sem=recv, device_id=device,
        device_id_type=MESH,
    )


def exchange(here, send_ref, recv_ref, send_sem, recv_sem, single=False):
    def desc(o):
        dest = (here.e + o) % NE
        return remote(
            send_ref.at[dest], recv_ref.at[here.e], send_sem.at[o], recv_sem.at[o],
            {"exp": dest, "ctx": here.c},
        )

    def incoming(o):
        source = (here.e + NE - o) % NE
        return remote(
            send_ref.at[source], recv_ref.at[source], send_sem.at[o], recv_sem.at[o],
            {"exp": source, "ctx": here.c},
        )

    def begin(first, last):
        def go(o, carry):
            desc(o).start()
            return carry

        lax.fori_loop(first, last, go, 0)

    def finish():
        def go(o, carry):
            desc(o).wait_send()
            incoming(o).wait_recv()
            return carry

        lax.fori_loop(1, NE, go, 0)

    return (desc if single else begin), finish


def add16(*refs):
    total = refs[0].astype(F32)
    for r in refs[1:]:
        total = total + r.astype(F32)
    return total


ORDER = [4, -3, 3, -2, 2, -1, 1, 0]
STEPS = [0, -1, 1, -2, 2, -3, 3, 4]
LANES = [0, -1, 1, -2]
DEEP = NZ // 2
KEYS = NX * TOK


def around(s):
    return [s] if s in (0, DEEP) else [-s, s]


def opposite(step):
    return step if step == DEEP else -step


def layer_kernel(
    ids_ref, gain_ref, x_ref, g_ref, key_ref, val_ref, q_hbm, do_hbm, gate_hbm, up_hbm, down_hbm,
    ao_ref, dq_ref, ret_ref, kvg_ref,
    q_ref, do_ref, gate_ref, up_ref, down_ref,
    send, recv, rows_ref, part, pmate, ysend, yrecv, full,
    kv, qs, dos, e_ref, mj, m_ref, l_ref, o_ref, d_ref, dq_acc,
    dkv, dmate, zsend, zrecv, sums, xsend, xrecv, tsend, trecv, kg, back,
    s_in, s_l, s_far, r_far, s_kx, r_kx, s_kz, r_kz, s_km, r_km,
    s_pm, r_pm, s_y, r_y, s_g, r_g, s_gm, r_gm,
    s_dm, r_dm, s_z, r_z, s_x, r_x, s_t, r_t, s_c, r_c, s_cm, r_cm, s_ret, r_ret,
):
    here = Place()
    k, z, x, e = here.k, here.z, here.x, here.e
    barrier = pltpu.get_barrier_semaphore()

    def greet(device):
        pl.semaphore_signal(barrier, inc=1, device_id=device, device_id_type=MESH)

    near = [here.mate] + [here.dev_y(s) for s in (1, -1, 2, -2, 4)]
    for device in near:
        greet(device)

    def greet_far(o, carry):
        greet({"exp": (e + o) % NE, "ctx": here.c})
        return carry

    lax.fori_loop(1, NE, greet_far, 0)

    loads = [
        pltpu.make_async_copy(a, b, s_in.at[i])
        for i, (a, b) in enumerate(
            [(gate_hbm, gate_ref), (up_hbm, up_ref), (down_hbm, down_ref), (q_hbm, q_ref), (do_hbm, do_ref)]
        )
    ]
    for c in loads:
        c.start()
    cols = pl.ds(pl.multiple_of((here.y // 2) * HEAD, HEAD), HEAD)
    own = kv.at[k, z, x]

    @pl.when(k == 0)
    def _():
        pltpu.make_async_copy(key_ref.at[:, cols], own, s_l.at[0]).start()

    @pl.when(k == 1)
    def _():
        pltpu.make_async_copy(val_ref.at[:, cols], own, s_l.at[0]).start()

    prepare(ids_ref, gain_ref, x_ref, g_ref, send)
    pltpu.make_async_copy(key_ref.at[:, cols], own, s_l.at[0]).wait()
    pl.semaphore_wait(barrier, len(near) + NE - 1)

    sends = []
    core_sends = ([], [])

    def go(c):
        c.start()
        sends.append(c)

    def by_core(zero, one):
        for core, f in enumerate((zero, one)):

            def start(make, *args, core=core):
                make(*args).start()
                core_sends[core].append((make, args))

            @pl.when(k == core)
            def _(f=f, start=start):
                f(start)

    begin, finish = exchange(here, send, recv, s_far, r_far)
    local = pltpu.make_async_copy(send.at[e], recv.at[e], s_l.at[1])
    local.start()

    def kz(j, zs, xs, to):
        spot = kv.at[k, here.at_z(zs), here.at_x(xs)]
        return remote(spot, spot, s_kz.at[j], r_kz.at[j], here.dev_z(to))

    def kx(j, zs, xs, to):
        spot = kv.at[k, here.at_z(zs), here.at_x(xs)]
        return remote(spot, spot, s_kx.at[j], r_kx.at[j], here.dev_x(to))

    def kv_mate(step):
        i, spot = STEPS.index(step), kv.at[k, here.at_z(step)]
        return remote(spot, spot, s_km.at[i], r_km.at[i], here.mate)

    def lane_start(start, xs):
        i = LANES.index(xs) * 8
        start(kz, i, 0, xs, 1)
        start(kz, i + DEEP, 0, xs, -1)

    def lane_step(start, s):
        for i, xs in enumerate(LANES):
            kz(i * 8 + s - 1, -s, xs, 1).wait_recv()
            if s < DEEP:
                start(kz, i * 8 + s, -s, xs, 1)
                kz(i * 8 + DEEP + s - 1, s, xs, -1).wait_recv()
                if s < DEEP - 1:
                    start(kz, i * 8 + DEEP + s, s, xs, -1)
        for step in around(s):
            start(kv_mate, step)

    def cross_start(start, s):
        for step in around(s):
            i = STEPS.index(step) * 3
            start(kx, i, step, 0, 1)
            start(kx, i + 2, step, 0, -1)

    def cross_mid(start, s):
        for step in around(s):
            i = STEPS.index(step) * 3
            kx(i, step, -1, 1).wait_recv()
            start(kx, i + 1, step, -1, 1)
            kx(i + 2, step, 1, -1).wait_recv()

    def cross_end(start, s):
        for step in around(s):
            kx(STEPS.index(step) * 3 + 1, step, -2, 1).wait_recv()
            start(kv_mate, step)

    def kv_step(t):
        def zero(start):
            if t == 0:
                start(kx, 0, 0, 0, 1)
                start(kx, 2, 0, 0, -1)
                lane_start(start, 0)
            elif t == 1:
                kx(0, 0, -1, 1).wait_recv()
                start(kx, 1, 0, -1, 1)
                lane_start(start, -1)
                kx(2, 0, 1, -1).wait_recv()
                lane_start(start, 1)
            elif t == 2:
                kx(1, 0, -2, 1).wait_recv()
                lane_start(start, -2)
                start(kv_mate, 0)
            else:
                lane_step(start, t - 2)

        def one(start):
            if t == 0:
                start(kz, 0, 0, 0, 1)
                start(kz, DEEP, 0, 0, -1)
                cross_start(start, 0)
                return
            if t <= DEEP:
                kz(t - 1, -t, 0, 1).wait_recv()
                if t < DEEP:
                    start(kz, t, -t, 0, 1)
                    kz(DEEP + t - 1, t, 0, -1).wait_recv()
                    if t < DEEP - 1:
                        start(kz, DEEP + t, t, 0, -1)
                cross_start(start, t)
            if t <= DEEP + 1:
                cross_mid(start, t - 1)
            if t >= 2:
                cross_end(start, t - 2)

        by_core(zero, one)

    def kv_ready(s):
        for step in around(s):
            i, spot = STEPS.index(opposite(step)), kv.at[1 - k, here.at_z(step)]
            remote(spot, spot, s_km.at[i], r_km.at[i], here.mate).wait_recv()

    def pack():
        table = pack_table(False, PACK)
        for g in range(NE // 8):
            slabs = [recv[source(y, i)] for y in (2 * g, 2 * g + 1) for i in range(NX)]
            packed = dot(table, jnp.concatenate(slabs, axis=0)).astype(BF16)
            for i in range(4):
                lanes = slice((i % 2) * 128, (i % 2 + 1) * 128)
                rows_ref[i // 2, g * PACK : (g + 1) * PACK, lanes] = packed[
                    i * PACK : (i + 1) * PACK, :
                ]

    first = first_local(ROWS)

    def product(m):
        if m < 2:
            w_ref = (gate_ref, up_ref)[m]
            rows = rows_ref[0]
            whole = jnp.where(first, dot(rows, w_ref[0]), dot(rows, w_ref[1]))
        else:
            rows = rows_ref[1]
            whole = jnp.where(first, dot_t(rows, down_ref[0]), dot_t(rows, down_ref[1]))
        whole = whole.astype(BF16)
        for c in range(2):
            for y in range(NY):
                part[c, y, m] = whole[y * YROWS : (y + 1) * YROWS, c * HALF : (c + 1) * HALF]
        for i, step in enumerate(ORDER):
            d = here.at_y(-step)
            j = m * 8 + i
            go(remote(part.at[1 - k, d, m], pmate.at[d, m], s_pm.at[j], r_pm.at[j], here.mate))

    def part_in(i, m):
        d = here.at_y(ORDER[i])
        j = m * 8 + i
        remote(part.at[k, d, m], pmate.at[d, m], s_pm.at[j], r_pm.at[j], here.mate).wait_recv()
        return d

    def yslot(i, m, to):
        j = m * 7 + i
        return remote(ysend.at[j], yrecv.at[j], s_y.at[j], r_y.at[j], here.dev_y(to))

    def y_step(s, m):
        d = part_in(ORDER.index(DEEP - s), m)
        j = m * 7 + s
        if s == 0:
            ysend[j] = add16(part[k, d, m], pmate[d, m]).astype(BF16)
        else:
            yslot(s - 1, m, 1).wait_recv()
            ysend[j] = add16(part[k, d, m], pmate[d, m], yrecv[j - 1]).astype(BF16)
        go(yslot(s, m, 1))
        if s < DEEP - 1:
            d = part_in(ORDER.index(s + 1 - DEEP), m)
            j = m * 7 + DEEP + s
            if s == 0:
                ysend[j] = add16(part[k, d, m], pmate[d, m]).astype(BF16)
            else:
                yslot(DEEP + s - 1, m, -1).wait_recv()
                ysend[j] = add16(part[k, d, m], pmate[d, m], yrecv[j - 1]).astype(BF16)
            go(yslot(DEEP + s, m, -1))

    def gcopy(i, m, origin, to):
        spot = full.at[k, here.at_y(origin), m]
        j = m * 7 + i
        return remote(spot, spot, s_g.at[j], r_g.at[j], here.dev_y(to))

    def g_mate(i, m, origin):
        spot = full.at[k, here.at_y(origin), m]
        j = m * 8 + i
        return remote(spot, spot, s_gm.at[j], r_gm.at[j], here.mate)

    def activate():
        total = []
        for m in range(3):
            d = part_in(ORDER.index(0), m)
            yslot(2 * DEEP - 2, m, -1).wait_recv()
            yslot(DEEP - 1, m, 1).wait_recv()
            total.append(
                add16(part[k, d, m], pmate[d, m], yrecv[m * 7 + 2 * DEEP - 2], yrecv[m * 7 + DEEP - 1])
            )
        gate, up, hidden_grad = total
        sig = 1.0 / (1.0 + jnp.exp(-gate))
        act = gate * sig
        full[k, here.y, 0] = (act * up).astype(BF16)
        full[k, here.y, 1] = (hidden_grad * up * sig * (1.0 + gate * (1.0 - sig))).astype(BF16)
        full[k, here.y, 2] = (hidden_grad * act).astype(BF16)
        for m in range(3):
            go(gcopy(0, m, 0, 1))
            go(gcopy(DEEP, m, 0, -1))
        for m in range(3):
            go(g_mate(0, m, 0))

    def gather_step(s):
        for m in range(3):
            gcopy(s - 1, m, -s, 1).wait_recv()
            if s < DEEP:
                go(gcopy(s, m, -s, 1))
            go(g_mate(s, m, -s))
            if s < DEEP:
                gcopy(DEEP + s - 1, m, s, -1).wait_recv()
                if s < DEEP - 1:
                    go(gcopy(DEEP + s, m, s, -1))
                go(g_mate(DEEP + s, m, s))

    def gather_ready(s):
        for m in range(3):
            for step in around(s):
                i = s if step != -s or s == 0 else DEEP + s
                spot = full.at[1 - k, here.at_y(step), m]
                j = m * 8 + i
                remote(spot, spot, s_gm.at[j], r_gm.at[j], here.mate).wait_recv()

    heads = q_ref.shape[1] // HEAD
    width = heads * TOK

    def stack():
        for h in range(heads):
            qs[h * TOK : (h + 1) * TOK, :] = q_ref[:, h * HEAD : (h + 1) * HEAD]
            dos[h * TOK : (h + 1) * TOK, :] = do_ref[:, h * HEAD : (h + 1) * HEAD]
        m_ref[...] = jnp.full((1, width), -jnp.inf, F32)
        l_ref[...] = jnp.zeros((1, width), F32)
        o_ref[...] = jnp.zeros((HEAD, width), F32)
        dq_acc[...] = jnp.zeros((HEAD, width), F32)

    def forward(step):
        j = here.at_z(step)
        lane = lax.broadcasted_iota(jnp.int32, (1, width), 1)
        q_pos = e * TOK + jnp.bitwise_and(lane, TOK - 1)
        row = lax.broadcasted_iota(jnp.int32, (KEYS, 1), 0) + j * KEYS
        s = dot_t(kv[0, j].reshape(KEYS, HEAD), qs[...]) * SCALE
        s = jnp.where(row <= q_pos, s, -jnp.inf)
        old = m_ref[...]
        m = jnp.maximum(old, jnp.max(s, axis=0, keepdims=True))
        p = jnp.exp(s - m)
        p16 = p.astype(BF16)
        e_ref[j] = p16
        mj[j] = m
        m_ref[...] = m
        fade = jnp.exp(old - m)
        l_ref[...] = l_ref[...] * fade + jnp.sum(p, axis=0, keepdims=True)
        o_ref[...] = o_ref[...] * fade + t_dot(kv[1, j].reshape(KEYS, HEAD), p16)

    def normalize():
        inv = 1.0 / l_ref[...]
        l_ref[...] = inv
        o16 = (o_ref[...] * inv).astype(BF16)
        turned = o16.astype(F32).T
        for h in range(heads):
            ao_ref[:, h * HEAD : (h + 1) * HEAD] = turned[h * TOK : (h + 1) * TOK, :].astype(BF16)
        do_t = dos[...].astype(F32).T
        d_ref[...] = jnp.sum(do_t * o16.astype(F32), axis=0, keepdims=True)

    def backward(step):
        j = here.at_z(step)
        keys = kv[0, j].reshape(KEYS, HEAD)
        dp = dot_t(kv[1, j].reshape(KEYS, HEAD), dos[...])
        p = e_ref[j].astype(F32) * (jnp.exp(mj[j] - m_ref[...]) * l_ref[...])
        ds = (p * (dp - d_ref[...])).astype(BF16)
        dkv[0, j] = (dot(ds, qs[...]) * SCALE).astype(BF16).reshape(NX, TOK, HEAD)
        dkv[1, j] = dot(p.astype(BF16), dos[...]).astype(BF16).reshape(NX, TOK, HEAD)
        dq_acc[...] += t_dot(keys, ds)
        i = ORDER.index(opposite(step))
        go(remote(dkv.at[1 - k, j], dmate.at[j], s_dm.at[i], r_dm.at[i], here.mate))

    def query_grad():
        turned = (dq_acc[...] * SCALE).T
        for h in range(heads):
            dq_ref[:, h * HEAD : (h + 1) * HEAD] = turned[h * TOK : (h + 1) * TOK, :].astype(BF16)

    def dkv_in(step):
        i, d = ORDER.index(step), here.at_z(step)
        remote(dkv.at[k, d], dmate.at[d], s_dm.at[i], r_dm.at[i], here.mate).wait_recv()
        return d

    def zslot(i, n, to):
        spot = pl.ds(i * n, n)
        return remote(zsend.at[spot], zrecv.at[spot], s_z.at[i], r_z.at[i], here.dev_z(to))

    def xslot(i, to):
        return remote(xsend.at[i], xrecv.at[i], s_x.at[i], r_x.at[i], here.dev_x(to))

    def wide_step(start, s, to):
        d = dkv_in(DEEP - s if to > 0 else s + 1 - DEEP)
        for h in range(2):
            i = (s if to > 0 else DEEP + s) * 2 + h
            blocks = pl.ds(2 * h, 2)
            terms = [dkv[k, d, blocks], dmate[d, blocks]]
            if s:
                zslot(i - 2, 2, to).wait_recv()
                terms.append(zrecv[2 * i - 4 : 2 * i - 2])
            zsend[2 * i : 2 * i + 2] = add16(*terms).astype(BF16)
            start(zslot, i, 2, to)

    def thin_step(start, s, to):
        i = s if to > 0 else DEEP + s
        total = sums[STEPS.index(DEEP - s if to > 0 else s + 1 - DEEP)]
        if s:
            zslot(i - 1, 1, to).wait_recv()
            total = total + zrecv[i - 1].astype(F32)
        zsend[i] = total.astype(BF16)
        start(zslot, i, 1, to)

    def x_start(start, s):
        for step in around(s):
            d, i = dkv_in(step), STEPS.index(step) * 3
            for slot, xs in ((0, 2), (2, -1)):
                j = here.at_x(xs)
                xsend[i + slot] = add16(dkv[k, d, j], dmate[d, j]).astype(BF16)
            start(xslot, i, 1)
            start(xslot, i + 2, -1)

    def x_mid(start, s):
        for step in around(s):
            d, i = here.at_z(step), STEPS.index(step) * 3
            j = here.at_x(1)
            xslot(i, 1).wait_recv()
            xsend[i + 1] = add16(dkv[k, d, j], dmate[d, j], xrecv[i]).astype(BF16)
            start(xslot, i + 1, 1)

    def x_end(s):
        for step in around(s):
            d, i = here.at_z(step), STEPS.index(step) * 3
            xslot(i + 2, -1).wait_recv()
            xslot(i + 1, 1).wait_recv()
            sums[i // 3] = add16(dkv[k, d, x], dmate[d, x], xrecv[i + 1], xrecv[i + 2])

    def grad_step(t):
        def zero(start):
            if t < DEEP:
                if t:
                    wide_step(start, t - 1, -1)
                wide_step(start, t, 1)
            elif t == DEEP:
                d = dkv_in(0)
                for i in (3, 2 * DEEP - 2):
                    for h in range(2):
                        zslot(2 * i + h, 2, 1 if i == 3 else -1).wait_recv()
                last = pl.ds(4 * (2 * DEEP - 2), 4)
                sums[0:4] = add16(dkv[k, d], dmate[d], zrecv[12:16], zrecv[last])
                xsend[0] = sums[here.at_x(2)].astype(BF16)
                start(xslot, 0, 1)
                xsend[2] = sums[here.at_x(-1)].astype(BF16)
                start(xslot, 2, -1)
            elif t == DEEP + 1:
                xslot(0, 1).wait_recv()
                xsend[1] = (sums[here.at_x(1)] + xrecv[0].astype(F32)).astype(BF16)
                start(xslot, 1, 1)
            else:
                xslot(2, -1).wait_recv()
                xslot(1, 1).wait_recv()
                tsend[...] = (sums[x] + add16(xrecv[2], xrecv[1])).astype(BF16)

        def one(start):
            if t <= DEEP:
                x_start(start, DEEP - t)
            if 1 <= t <= DEEP + 1:
                x_mid(start, DEEP + 1 - t)
            if t >= 2:
                x_end(DEEP + 2 - t)
                if t < DEEP + 2:
                    thin_step(start, t - 2, 1)
                    if t > 2:
                        thin_step(start, t - 3, -1)
                else:
                    zslot(DEEP - 1, 1, 1).wait_recv()
                    zslot(2 * DEEP - 2, 1, -1).wait_recv()
                    total = sums[0] + add16(zrecv[DEEP - 1], zrecv[2 * DEEP - 2])
                    tsend[...] = total.astype(BF16)

        by_core(zero, one)
        if t == DEEP + 2:
            go(twin)

    twin = remote(tsend, trecv, s_t.at[0], r_t.at[0], here.twin)

    def spot(which, step):
        head = here.at_y(step) // 2
        return kvg_ref.at[which, :, pl.ds(pl.multiple_of(head * HEAD, HEAD), HEAD)]

    mine = pltpu.make_async_copy(kg, spot(k, 0), s_l.at[2])

    def spread():
        twin.wait_recv()
        kg[...] = add16(tsend[...], trecv[...]).astype(BF16)
        for i, step in enumerate((2, 4, 6)):
            go(remote(kg, spot(k, 0), s_c.at[i], r_c.at[i], here.dev_y(step)))
        go(remote(kg, spot(k, 0), s_cm.at[3], r_cm.at[3], here.mate))
        mine.start()

    def spread_end():
        for i, step in enumerate((2, 4, 6)):
            remote(kg, spot(k, -step), s_c.at[i], r_c.at[i], here.dev_y(-step)).wait_recv()
            go(remote(spot(k, -step), spot(k, -step), s_cm.at[i], r_cm.at[i], here.mate))
        for i, step in enumerate((2, 4, 6)):
            there = spot(1 - k, step)
            remote(there, there, s_cm.at[i], r_cm.at[i], here.mate).wait_recv()
        remote(kg, spot(1 - k, 0), s_cm.at[3], r_cm.at[3], here.mate).wait_recv()
        mine.wait()

    ret_one, ret_finish = exchange(here, back, ret_ref, s_ret, r_ret, True)
    ret_local = pltpu.make_async_copy(back.at[e], ret_ref.at[e], s_l.at[3])

    def experts_out(s):
        blocks = [here.at_y(step) for step in around(s)]
        rows = len(blocks) * YROWS
        near = first_local(rows)

        def both(m, weight, transposed):
            parts = [
                jnp.concatenate([full[0, y, m], full[1, y, m]], axis=1) for y in blocks
            ]
            whole = jnp.concatenate(parts, axis=0)
            f = dot_t if transposed else dot
            return jnp.where(near, f(whole, weight[0]), f(whole, weight[1]))

        route_out = both(0, down_ref, False).astype(BF16)
        route_in = (both(1, gate_ref, True) + both(2, up_ref, True)).astype(BF16)
        quarters = [route_out[:, :128], route_out[:, 128:], route_in[:, :128], route_in[:, 128:]]
        out = dot(pack_table(True, rows), jnp.concatenate(quarters, axis=0)).astype(BF16)
        for b, y in enumerate(blocks):
            for i in range(NX):
                dest = source(y, i)
                r = (b * NX + i) * SLAB
                back[dest] = out[r : r + SLAB]
                offset = (dest + NE - e) % NE

                @pl.when(offset != 0)
                def _():
                    ret_one(offset).start()

                @pl.when(offset == 0)
                def _():
                    ret_local.start()

    kv_step(0)
    begin(1, 9)
    kv_step(1)
    begin(9, 17)
    kv_step(2)
    begin(17, 25)
    for c in loads:
        c.wait()
    stack()
    kv_step(3)
    begin(25, NE)
    kv_ready(0)
    forward(0)
    kv_step(4)
    kv_ready(1)
    forward(-1)
    forward(1)
    local.wait()
    finish()
    pack()
    product(0)
    kv_step(5)
    product(1)
    y_step(0, 0)
    product(2)
    y_step(0, 1)
    kv_step(6)
    y_step(0, 2)
    kv_ready(2)
    forward(-2)
    forward(2)
    for m in range(3):
        y_step(1, m)
    kv_ready(3)
    forward(-3)
    forward(3)
    for m in range(3):
        y_step(2, m)
    kv_ready(4)
    forward(4)
    normalize()
    for m in range(3):
        y_step(3, m)
    backward(4)
    grad_step(0)
    backward(-3)
    activate()
    backward(3)
    grad_step(1)
    gather_step(1)
    gather_ready(0)
    experts_out(0)
    backward(-2)
    backward(2)
    grad_step(2)
    gather_step(2)
    gather_ready(1)
    experts_out(1)
    backward(-1)
    backward(1)
    grad_step(3)
    gather_step(3)
    gather_ready(2)
    experts_out(2)
    backward(0)
    grad_step(4)
    gather_step(4)
    gather_ready(3)
    experts_out(3)
    grad_step(5)
    gather_ready(4)
    experts_out(4)
    query_grad()
    grad_step(6)
    spread()
    spread_end()
    ret_finish()
    ret_local.wait()
    for c in sends:
        c.wait_send()
    for core in range(2):

        @pl.when(k == core)
        def _(core=core):
            for make, args in core_sends[core]:
                make(*args).wait_send()


def vmem():
    return pl.BlockSpec(memory_space=pltpu.VMEM)


def dma(n):
    return pltpu.SemaphoreType.DMA((n,))


def call(kernel, outs, scratch, *args, specs=None, collective=None, name=None, flops=0):
    params = {"vmem_limit_bytes": VMEM_LIMIT}
    if collective is not None:
        params.update(collective_id=collective, has_side_effects=True)
    return pl.pallas_call(
        kernel,
        out_shape=outs,
        in_specs=specs or [vmem()] * len(args),
        out_specs=jax.tree.map(lambda o: vmem(), outs),
        scratch_shapes=scratch,
        compiler_params=pltpu.CompilerParams(**params),
        name=name,
    )(*args)


def shape(*dims, dtype=BF16):
    return jax.ShapeDtypeStruct(dims, dtype)


def body(q, key, val, do, x, g, ids, gain, gate, up, down):
    ids, gain = ids.T, gain.T
    hbm = pl.BlockSpec(memory_space=pl.ANY)
    heads = q.shape[1] // HEAD
    width = heads * TOK
    yslab, zslab, block = (YROWS, HALF), (NX, TOK, HEAD), (TOK, HEAD)

    def f32(*dims):
        return pltpu.VMEM(dims, F32)

    def b16(*dims):
        return pltpu.VMEM(dims, BF16)

    sems = [5, 4, NE, NE, 24, 24, 32, 32, 8, 8, 24, 24, 21, 21, 21, 21, 24, 24]
    sems += [8, 8, 14, 14, 24, 24, 1, 1, 3, 3, 4, 4, NE, NE]
    attn_out, dq, returned, kvg = call(
        layer_kernel,
        (shape(*q.shape), shape(*q.shape), shape(NE, SLAB, 128), shape(2, TOK, 4 * HEAD)),
        [
            b16(*q.shape), b16(*do.shape), b16(*gate.shape), b16(*up.shape), b16(*down.shape),
            b16(NE, SLAB, 128), b16(NE, SLAB, 128), b16(2, ROWS, 256),
            b16(2, NY, 3, *yslab), b16(NY, 3, *yslab), b16(21, *yslab), b16(21, *yslab),
            b16(2, NY, 3, *yslab),
            b16(2, NZ, *zslab), b16(width, HEAD), b16(width, HEAD), b16(NZ, KEYS, width),
            f32(NZ, 1, width), f32(1, width), f32(1, width), f32(HEAD, width), f32(1, width),
            f32(HEAD, width),
            b16(2, NZ, *zslab), b16(NZ, *zslab), b16(28, *block), b16(28, *block), f32(8, *block),
            b16(24, *block), b16(24, *block), b16(*block), b16(*block), b16(*block),
            b16(NE, SLAB, 128),
        ]
        + [dma(n) for n in sems],
        ids, gain, x, g, key, val, q, do, gate, up, down,
        specs=[vmem()] * 4 + [hbm] * 7, collective=0, name="layer",
    )
    moe_out, input_grad, key_grad, value_grad, attn_out, dq = call(
        combine_kernel,
        (shape(TOK, 256), shape(TOK, 256), shape(TOK, 512), shape(TOK, 512),
         shape(*q.shape), shape(*q.shape)), [],
        ids, gain, returned.reshape(NE * SLAB, 128), kvg, attn_out, dq, name="combine",
    )
    return attn_out, dq, key_grad, value_grad, moe_out, input_grad


def solution(mesh):
    rows, both = P("exp", None), P("exp", "ctx")
    return jax.shard_map(
        body,
        mesh=mesh,
        in_specs=(
            both, rows, rows, both, both, both, rows, rows,
            P("exp", "ctx", None), P("exp", "ctx", None), P("exp", None, "ctx"),
        ),
        out_specs=(both, both, rows, rows, both, both),
        check_vma=False,
    )
```

```python
import functools

import jax
import jax.numpy as jnp
from jax import lax
from jax.experimental import pallas as pl
from jax.experimental.pallas import tpu as pltpu
from jax.sharding import PartitionSpec as P

MESH = pl.DeviceIdType.MESH
F32 = jnp.float32
BF16 = jnp.bfloat16
HEAD = 128
NX, NZ, NY = 4, 8, 8
NE = NX * NZ
TOK = 128
LOCAL = 2
EXPERTS = LOCAL * NE
SLOT = 6
GROUP = LOCAL * SLOT
SLAB = 4 * GROUP
ROWS = NE * GROUP
FF = 768
HALF = FF // 2
YROWS = ROWS // NY
SCALE = HEAD ** (-0.5)
VMEM_LIMIT = 60 * 1024 * 1024


def dot(a, b):
    return jnp.dot(a, b, preferred_element_type=F32)


def dot_t(a, b):
    return lax.dot_general(a, b, (((1,), (1,)), ((), ())), preferred_element_type=F32)


def t_dot(a, b):
    return lax.dot_general(a, b, (((0,), (0,)), ((), ())), preferred_element_type=F32)


def fdiv(a, n):
    return jnp.floor((a + 0.5) * (1.0 / n))


def fiota(shape, dim):
    return lax.broadcasted_iota(jnp.int32, shape, dim).astype(F32)


def column(row):
    return jnp.broadcast_to(row, (TOK, TOK)).T


def route_tables(ids):
    lane = fiota((TOK, EXPERTS), 1)
    ids = ids.astype(F32)
    first = jnp.where(column(ids[0:1])[:, :EXPERTS] == lane, 1.0, 0.0)
    second = jnp.where(column(ids[1:2])[:, :EXPERTS] == lane, 1.0, 0.0)
    row = lax.broadcasted_iota(jnp.int32, (TOK, TOK), 0)
    col = lax.broadcasted_iota(jnp.int32, (TOK, TOK), 1)
    before = jnp.where(col < row, 1.0, 0.0).astype(BF16)
    place = dot(before, (first + second).astype(BF16)) + 1.0
    return (first * place).astype(BF16), (second * place).astype(BF16)


def slab_index(p):
    dest = fdiv(p, SLAB)
    inner = p - dest * SLAB
    quarter = fdiv(inner, GROUP)
    inner = inner - quarter * GROUP
    local = fdiv(inner, SLOT)
    slot = inner - local * SLOT
    return dest * LOCAL + local, quarter, slot


def prepare(ids_ref, gain_ref, x_ref, g_ref, out_ref):
    v0, v1 = route_tables(ids_ref[...])
    total = NE * SLAB
    expert, quarter, slot = slab_index(fiota((total, 1), 0))
    pick = jnp.where(expert == fiota((total, EXPERTS), 1), 1.0, 0.0).astype(BF16)
    y0 = dot_t(pick, v0)
    y1 = dot_t(pick, v1)
    want = slot + 1.0
    hit0 = jnp.where(y0 == want, 1.0, 0.0)
    hit1 = jnp.where(y1 == want, 1.0, 0.0)
    both = hit0 + hit1
    q = [jnp.where(quarter == float(i), 1.0, 0.0) for i in range(4)]
    table = jnp.concatenate(
        [both * q[0], both * q[1], hit0 * q[2], hit0 * q[3], hit1 * q[2], hit1 * q[3]], axis=1
    ).astype(BF16)
    x = x_ref[...]
    g = g_ref[...].astype(F32)
    gain = gain_ref[...]
    w0, w1 = column(gain[0:1]), column(gain[1:2])
    lo, hi = g[:, :128], g[:, 128:]
    scaled = [(a * w).astype(BF16) for w in (w0, w1) for a in (lo, hi)]
    rows = jnp.concatenate([x[:, :128], x[:, 128:]] + scaled, axis=0)
    out_ref[...] = dot(table, rows).astype(BF16).reshape(NE, SLAB, 128)


def combine_kernel(
    ids_ref, gain_ref, back_ref, kvg_ref, ao_ref, dq_ref,
    out_ref, in_ref, kg_ref, vg_ref, ao_out, dq_out,
):
    v0, v1 = route_tables(ids_ref[...])
    total = NE * SLAB
    expert, quarter, slot = slab_index(fiota((1, total), 1))
    pick = jnp.where(expert == fiota((EXPERTS, total), 0), 1.0, 0.0).astype(BF16)
    y0 = dot(v0, pick)
    y1 = dot(v1, pick)
    want = slot + 1.0
    hit0 = jnp.where(y0 == want, 1.0, 0.0)
    hit1 = jnp.where(y1 == want, 1.0, 0.0)
    both = hit0 + hit1
    q = [jnp.where(quarter == float(i), 1.0, 0.0) for i in range(4)]
    back = back_ref[...]
    gain = gain_ref[...]
    w0, w1 = column(gain[0:1]), column(gain[1:2])
    for i in range(2):
        part0 = dot((hit0 * q[i]).astype(BF16), back)
        part1 = dot((hit1 * q[i]).astype(BF16), back)
        out_ref[:, i * 128 : (i + 1) * 128] = (part0 * w0 + part1 * w1).astype(BF16)
        in_ref[:, i * 128 : (i + 1) * 128] = dot((both * q[2 + i]).astype(BF16), back).astype(BF16)
    kg_ref[...] = kvg_ref[0]
    vg_ref[...] = kvg_ref[1]
    ao_out[...] = ao_ref[...]
    dq_out[...] = dq_ref[...]


PACK = 8 * GROUP


def pack_table(transposed, rows):
    n = 4 * rows
    r = fiota((1, n) if transposed else (n, 1), 1 if transposed else 0)
    quarter = fdiv(r, rows)
    inner = r - quarter * rows
    source = fdiv(inner, GROUP)
    p = source * SLAB + quarter * GROUP + (inner - source * GROUP)
    return jnp.where(p == fiota((n, n), 0 if transposed else 1), 1.0, 0.0).astype(BF16)


def first_local(rows):
    r = fiota((rows, 1), 0)
    inner = r - fdiv(r, GROUP) * GROUP
    return inner < float(SLOT)


def source(y, i):
    return ((y - 2 * i + 2 * NZ) % NZ) * NX + i


class Place:
    def __init__(self):
        self.e = lax.axis_index("exp")
        self.c = lax.axis_index("ctx")
        self.z, self.x = self.e // NX, self.e % NX
        self.y, self.k = self.c // 2, self.c % 2
        self.sgn = 1 - 2 * self.k
        self.mate = {"exp": self.e, "ctx": self.y * 2 + 1 - self.k}
        self.twin = {"exp": self.e, "ctx": (self.y + 1 - 2 * (self.y % 2)) * 2 + self.k}

    def at_z(self, step):
        return (self.z + self.sgn * step + 2 * NZ) % NZ

    def at_x(self, step):
        return (self.x + self.sgn * step + 2 * NX) % NX

    def at_y(self, step):
        return (self.y + self.sgn * step + 2 * NY) % NY

    def dev_z(self, step):
        return {"exp": self.at_z(step) * NX + self.x, "ctx": self.c}

    def dev_x(self, step):
        return {"exp": self.z * NX + self.at_x(step), "ctx": self.c}

    def dev_y(self, step):
        return {"exp": self.e, "ctx": self.at_y(step) * 2 + self.k}


def remote(src, dst, send, recv, device):
    return pltpu.make_async_remote_copy(
        src_ref=src, dst_ref=dst, send_sem=send, recv_sem=recv, device_id=device,
        device_id_type=MESH,
    )


def remote(src, dst, send, recv, device):
    return pltpu.make_async_remote_copy(
        src_ref=src, dst_ref=dst, send_sem=send, recv_sem=recv, device_id=device,
        device_id_type=MESH,
    )


def exchange(here, send_ref, recv_ref, send_sem, recv_sem, single=False):
    def one(o):
        dest = (here.e + o) % NE
        return remote(
            send_ref.at[dest], recv_ref.at[here.e], send_sem.at[0], recv_sem.at[0],
            {"exp": dest, "ctx": here.c},
        )

    def begin(first, last):
        def go(o, carry):
            one(o).start()
            return carry

        lax.fori_loop(first, last, go, 0)

    def finish():
        rest = pl.ds(0, NE - 1)
        every = remote(send_ref.at[rest], recv_ref.at[rest], send_sem.at[0], recv_sem.at[0], here.mate)
        every.wait_send()
        every.wait_recv()

    return one, begin, finish


def add16(*refs):
    total = refs[0].astype(F32)
    for r in refs[1:]:
        total = total + r.astype(F32)
    return total


ORDER = [4, -3, 3, -2, 2, -1, 1, 0]
STEPS = [0, -1, 1, -2, 2, -3, 3, 4]
LANES = [0, -1, 1, -2]
DEEP = NZ // 2
KEYS = NX * TOK


def around(s):
    return [s] if s in (0, DEEP) else [-s, s]


def opposite(step):
    return step if step == DEEP else -step


def layer_kernel(
    ids_ref, gain_ref, x_ref, g_ref, key_ref, val_ref, q_hbm, do_hbm, gate_hbm, up_hbm, down_hbm,
    ao_ref, dq_ref, ret_ref, kvg_ref,
    q_ref, do_ref, gate_ref, up_ref, down_ref,
    send, recv, rows_ref, part, pmate, ysend, yrecv, full,
    kv, qs, dos, e_ref, mj, m_ref, l_ref, o_ref, d_ref, dq_acc,
    dkv, dmate, zsend, zrecv, sums, xsend, xrecv, tsend, trecv, kg, back,
    s_in, s_l, s_far, r_far, s_kx, r_kx, s_kz, r_kz, s_km, r_km,
    s_pm, r_pm, s_y, r_y, s_g, r_g, s_gm, r_gm,
    s_dm, r_dm, s_z, r_z, s_x, r_x, s_t, r_t, s_c, r_c, s_cm, r_cm, s_ret, r_ret,
):
    here = Place()
    k, z, x, e = here.k, here.z, here.x, here.e
    barrier = pltpu.get_barrier_semaphore()

    def greet(device):
        pl.semaphore_signal(barrier, inc=1, device_id=device, device_id_type=MESH)

    near = [here.mate] + [here.dev_y(s) for s in (1, -1, 2, -2, 4)]
    for device in near:
        greet(device)

    def greet_far(o, carry):
        greet({"exp": (e + o) % NE, "ctx": here.c})
        return carry

    lax.fori_loop(1, NE, greet_far, 0)

    loads = [
        pltpu.make_async_copy(a, b, s_in.at[i])
        for i, (a, b) in enumerate(
            [(gate_hbm, gate_ref), (up_hbm, up_ref), (down_hbm, down_ref), (q_hbm, q_ref), (do_hbm, do_ref)]
        )
    ]
    for c in loads:
        c.start()
    cols = pl.ds(pl.multiple_of((here.y // 2) * HEAD, HEAD), HEAD)
    own = kv.at[k, z, x]

    @pl.when(k == 0)
    def _():
        pltpu.make_async_copy(key_ref.at[:, cols], own, s_l.at[0]).start()

    @pl.when(k == 1)
    def _():
        pltpu.make_async_copy(val_ref.at[:, cols], own, s_l.at[0]).start()

    prepare(ids_ref, gain_ref, x_ref, g_ref, send)
    pltpu.make_async_copy(key_ref.at[:, cols], own, s_l.at[0]).wait()
    pl.semaphore_wait(barrier, len(near) + NE - 1)

    sends = []

    def go(c):
        c.start()
        sends.append(c)

    def by_core(zero, one):
        for core, f in enumerate((zero, one)):

            def start(make, *args):
                make(*args).start()

            @pl.when(k == core)
            def _(f=f, start=start):
                f(start)

    far_one, begin, finish = exchange(here, send, recv, s_far, r_far)
    local = pltpu.make_async_copy(send.at[e], recv.at[e], s_l.at[1])
    local.start()

    def kz(j, zs, xs, to):
        spot = kv.at[k, here.at_z(zs), here.at_x(xs)]
        return remote(spot, spot, s_kz.at[0], r_kz.at[j], here.dev_z(to))

    def kx(j, zs, xs, to):
        spot = kv.at[k, here.at_z(zs), here.at_x(xs)]
        return remote(spot, spot, s_kx.at[0], r_kx.at[j], here.dev_x(to))

    def kv_mate(step):
        i, spot = STEPS.index(step), kv.at[k, here.at_z(step)]
        return remote(spot, spot, s_km.at[0], r_km.at[i], here.mate)

    def lane_start(start, xs):
        i = LANES.index(xs) * 8
        start(kz, i, 0, xs, 1)
        start(kz, i + DEEP, 0, xs, -1)

    def lane_step(start, s):
        for i, xs in enumerate(LANES):
            kz(i * 8 + s - 1, -s, xs, 1).wait_recv()
            if s < DEEP:
                start(kz, i * 8 + s, -s, xs, 1)
                kz(i * 8 + DEEP + s - 1, s, xs, -1).wait_recv()
                if s < DEEP - 1:
                    start(kz, i * 8 + DEEP + s, s, xs, -1)
        for step in around(s):
            start(kv_mate, step)

    def cross_start(start, s):
        for step in around(s):
            i = STEPS.index(step) * 3
            start(kx, i, step, 0, 1)
            start(kx, i + 2, step, 0, -1)

    def cross_mid(start, s):
        for step in around(s):
            i = STEPS.index(step) * 3
            kx(i, step, -1, 1).wait_recv()
            start(kx, i + 1, step, -1, 1)
            kx(i + 2, step, 1, -1).wait_recv()

    def cross_end(start, s):
        for step in around(s):
            kx(STEPS.index(step) * 3 + 1, step, -2, 1).wait_recv()
            start(kv_mate, step)

    def kv_step(t):
        def zero(start):
            if t == 0:
                start(kx, 0, 0, 0, 1)
                start(kx, 2, 0, 0, -1)
                lane_start(start, 0)
            elif t == 1:
                kx(0, 0, -1, 1).wait_recv()
                start(kx, 1, 0, -1, 1)
                lane_start(start, -1)
                kx(2, 0, 1, -1).wait_recv()
                lane_start(start, 1)
            elif t == 2:
                kx(1, 0, -2, 1).wait_recv()
                lane_start(start, -2)
                start(kv_mate, 0)
            else:
                lane_step(start, t - 2)

        def one(start):
            if t == 0:
                start(kz, 0, 0, 0, 1)
                start(kz, DEEP, 0, 0, -1)
                cross_start(start, 0)
                return
            if t <= DEEP:
                kz(t - 1, -t, 0, 1).wait_recv()
                if t < DEEP:
                    start(kz, t, -t, 0, 1)
                    kz(DEEP + t - 1, t, 0, -1).wait_recv()
                    if t < DEEP - 1:
                        start(kz, DEEP + t, t, 0, -1)
                cross_start(start, t)
            if t <= DEEP + 1:
                cross_mid(start, t - 1)
            if t >= 2:
                cross_end(start, t - 2)

        by_core(zero, one)

    def kv_ready(s):
        for step in around(s):
            i, spot = STEPS.index(opposite(step)), kv.at[1 - k, here.at_z(step)]
            remote(spot, spot, s_km.at[0], r_km.at[i], here.mate).wait_recv()

    def pack():
        table = pack_table(False, PACK)
        for g in range(NE // 8):
            slabs = [recv[source(y, i)] for y in (2 * g, 2 * g + 1) for i in range(NX)]
            packed = dot(table, jnp.concatenate(slabs, axis=0)).astype(BF16)
            for i in range(4):
                lanes = slice((i % 2) * 128, (i % 2 + 1) * 128)
                rows_ref[i // 2, g * PACK : (g + 1) * PACK, lanes] = packed[
                    i * PACK : (i + 1) * PACK, :
                ]

    first = first_local(ROWS)

    def product(m):
        if m < 2:
            w_ref = (gate_ref, up_ref)[m]
            rows = rows_ref[0]
            whole = jnp.where(first, dot(rows, w_ref[0]), dot(rows, w_ref[1]))
        else:
            rows = rows_ref[1]
            whole = jnp.where(first, dot_t(rows, down_ref[0]), dot_t(rows, down_ref[1]))
        whole = whole.astype(BF16)
        for c in range(2):
            for y in range(NY):
                part[c, y, m] = whole[y * YROWS : (y + 1) * YROWS, c * HALF : (c + 1) * HALF]
        go(part_mate(m))

    def part_mate(m):
        return remote(part.at[1 - k, :, m], pmate.at[:, m], s_pm.at[m], r_pm.at[m], here.mate)

    def yslot(i, m, to):
        j = m * 7 + i
        return remote(ysend.at[j], yrecv.at[j], s_y.at[0], r_y.at[j], here.dev_y(to))

    def y_step(s, m):
        d = here.at_y(DEEP - s)
        if s == 0:
            part_mate(m).wait_recv()
        j = m * 7 + s
        if s == 0:
            ysend[j] = add16(part[k, d, m], pmate[d, m]).astype(BF16)
        else:
            yslot(s - 1, m, 1).wait_recv()
            ysend[j] = add16(part[k, d, m], pmate[d, m], yrecv[j - 1]).astype(BF16)
        yslot(s, m, 1).start()
        if s < DEEP - 1:
            d = here.at_y(s + 1 - DEEP)
            j = m * 7 + DEEP + s
            if s == 0:
                ysend[j] = add16(part[k, d, m], pmate[d, m]).astype(BF16)
            else:
                yslot(DEEP + s - 1, m, -1).wait_recv()
                ysend[j] = add16(part[k, d, m], pmate[d, m], yrecv[j - 1]).astype(BF16)
            yslot(DEEP + s, m, -1).start()

    def gcopy(i, m, origin, to):
        spot = full.at[k, here.at_y(origin), m]
        j = m * 7 + i
        return remote(spot, spot, s_g.at[0], r_g.at[j], here.dev_y(to))

    def g_mate(i, origin):
        spot = full.at[k, here.at_y(origin)]
        return remote(spot, spot, s_gm.at[0], r_gm.at[i], here.mate)

    def activate():
        total = []
        for m in range(3):
            d = here.y
            yslot(2 * DEEP - 2, m, -1).wait_recv()
            yslot(DEEP - 1, m, 1).wait_recv()
            total.append(
                add16(part[k, d, m], pmate[d, m], yrecv[m * 7 + 2 * DEEP - 2], yrecv[m * 7 + DEEP - 1])
            )
        gate, up, hidden_grad = total
        sig = 1.0 / (1.0 + jnp.exp(-gate))
        act = gate * sig
        full[k, here.y, 0] = (act * up).astype(BF16)
        full[k, here.y, 1] = (hidden_grad * up * sig * (1.0 + gate * (1.0 - sig))).astype(BF16)
        full[k, here.y, 2] = (hidden_grad * act).astype(BF16)
        for m in range(3):
            gcopy(0, m, 0, 1).start()
            gcopy(DEEP, m, 0, -1).start()
        g_mate(0, 0).start()

    def gather_step(s):
        for m in range(3):
            gcopy(s - 1, m, -s, 1).wait_recv()
            if s < DEEP:
                gcopy(s, m, -s, 1).start()
                gcopy(DEEP + s - 1, m, s, -1).wait_recv()
                if s < DEEP - 1:
                    gcopy(DEEP + s, m, s, -1).start()
        g_mate(s, -s).start()
        if s < DEEP:
            g_mate(DEEP + s, s).start()

    def gather_ready(s):
        for step in around(s):
            i = s if step != -s or s == 0 else DEEP + s
            spot = full.at[1 - k, here.at_y(step)]
            remote(spot, spot, s_gm.at[0], r_gm.at[i], here.mate).wait_recv()

    heads = q_ref.shape[1] // HEAD
    width = heads * TOK

    def stack():
        for h in range(heads):
            qs[h * TOK : (h + 1) * TOK, :] = q_ref[:, h * HEAD : (h + 1) * HEAD]
            dos[h * TOK : (h + 1) * TOK, :] = do_ref[:, h * HEAD : (h + 1) * HEAD]
        m_ref[...] = jnp.full((1, width), -jnp.inf, F32)
        l_ref[...] = jnp.zeros((1, width), F32)
        o_ref[...] = jnp.zeros((HEAD, width), F32)
        dq_acc[...] = jnp.zeros((HEAD, width), F32)

    def forward(step):
        j = here.at_z(step)
        lane = lax.broadcasted_iota(jnp.int32, (1, width), 1)
        q_pos = e * TOK + jnp.bitwise_and(lane, TOK - 1)
        row = lax.broadcasted_iota(jnp.int32, (KEYS, 1), 0) + j * KEYS
        s = dot_t(kv[0, j].reshape(KEYS, HEAD), qs[...]) * SCALE
        s = jnp.where(row <= q_pos, s, -jnp.inf)
        old = m_ref[...]
        m = jnp.maximum(old, jnp.max(s, axis=0, keepdims=True))
        p = jnp.exp(s - m)
        p16 = p.astype(BF16)
        e_ref[j] = p16
        mj[j] = m
        m_ref[...] = m
        fade = jnp.exp(old - m)
        l_ref[...] = l_ref[...] * fade + jnp.sum(p, axis=0, keepdims=True)
        o_ref[...] = o_ref[...] * fade + t_dot(kv[1, j].reshape(KEYS, HEAD), p16)

    def normalize():
        inv = 1.0 / l_ref[...]
        l_ref[...] = inv
        o16 = (o_ref[...] * inv).astype(BF16)
        turned = o16.astype(F32).T
        for h in range(heads):
            ao_ref[:, h * HEAD : (h + 1) * HEAD] = turned[h * TOK : (h + 1) * TOK, :].astype(BF16)
        do_t = dos[...].astype(F32).T
        d_ref[...] = jnp.sum(do_t * o16.astype(F32), axis=0, keepdims=True)

    def backward(step):
        j = here.at_z(step)
        keys = kv[0, j].reshape(KEYS, HEAD)
        dp = dot_t(kv[1, j].reshape(KEYS, HEAD), dos[...])
        p = e_ref[j].astype(F32) * (jnp.exp(mj[j] - m_ref[...]) * l_ref[...])
        ds = (p * (dp - d_ref[...])).astype(BF16)
        dkv[0, j] = (dot(ds, qs[...]) * SCALE).astype(BF16).reshape(NX, TOK, HEAD)
        dkv[1, j] = dot(p.astype(BF16), dos[...]).astype(BF16).reshape(NX, TOK, HEAD)
        dq_acc[...] += t_dot(keys, ds)
        i = ORDER.index(opposite(step))
        remote(dkv.at[1 - k, j], dmate.at[j], s_dm.at[0], r_dm.at[i], here.mate).start()

    def query_grad():
        turned = (dq_acc[...] * SCALE).T
        for h in range(heads):
            dq_ref[:, h * HEAD : (h + 1) * HEAD] = turned[h * TOK : (h + 1) * TOK, :].astype(BF16)

    def dkv_in(step):
        i, d = ORDER.index(step), here.at_z(step)
        remote(dkv.at[k, d], dmate.at[d], s_dm.at[0], r_dm.at[i], here.mate).wait_recv()
        return d

    def zslot(i, n, to):
        spot = pl.ds(i * n, n)
        return remote(zsend.at[spot], zrecv.at[spot], s_z.at[0], r_z.at[i], here.dev_z(to))

    def xslot(i, to):
        return remote(xsend.at[i], xrecv.at[i], s_x.at[0], r_x.at[i], here.dev_x(to))

    def wide_step(start, s, to):
        d = dkv_in(DEEP - s if to > 0 else s + 1 - DEEP)
        for h in range(2):
            i = (s if to > 0 else DEEP + s) * 2 + h
            blocks = pl.ds(2 * h, 2)
            terms = [dkv[k, d, blocks], dmate[d, blocks]]
            if s:
                zslot(i - 2, 2, to).wait_recv()
                terms.append(zrecv[2 * i - 4 : 2 * i - 2])
            zsend[2 * i : 2 * i + 2] = add16(*terms).astype(BF16)
            start(zslot, i, 2, to)

    def thin_step(start, s, to):
        i = s if to > 0 else DEEP + s
        total = sums[STEPS.index(DEEP - s if to > 0 else s + 1 - DEEP)]
        if s:
            zslot(i - 1, 1, to).wait_recv()
            total = total + zrecv[i - 1].astype(F32)
        zsend[i] = total.astype(BF16)
        start(zslot, i, 1, to)

    def x_start(start, s):
        for step in around(s):
            d, i = dkv_in(step), STEPS.index(step) * 3
            for slot, xs in ((0, 2), (2, -1)):
                j = here.at_x(xs)
                xsend[i + slot] = add16(dkv[k, d, j], dmate[d, j]).astype(BF16)
            start(xslot, i, 1)
            start(xslot, i + 2, -1)

    def x_mid(start, s):
        for step in around(s):
            d, i = here.at_z(step), STEPS.index(step) * 3
            j = here.at_x(1)
            xslot(i, 1).wait_recv()
            xsend[i + 1] = add16(dkv[k, d, j], dmate[d, j], xrecv[i]).astype(BF16)
            start(xslot, i + 1, 1)

    def x_end(s):
        for step in around(s):
            d, i = here.at_z(step), STEPS.index(step) * 3
            xslot(i + 2, -1).wait_recv()
            xslot(i + 1, 1).wait_recv()
            sums[i // 3] = add16(dkv[k, d, x], dmate[d, x], xrecv[i + 1], xrecv[i + 2])

    def grad_step(t):
        def zero(start):
            if t < DEEP:
                if t:
                    wide_step(start, t - 1, -1)
                wide_step(start, t, 1)
            elif t == DEEP:
                d = dkv_in(0)
                for i in (3, 2 * DEEP - 2):
                    for h in range(2):
                        zslot(2 * i + h, 2, 1 if i == 3 else -1).wait_recv()
                last = pl.ds(4 * (2 * DEEP - 2), 4)
                sums[0:4] = add16(dkv[k, d], dmate[d], zrecv[12:16], zrecv[last])
                xsend[0] = sums[here.at_x(2)].astype(BF16)
                start(xslot, 0, 1)
                xsend[2] = sums[here.at_x(-1)].astype(BF16)
                start(xslot, 2, -1)
            elif t == DEEP + 1:
                xslot(0, 1).wait_recv()
                xsend[1] = (sums[here.at_x(1)] + xrecv[0].astype(F32)).astype(BF16)
                start(xslot, 1, 1)
            else:
                xslot(2, -1).wait_recv()
                xslot(1, 1).wait_recv()
                tsend[...] = (sums[x] + add16(xrecv[2], xrecv[1])).astype(BF16)

        def one(start):
            if t <= DEEP:
                x_start(start, DEEP - t)
            if 1 <= t <= DEEP + 1:
                x_mid(start, DEEP + 1 - t)
            if t >= 2:
                x_end(DEEP + 2 - t)
                if t < DEEP + 2:
                    thin_step(start, t - 2, 1)
                    if t > 2:
                        thin_step(start, t - 3, -1)
                else:
                    zslot(DEEP - 1, 1, 1).wait_recv()
                    zslot(2 * DEEP - 2, 1, -1).wait_recv()
                    total = sums[0] + add16(zrecv[DEEP - 1], zrecv[2 * DEEP - 2])
                    tsend[...] = total.astype(BF16)

        by_core(zero, one)
        if t == DEEP + 2:
            go(twin)

    twin = remote(tsend, trecv, s_t.at[0], r_t.at[0], here.twin)

    def spot(which, step):
        head = here.at_y(step) // 2
        return kvg_ref.at[which, :, pl.ds(pl.multiple_of(head * HEAD, HEAD), HEAD)]

    mine = pltpu.make_async_copy(kg, spot(k, 0), s_l.at[2])

    def spread():
        twin.wait_recv()
        kg[...] = add16(tsend[...], trecv[...]).astype(BF16)
        for i, step in enumerate((4, 2, 6)):
            go(remote(kg, spot(k, 0), s_c.at[i], r_c.at[i], here.dev_y(step)))
        go(remote(kg, spot(k, 0), s_cm.at[3], r_cm.at[3], here.mate))
        mine.start()

    def spread_end():
        order = (4, 2, 6)
        for i in (1, 2, 0):
            there = spot(k, -order[i])
            remote(kg, there, s_c.at[i], r_c.at[i], here.dev_y(-order[i])).wait_recv()
            go(remote(there, there, s_cm.at[i], r_cm.at[i], here.mate))
        remote(kg, spot(1 - k, 0), s_cm.at[3], r_cm.at[3], here.mate).wait_recv()
        for i in (1, 2, 0):
            there = spot(1 - k, order[i])
            remote(there, there, s_cm.at[i], r_cm.at[i], here.mate).wait_recv()
        mine.wait()

    ret_one, ret_begin, ret_finish = exchange(here, back, ret_ref, s_ret, r_ret)
    ret_local = pltpu.make_async_copy(back.at[e], ret_ref.at[e], s_l.at[3])

    def experts_out(s):
        blocks = [here.at_y(step) for step in around(s)]
        rows = len(blocks) * YROWS
        near = first_local(rows)

        def both(m, weight, transposed):
            parts = [
                jnp.concatenate([full[0, y, m], full[1, y, m]], axis=1) for y in blocks
            ]
            whole = jnp.concatenate(parts, axis=0)
            f = dot_t if transposed else dot
            return jnp.where(near, f(whole, weight[0]), f(whole, weight[1]))

        route_out = both(0, down_ref, False).astype(BF16)
        route_in = (both(1, gate_ref, True) + both(2, up_ref, True)).astype(BF16)
        quarters = [route_out[:, :128], route_out[:, 128:], route_in[:, :128], route_in[:, 128:]]
        out = dot(pack_table(True, rows), jnp.concatenate(quarters, axis=0)).astype(BF16)
        for b, y in enumerate(blocks):
            for i in range(NX):
                dest = source(y, i)
                r = (b * NX + i) * SLAB
                back[dest] = out[r : r + SLAB]
                offset = (dest + NE - e) % NE

                @pl.when(offset != 0)
                def _():
                    ret_one(offset).start()

                @pl.when(offset == 0)
                def _():
                    ret_local.start()

    def each_y(s):
        for m in range(3):
            y_step(s, m)

    def drain(sem, ref):
        remote(ref, ref, sem.at[0], sem.at[0], here.mate).wait_send()

    kv_step(0)
    begin(1, 17)
    kv_step(1)
    begin(17, NE)
    for c in loads:
        c.wait()
    stack()
    kv_step(2)
    kv_step(3)
    local.wait()
    finish()
    pack()
    product(0)
    kv_step(4)
    product(1)
    y_step(0, 0)
    product(2)
    y_step(0, 1)
    kv_step(5)
    y_step(0, 2)
    kv_ready(0)
    forward(0)
    kv_ready(1)
    forward(-1)
    forward(1)
    kv_step(6)
    each_y(1)
    kv_ready(2)
    forward(-2)
    forward(2)
    each_y(2)
    kv_ready(3)
    forward(-3)
    forward(3)
    kv_ready(4)
    forward(4)
    normalize()
    each_y(3)
    backward(4)
    backward(-3)
    grad_step(0)
    activate()
    backward(3)
    grad_step(1)
    backward(-2)
    gather_step(1)
    backward(2)
    grad_step(2)
    backward(-1)
    gather_step(2)
    backward(1)
    grad_step(3)
    gather_ready(0)
    experts_out(0)
    gather_step(3)
    backward(0)
    grad_step(4)
    gather_ready(1)
    experts_out(1)
    gather_step(4)
    grad_step(5)
    gather_ready(2)
    experts_out(2)
    gather_ready(3)
    experts_out(3)
    gather_ready(4)
    experts_out(4)
    grad_step(6)
    query_grad()
    spread()
    spread_end()
    ret_finish()
    ret_local.wait()
    for c in sends:
        c.wait_send()
    drain(s_km, kv.at[k])
    drain(s_y, ysend)
    drain(s_g, full.at[k, pl.ds(0, 7)])
    drain(s_gm, full.at[k])
    drain(s_dm, dkv.at[1 - k])

    def drain_zero(start):
        drain(s_kx, kv.at[k, 0, pl.ds(0, 3)])
        drain(s_kz, kv.at[k, pl.ds(0, 7)])
        drain(s_z, zsend)
        drain(s_x, xsend.at[pl.ds(0, 3)])

    def drain_one(start):
        drain(s_kx, kv.at[k, :, pl.ds(0, 3)])
        drain(s_kz, kv.at[k, pl.ds(0, 7), 0])
        drain(s_z, zsend.at[pl.ds(0, 7)])
        drain(s_x, xsend)

    by_core(drain_zero, drain_one)


def vmem():
    return pl.BlockSpec(memory_space=pltpu.VMEM)


def dma(n):
    return pltpu.SemaphoreType.DMA((n,))


def call(kernel, outs, scratch, *args, specs=None, collective=None, name=None, flops=0):
    params = {"vmem_limit_bytes": VMEM_LIMIT}
    if collective is not None:
        params.update(collective_id=collective, has_side_effects=True)
    return pl.pallas_call(
        kernel,
        out_shape=outs,
        in_specs=specs or [vmem()] * len(args),
        out_specs=jax.tree.map(lambda o: vmem(), outs),
        scratch_shapes=scratch,
        compiler_params=pltpu.CompilerParams(**params),
        name=name,
    )(*args)


def shape(*dims, dtype=BF16):
    return jax.ShapeDtypeStruct(dims, dtype)


def body(q, key, val, do, x, g, ids, gain, gate, up, down):
    ids, gain = ids.T, gain.T
    hbm = pl.BlockSpec(memory_space=pl.ANY)
    heads = q.shape[1] // HEAD
    width = heads * TOK
    yslab, zslab, block = (YROWS, HALF), (NX, TOK, HEAD), (TOK, HEAD)

    def f32(*dims):
        return pltpu.VMEM(dims, F32)

    def b16(*dims):
        return pltpu.VMEM(dims, BF16)

    sems = [5, 4, 1, 1, 1, 24, 1, 32, 1, 8, 3, 3, 1, 21, 1, 21, 1, 8]
    sems += [1, 8, 1, 14, 1, 24, 1, 1, 3, 3, 4, 4, 1, 1]
    attn_out, dq, returned, kvg = call(
        layer_kernel,
        (shape(*q.shape), shape(*q.shape), shape(NE, SLAB, 128), shape(2, TOK, 4 * HEAD)),
        [
            b16(*q.shape), b16(*do.shape), b16(*gate.shape), b16(*up.shape), b16(*down.shape),
            b16(NE, SLAB, 128), b16(NE, SLAB, 128), b16(2, ROWS, 256),
            b16(2, NY, 3, *yslab), b16(NY, 3, *yslab), b16(21, *yslab), b16(21, *yslab),
            b16(2, NY, 3, *yslab),
            b16(2, NZ, *zslab), b16(width, HEAD), b16(width, HEAD), b16(NZ, KEYS, width),
            f32(NZ, 1, width), f32(1, width), f32(1, width), f32(HEAD, width), f32(1, width),
            f32(HEAD, width),
            b16(2, NZ, *zslab), b16(NZ, *zslab), b16(28, *block), b16(28, *block), f32(8, *block),
            b16(24, *block), b16(24, *block), b16(*block), b16(*block), b16(*block),
            b16(NE, SLAB, 128),
        ]
        + [dma(n) for n in sems],
        ids, gain, x, g, key, val, q, do, gate, up, down,
        specs=[vmem()] * 4 + [hbm] * 7, collective=0, name="layer",
    )
    moe_out, input_grad, key_grad, value_grad, attn_out, dq = call(
        combine_kernel,
        (shape(TOK, 256), shape(TOK, 256), shape(TOK, 512), shape(TOK, 512),
         shape(*q.shape), shape(*q.shape)), [],
        ids, gain, returned.reshape(NE * SLAB, 128), kvg, attn_out, dq, name="combine",
    )
    return attn_out, dq, key_grad, value_grad, moe_out, input_grad


def solution(mesh):
    rows, both = P("exp", None), P("exp", "ctx")
    return jax.shard_map(
        body,
        mesh=mesh,
        in_specs=(
            both, rows, rows, both, both, both, rows, rows,
            P("exp", "ctx", None), P("exp", "ctx", None), P("exp", None, "ctx"),
        ),
        out_specs=(both, both, rows, rows, both, both),
        check_vma=False,
    )
```

```python
import functools

import jax
import jax.numpy as jnp
from jax import lax
from jax.experimental import pallas as pl
from jax.experimental.pallas import tpu as pltpu
from jax.sharding import PartitionSpec as P

MESH = pl.DeviceIdType.MESH
F32 = jnp.float32
BF16 = jnp.bfloat16
HEAD = 128
NX, NZ, NY = 4, 8, 8
NE = NX * NZ
TOK = 128
LOCAL = 2
EXPERTS = LOCAL * NE
SLOT = 6
GROUP = LOCAL * SLOT
SLAB = 4 * GROUP
ROWS = NE * GROUP
FF = 768
HALF = FF // 2
YROWS = ROWS // NY
SCALE = HEAD ** (-0.5)
VMEM_LIMIT = 60 * 1024 * 1024


def dot(a, b):
    return jnp.dot(a, b, preferred_element_type=F32)


def dot_t(a, b):
    return lax.dot_general(a, b, (((1,), (1,)), ((), ())), preferred_element_type=F32)


def t_dot(a, b):
    return lax.dot_general(a, b, (((0,), (0,)), ((), ())), preferred_element_type=F32)


def fdiv(a, n):
    return jnp.floor((a + 0.5) * (1.0 / n))


def fiota(shape, dim):
    return lax.broadcasted_iota(jnp.int32, shape, dim).astype(F32)


def column(row):
    return jnp.broadcast_to(row, (TOK, TOK)).T


def route_tables(ids):
    lane = fiota((TOK, EXPERTS), 1)
    ids = ids.astype(F32)
    first = jnp.where(column(ids[0:1])[:, :EXPERTS] == lane, 1.0, 0.0)
    second = jnp.where(column(ids[1:2])[:, :EXPERTS] == lane, 1.0, 0.0)
    row = lax.broadcasted_iota(jnp.int32, (TOK, TOK), 0)
    col = lax.broadcasted_iota(jnp.int32, (TOK, TOK), 1)
    before = jnp.where(col < row, 1.0, 0.0).astype(BF16)
    place = dot(before, (first + second).astype(BF16)) + 1.0
    return (first * place).astype(BF16), (second * place).astype(BF16)


def slab_index(p):
    dest = fdiv(p, SLAB)
    inner = p - dest * SLAB
    quarter = fdiv(inner, GROUP)
    inner = inner - quarter * GROUP
    local = fdiv(inner, SLOT)
    slot = inner - local * SLOT
    return dest * LOCAL + local, quarter, slot


def prepare(ids_ref, gain_ref, x_ref, g_ref, out_ref):
    v0, v1 = route_tables(ids_ref[...])
    total = NE * SLAB
    expert, quarter, slot = slab_index(fiota((total, 1), 0))
    pick = jnp.where(expert == fiota((total, EXPERTS), 1), 1.0, 0.0).astype(BF16)
    y0 = dot_t(pick, v0)
    y1 = dot_t(pick, v1)
    want = slot + 1.0
    hit0 = jnp.where(y0 == want, 1.0, 0.0)
    hit1 = jnp.where(y1 == want, 1.0, 0.0)
    both = hit0 + hit1
    q = [jnp.where(quarter == float(i), 1.0, 0.0) for i in range(4)]
    table = jnp.concatenate(
        [both * q[0], both * q[1], hit0 * q[2], hit0 * q[3], hit1 * q[2], hit1 * q[3]], axis=1
    ).astype(BF16)
    x = x_ref[...]
    g = g_ref[...].astype(F32)
    gain = gain_ref[...]
    w0, w1 = column(gain[0:1]), column(gain[1:2])
    lo, hi = g[:, :128], g[:, 128:]
    scaled = [(a * w).astype(BF16) for w in (w0, w1) for a in (lo, hi)]
    rows = jnp.concatenate([x[:, :128], x[:, 128:]] + scaled, axis=0)
    out_ref[...] = dot(table, rows).astype(BF16).reshape(NE, SLAB, 128)


def combine_kernel(
    ids_ref, gain_ref, back_ref, kvg_ref, ao_ref, dq_ref,
    out_ref, in_ref, kg_ref, vg_ref, ao_out, dq_out,
):
    v0, v1 = route_tables(ids_ref[...])
    total = NE * SLAB
    expert, quarter, slot = slab_index(fiota((1, total), 1))
    pick = jnp.where(expert == fiota((EXPERTS, total), 0), 1.0, 0.0).astype(BF16)
    y0 = dot(v0, pick)
    y1 = dot(v1, pick)
    want = slot + 1.0
    hit0 = jnp.where(y0 == want, 1.0, 0.0)
    hit1 = jnp.where(y1 == want, 1.0, 0.0)
    both = hit0 + hit1
    q = [jnp.where(quarter == float(i), 1.0, 0.0) for i in range(4)]
    back = back_ref[...]
    gain = gain_ref[...]
    w0, w1 = column(gain[0:1]), column(gain[1:2])
    for i in range(2):
        part0 = dot((hit0 * q[i]).astype(BF16), back)
        part1 = dot((hit1 * q[i]).astype(BF16), back)
        out_ref[:, i * 128 : (i + 1) * 128] = (part0 * w0 + part1 * w1).astype(BF16)
        in_ref[:, i * 128 : (i + 1) * 128] = dot((both * q[2 + i]).astype(BF16), back).astype(BF16)
    kg_ref[...] = kvg_ref[0]
    vg_ref[...] = kvg_ref[1]
    ao_out[...] = ao_ref[...]
    dq_out[...] = dq_ref[...]


PACK = 8 * GROUP


def pack_table(transposed, rows):
    n = 4 * rows
    r = fiota((1, n) if transposed else (n, 1), 1 if transposed else 0)
    quarter = fdiv(r, rows)
    inner = r - quarter * rows
    source = fdiv(inner, GROUP)
    p = source * SLAB + quarter * GROUP + (inner - source * GROUP)
    return jnp.where(p == fiota((n, n), 0 if transposed else 1), 1.0, 0.0).astype(BF16)


def first_local(rows):
    r = fiota((rows, 1), 0)
    inner = r - fdiv(r, GROUP) * GROUP
    return inner < float(SLOT)


def source(y, i):
    return ((y - 2 * i + 2 * NZ) % NZ) * NX + i


class Place:
    def __init__(self):
        self.e = lax.axis_index("exp")
        self.c = lax.axis_index("ctx")
        self.z, self.x = self.e // NX, self.e % NX
        self.y, self.k = self.c // 2, self.c % 2
        self.sgn = 1 - 2 * self.k
        self.mate = {"exp": self.e, "ctx": self.y * 2 + 1 - self.k}
        self.twin = {"exp": self.e, "ctx": (self.y + 1 - 2 * (self.y % 2)) * 2 + self.k}

    def at_z(self, step):
        return (self.z + self.sgn * step + 2 * NZ) % NZ

    def at_x(self, step):
        return (self.x + self.sgn * step + 2 * NX) % NX

    def at_y(self, step):
        return (self.y + self.sgn * step + 2 * NY) % NY

    def dev_z(self, step):
        return {"exp": self.at_z(step) * NX + self.x, "ctx": self.c}

    def dev_x(self, step):
        return {"exp": self.z * NX + self.at_x(step), "ctx": self.c}

    def dev_y(self, step):
        return {"exp": self.e, "ctx": self.at_y(step) * 2 + self.k}


def remote(src, dst, send, recv, device):
    return pltpu.make_async_remote_copy(
        src_ref=src, dst_ref=dst, send_sem=send, recv_sem=recv, device_id=device,
        device_id_type=MESH,
    )


def remote(src, dst, send, recv, device):
    return pltpu.make_async_remote_copy(
        src_ref=src, dst_ref=dst, send_sem=send, recv_sem=recv, device_id=device,
        device_id_type=MESH,
    )


def exchange(here, send_ref, recv_ref, send_sem, recv_sem, single=False):
    def one(o):
        dest = (here.e + o) % NE
        return remote(
            send_ref.at[dest], recv_ref.at[here.e], send_sem.at[0], recv_sem.at[0],
            {"exp": dest, "ctx": here.c},
        )

    def begin(first, last):
        def go(o, carry):
            one(o).start()
            return carry

        lax.fori_loop(first, last, go, 0)

    def finish():
        rest = pl.ds(0, NE - 1)
        every = remote(send_ref.at[rest], recv_ref.at[rest], send_sem.at[0], recv_sem.at[0], here.mate)
        every.wait_send()
        every.wait_recv()

    return one, begin, finish


def add16(*refs):
    total = refs[0].astype(F32)
    for r in refs[1:]:
        total = total + r.astype(F32)
    return total


ORDER = [4, -3, 3, -2, 2, -1, 1, 0]
STEPS = [0, -1, 1, -2, 2, -3, 3, 4]
LANES = [0, -1, 1, -2]
PEERS = [2, 1, -1]
DEEP = NZ // 2
KEYS = NX * TOK


def around(s):
    return [s] if s in (0, DEEP) else [-s, s]


def opposite(step):
    return step if step == DEEP else -step


def layer_kernel(
    ids_ref, gain_ref, x_ref, g_ref, key_ref, val_ref, q_hbm, do_hbm, gate_hbm, up_hbm, down_hbm,
    ao_ref, dq_ref, ret_ref, kvg_ref,
    q_ref, do_ref, gate_ref, up_ref, down_ref,
    send, recv, rows_ref, part, pmate, ysend, yrecv, full,
    kv, qs, dos, e_ref, mj, m_ref, l_ref, o_ref, d_ref, dq_acc,
    dkv, dmate, zsend, zrecv, sums, xsend, xrecv, tsend, trecv, kg, back,
    s_in, s_l, s_far, r_far, s_kx, r_kx, s_kz, r_kz, s_km, r_km,
    s_pm, r_pm, s_y, r_y, s_g, r_g, s_gm, r_gm,
    s_dm, r_dm, s_z, r_z, s_x, r_x, s_t, r_t, s_c, r_c, s_cm, r_cm, s_ret, r_ret,
):
    here = Place()
    k, z, x, e = here.k, here.z, here.x, here.e
    barrier = pltpu.get_barrier_semaphore()

    def greet(device):
        pl.semaphore_signal(barrier, inc=1, device_id=device, device_id_type=MESH)

    near = [here.mate] + [here.dev_y(s) for s in (1, -1, 2, -2, 4)]
    for device in near:
        greet(device)

    def greet_far(o, carry):
        greet({"exp": (e + o) % NE, "ctx": here.c})
        return carry

    lax.fori_loop(1, NE, greet_far, 0)

    loads = [
        pltpu.make_async_copy(a, b, s_in.at[i])
        for i, (a, b) in enumerate(
            [(gate_hbm, gate_ref), (up_hbm, up_ref), (down_hbm, down_ref), (q_hbm, q_ref), (do_hbm, do_ref)]
        )
    ]
    for c in loads:
        c.start()
    cols = pl.ds(pl.multiple_of((here.y // 2) * HEAD, HEAD), HEAD)
    own = kv.at[k, z, x]

    @pl.when(k == 0)
    def _():
        pltpu.make_async_copy(key_ref.at[:, cols], own, s_l.at[0]).start()

    @pl.when(k == 1)
    def _():
        pltpu.make_async_copy(val_ref.at[:, cols], own, s_l.at[0]).start()

    prepare(ids_ref, gain_ref, x_ref, g_ref, send)
    pltpu.make_async_copy(key_ref.at[:, cols], own, s_l.at[0]).wait()
    pl.semaphore_wait(barrier, len(near) + NE - 1)

    sends = []

    def go(c):
        c.start()
        sends.append(c)

    def by_core(zero, one):
        for core, f in enumerate((zero, one)):

            def start(make, *args):
                make(*args).start()

            @pl.when(k == core)
            def _(f=f, start=start):
                f(start)

    far_one, begin, finish = exchange(here, send, recv, s_far, r_far)
    local = pltpu.make_async_copy(send.at[e], recv.at[e], s_l.at[1])
    local.start()

    def kz(j, zs, xs, to):
        spot = kv.at[k, here.at_z(zs), here.at_x(xs)]
        return remote(spot, spot, s_kz.at[0], r_kz.at[j], here.dev_z(to))

    def kx(j, zs, xs, to):
        spot = kv.at[k, here.at_z(zs), here.at_x(xs)]
        return remote(spot, spot, s_kx.at[0], r_kx.at[j], here.dev_x(to))

    def kv_mate(step):
        i, spot = STEPS.index(step), kv.at[k, here.at_z(step)]
        return remote(spot, spot, s_km.at[0], r_km.at[i], here.mate)

    def lane_start(start, xs):
        i = LANES.index(xs) * 8
        start(kz, i, 0, xs, 1)
        start(kz, i + DEEP, 0, xs, -1)

    def lane_step(start, s):
        for i, xs in enumerate(LANES):
            kz(i * 8 + s - 1, -s, xs, 1).wait_recv()
            if s < DEEP:
                start(kz, i * 8 + s, -s, xs, 1)
                kz(i * 8 + DEEP + s - 1, s, xs, -1).wait_recv()
                if s < DEEP - 1:
                    start(kz, i * 8 + DEEP + s, s, xs, -1)
        for step in around(s):
            start(kv_mate, step)

    def cross_start(start, s):
        for step in around(s):
            i = STEPS.index(step) * 3
            start(kx, i, step, 0, 1)
            start(kx, i + 2, step, 0, -1)

    def cross_mid(start, s):
        for step in around(s):
            i = STEPS.index(step) * 3
            kx(i, step, -1, 1).wait_recv()
            start(kx, i + 1, step, -1, 1)
            kx(i + 2, step, 1, -1).wait_recv()

    def cross_end(start, s):
        for step in around(s):
            kx(STEPS.index(step) * 3 + 1, step, -2, 1).wait_recv()
            start(kv_mate, step)

    def kv_step(t):
        def zero(start):
            if t == 0:
                start(kx, 0, 0, 0, 1)
                start(kx, 2, 0, 0, -1)
                lane_start(start, 0)
            elif t == 1:
                kx(0, 0, -1, 1).wait_recv()
                start(kx, 1, 0, -1, 1)
                lane_start(start, -1)
                kx(2, 0, 1, -1).wait_recv()
                lane_start(start, 1)
            elif t == 2:
                kx(1, 0, -2, 1).wait_recv()
                lane_start(start, -2)
                start(kv_mate, 0)
            else:
                lane_step(start, t - 2)

        def one(start):
            if t == 0:
                start(kz, 0, 0, 0, 1)
                start(kz, DEEP, 0, 0, -1)
                cross_start(start, 0)
                return
            if t <= DEEP:
                kz(t - 1, -t, 0, 1).wait_recv()
                if t < DEEP:
                    start(kz, t, -t, 0, 1)
                    kz(DEEP + t - 1, t, 0, -1).wait_recv()
                    if t < DEEP - 1:
                        start(kz, DEEP + t, t, 0, -1)
                cross_start(start, t)
            if t <= DEEP + 1:
                cross_mid(start, t - 1)
            if t >= 2:
                cross_end(start, t - 2)

        by_core(zero, one)

    def kv_ready(s):
        for step in around(s):
            i, spot = STEPS.index(opposite(step)), kv.at[1 - k, here.at_z(step)]
            remote(spot, spot, s_km.at[0], r_km.at[i], here.mate).wait_recv()

    def pack():
        table = pack_table(False, PACK)
        for g in range(NE // 8):
            slabs = [recv[source(y, i)] for y in (2 * g, 2 * g + 1) for i in range(NX)]
            packed = dot(table, jnp.concatenate(slabs, axis=0)).astype(BF16)
            for i in range(4):
                lanes = slice((i % 2) * 128, (i % 2 + 1) * 128)
                rows_ref[i // 2, g * PACK : (g + 1) * PACK, lanes] = packed[
                    i * PACK : (i + 1) * PACK, :
                ]

    first = first_local(ROWS)

    def product(m):
        if m < 2:
            w_ref = (gate_ref, up_ref)[m]
            rows = rows_ref[0]
            whole = jnp.where(first, dot(rows, w_ref[0]), dot(rows, w_ref[1]))
        else:
            rows = rows_ref[1]
            whole = jnp.where(first, dot_t(rows, down_ref[0]), dot_t(rows, down_ref[1]))
        whole = whole.astype(BF16)
        for c in range(2):
            for y in range(NY):
                part[c, y, m] = whole[y * YROWS : (y + 1) * YROWS, c * HALF : (c + 1) * HALF]
        go(part_mate(m))

    def part_mate(m):
        return remote(part.at[1 - k, :, m], pmate.at[:, m], s_pm.at[m], r_pm.at[m], here.mate)

    def yslot(i, m, to):
        j = m * 7 + i
        return remote(ysend.at[j], yrecv.at[j], s_y.at[0], r_y.at[j], here.dev_y(to))

    def y_step(s, m):
        d = here.at_y(DEEP - s)
        if s == 0:
            part_mate(m).wait_recv()
        j = m * 7 + s
        if s == 0:
            ysend[j] = add16(part[k, d, m], pmate[d, m]).astype(BF16)
        else:
            yslot(s - 1, m, 1).wait_recv()
            ysend[j] = add16(part[k, d, m], pmate[d, m], yrecv[j - 1]).astype(BF16)
        yslot(s, m, 1).start()
        if s < DEEP - 1:
            d = here.at_y(s + 1 - DEEP)
            j = m * 7 + DEEP + s
            if s == 0:
                ysend[j] = add16(part[k, d, m], pmate[d, m]).astype(BF16)
            else:
                yslot(DEEP + s - 1, m, -1).wait_recv()
                ysend[j] = add16(part[k, d, m], pmate[d, m], yrecv[j - 1]).astype(BF16)
            yslot(DEEP + s, m, -1).start()

    def gcopy(i, m, origin, to):
        spot = full.at[k, here.at_y(origin), m]
        j = m * 7 + i
        return remote(spot, spot, s_g.at[0], r_g.at[j], here.dev_y(to))

    def g_mate(i, origin):
        spot = full.at[k, here.at_y(origin)]
        return remote(spot, spot, s_gm.at[0], r_gm.at[i], here.mate)

    def activate():
        total = []
        for m in range(3):
            d = here.y
            yslot(2 * DEEP - 2, m, -1).wait_recv()
            yslot(DEEP - 1, m, 1).wait_recv()
            total.append(
                add16(part[k, d, m], pmate[d, m], yrecv[m * 7 + 2 * DEEP - 2], yrecv[m * 7 + DEEP - 1])
            )
        gate, up, hidden_grad = total
        sig = 1.0 / (1.0 + jnp.exp(-gate))
        act = gate * sig
        full[k, here.y, 0] = (act * up).astype(BF16)
        full[k, here.y, 1] = (hidden_grad * up * sig * (1.0 + gate * (1.0 - sig))).astype(BF16)
        full[k, here.y, 2] = (hidden_grad * act).astype(BF16)
        for m in range(3):
            gcopy(0, m, 0, 1).start()
            gcopy(DEEP, m, 0, -1).start()
        g_mate(0, 0).start()

    def gather_step(s):
        for m in range(3):
            gcopy(s - 1, m, -s, 1).wait_recv()
            if s < DEEP:
                gcopy(s, m, -s, 1).start()
                gcopy(DEEP + s - 1, m, s, -1).wait_recv()
                if s < DEEP - 1:
                    gcopy(DEEP + s, m, s, -1).start()
        g_mate(s, -s).start()
        if s < DEEP:
            g_mate(DEEP + s, s).start()

    def gather_ready(s):
        for step in around(s):
            i = s if step != -s or s == 0 else DEEP + s
            spot = full.at[1 - k, here.at_y(step)]
            remote(spot, spot, s_gm.at[0], r_gm.at[i], here.mate).wait_recv()

    heads = q_ref.shape[1] // HEAD
    width = heads * TOK

    def stack():
        for h in range(heads):
            qs[h * TOK : (h + 1) * TOK, :] = q_ref[:, h * HEAD : (h + 1) * HEAD]
            dos[h * TOK : (h + 1) * TOK, :] = do_ref[:, h * HEAD : (h + 1) * HEAD]
        m_ref[...] = jnp.full((1, width), -jnp.inf, F32)
        l_ref[...] = jnp.zeros((1, width), F32)
        o_ref[...] = jnp.zeros((HEAD, width), F32)
        dq_acc[...] = jnp.zeros((HEAD, width), F32)

    def forward(step):
        j = here.at_z(step)
        lane = lax.broadcasted_iota(jnp.int32, (1, width), 1)
        q_pos = e * TOK + jnp.bitwise_and(lane, TOK - 1)
        row = lax.broadcasted_iota(jnp.int32, (KEYS, 1), 0) + j * KEYS
        s = dot_t(kv[0, j].reshape(KEYS, HEAD), qs[...]) * SCALE
        s = jnp.where(row <= q_pos, s, -jnp.inf)
        old = m_ref[...]
        m = jnp.maximum(old, jnp.max(s, axis=0, keepdims=True))
        p = jnp.exp(s - m)
        p16 = p.astype(BF16)
        e_ref[j] = p16
        mj[j] = m
        m_ref[...] = m
        fade = jnp.exp(old - m)
        l_ref[...] = l_ref[...] * fade + jnp.sum(p, axis=0, keepdims=True)
        o_ref[...] = o_ref[...] * fade + t_dot(kv[1, j].reshape(KEYS, HEAD), p16)

    def normalize():
        inv = 1.0 / l_ref[...]
        l_ref[...] = inv
        o16 = (o_ref[...] * inv).astype(BF16)
        turned = o16.astype(F32).T
        for h in range(heads):
            ao_ref[:, h * HEAD : (h + 1) * HEAD] = turned[h * TOK : (h + 1) * TOK, :].astype(BF16)
        do_t = dos[...].astype(F32).T
        d_ref[...] = jnp.sum(do_t * o16.astype(F32), axis=0, keepdims=True)

    def backward(step):
        j = here.at_z(step)
        keys = kv[0, j].reshape(KEYS, HEAD)
        dp = dot_t(kv[1, j].reshape(KEYS, HEAD), dos[...])
        p = e_ref[j].astype(F32) * (jnp.exp(mj[j] - m_ref[...]) * l_ref[...])
        ds = (p * (dp - d_ref[...])).astype(BF16)
        dkv[0, j] = (dot(ds, qs[...]) * SCALE).astype(BF16).reshape(NX, TOK, HEAD)
        dkv[1, j] = dot(p.astype(BF16), dos[...]).astype(BF16).reshape(NX, TOK, HEAD)
        dq_acc[...] += t_dot(keys, ds)
        i = ORDER.index(opposite(step))
        remote(dkv.at[1 - k, j], dmate.at[j], s_dm.at[0], r_dm.at[i], here.mate).start()

    def query_grad():
        turned = (dq_acc[...] * SCALE).T
        for h in range(heads):
            dq_ref[:, h * HEAD : (h + 1) * HEAD] = turned[h * TOK : (h + 1) * TOK, :].astype(BF16)

    def dkv_in(step):
        i, d = ORDER.index(step), here.at_z(step)
        remote(dkv.at[k, d], dmate.at[d], s_dm.at[0], r_dm.at[i], here.mate).wait_recv()
        return d

    def zslot(i, n, to):
        spot = pl.ds(i * n, n)
        return remote(zsend.at[spot], zrecv.at[spot], s_z.at[0], r_z.at[i], here.dev_z(to))

    def xslot(i, to):
        return remote(xsend.at[i], xrecv.at[i], s_x.at[0], r_x.at[i], here.dev_x(to))

    def wide_step(start, s, to):
        d = dkv_in(DEEP - s if to > 0 else s + 1 - DEEP)
        for h in range(2):
            i = (s if to > 0 else DEEP + s) * 2 + h
            blocks = pl.ds(2 * h, 2)
            terms = [dkv[k, d, blocks], dmate[d, blocks]]
            if s:
                zslot(i - 2, 2, to).wait_recv()
                terms.append(zrecv[2 * i - 4 : 2 * i - 2])
            zsend[2 * i : 2 * i + 2] = add16(*terms).astype(BF16)
            start(zslot, i, 2, to)

    def thin_step(start, s, to):
        i = s if to > 0 else DEEP + s
        total = sums[STEPS.index(DEEP - s if to > 0 else s + 1 - DEEP)]
        if s:
            zslot(i - 1, 1, to).wait_recv()
            total = total + zrecv[i - 1].astype(F32)
        zsend[i] = total.astype(BF16)
        start(zslot, i, 1, to)

    def x_start(start, s):
        for step in around(s):
            d, i = dkv_in(step), STEPS.index(step) * 3
            for slot, xs in enumerate(PEERS):
                j = here.at_x(xs)
                xsend[i + slot] = add16(dkv[k, d, j], dmate[d, j]).astype(BF16)
                start(xslot, i + slot, xs)

    def x_end(s):
        for step in around(s):
            d, i = here.at_z(step), STEPS.index(step) * 3
            for slot, xs in enumerate(PEERS):
                xslot(i + slot, xs).wait_recv()
            sums[i // 3] = add16(
                dkv[k, d, x], dmate[d, x], xrecv[i], xrecv[i + 1], xrecv[i + 2]
            )

    def grad_step(t):
        def zero(start):
            if t < DEEP:
                if t:
                    wide_step(start, t - 1, -1)
                wide_step(start, t, 1)
            elif t == DEEP:
                d = dkv_in(0)
                for i in (3, 2 * DEEP - 2):
                    for h in range(2):
                        zslot(2 * i + h, 2, 1 if i == 3 else -1).wait_recv()
                last = pl.ds(4 * (2 * DEEP - 2), 4)
                sums[0:4] = add16(dkv[k, d], dmate[d], zrecv[12:16], zrecv[last])
                for slot, xs in enumerate(PEERS):
                    xsend[slot] = sums[here.at_x(xs)].astype(BF16)
                    start(xslot, slot, xs)
            else:
                for slot, xs in enumerate(PEERS):
                    xslot(slot, xs).wait_recv()
                tsend[...] = (sums[x] + add16(xrecv[0], xrecv[1], xrecv[2])).astype(BF16)

        def one(start):
            if t <= DEEP:
                x_start(start, DEEP - t)
            if t >= 1:
                x_end(DEEP + 1 - t)
                if t <= DEEP:
                    thin_step(start, t - 1, 1)
                    if t > 1:
                        thin_step(start, t - 2, -1)
                else:
                    zslot(DEEP - 1, 1, 1).wait_recv()
                    zslot(2 * DEEP - 2, 1, -1).wait_recv()
                    total = sums[0] + add16(zrecv[DEEP - 1], zrecv[2 * DEEP - 2])
                    tsend[...] = total.astype(BF16)

        by_core(zero, one)
        if t == DEEP + 1:
            go(twin)

    twin = remote(tsend, trecv, s_t.at[0], r_t.at[0], here.twin)

    def spot(which, step):
        head = here.at_y(step) // 2
        return kvg_ref.at[which, :, pl.ds(pl.multiple_of(head * HEAD, HEAD), HEAD)]

    mine = pltpu.make_async_copy(kg, spot(k, 0), s_l.at[2])

    def spread():
        twin.wait_recv()
        kg[...] = add16(tsend[...], trecv[...]).astype(BF16)
        for i, step in enumerate((4, 2, 6)):
            go(remote(kg, spot(k, 0), s_c.at[i], r_c.at[i], here.dev_y(step)))
        go(remote(kg, spot(k, 0), s_cm.at[3], r_cm.at[3], here.mate))
        mine.start()

    def spread_end():
        order = (4, 2, 6)
        for i in (1, 2, 0):
            there = spot(k, -order[i])
            remote(kg, there, s_c.at[i], r_c.at[i], here.dev_y(-order[i])).wait_recv()
            go(remote(there, there, s_cm.at[i], r_cm.at[i], here.mate))
        remote(kg, spot(1 - k, 0), s_cm.at[3], r_cm.at[3], here.mate).wait_recv()
        for i in (1, 2, 0):
            there = spot(1 - k, order[i])
            remote(there, there, s_cm.at[i], r_cm.at[i], here.mate).wait_recv()
        mine.wait()

    ret_one, ret_begin, ret_finish = exchange(here, back, ret_ref, s_ret, r_ret)
    ret_local = pltpu.make_async_copy(back.at[e], ret_ref.at[e], s_l.at[3])

    def experts_out(s):
        blocks = [here.at_y(step) for step in around(s)]
        rows = len(blocks) * YROWS
        near = first_local(rows)

        def both(m, weight, transposed):
            parts = [
                jnp.concatenate([full[0, y, m], full[1, y, m]], axis=1) for y in blocks
            ]
            whole = jnp.concatenate(parts, axis=0)
            f = dot_t if transposed else dot
            return jnp.where(near, f(whole, weight[0]), f(whole, weight[1]))

        route_out = both(0, down_ref, False).astype(BF16)
        route_in = (both(1, gate_ref, True) + both(2, up_ref, True)).astype(BF16)
        quarters = [route_out[:, :128], route_out[:, 128:], route_in[:, :128], route_in[:, 128:]]
        out = dot(pack_table(True, rows), jnp.concatenate(quarters, axis=0)).astype(BF16)
        for b, y in enumerate(blocks):
            for i in range(NX):
                dest = source(y, i)
                r = (b * NX + i) * SLAB
                back[dest] = out[r : r + SLAB]
                offset = (dest + NE - e) % NE

                @pl.when(offset != 0)
                def _():
                    ret_one(offset).start()

                @pl.when(offset == 0)
                def _():
                    ret_local.start()

    def each_y(s):
        for m in range(3):
            y_step(s, m)

    def drain(sem, ref):
        remote(ref, ref, sem.at[0], sem.at[0], here.mate).wait_send()

    kv_step(0)
    begin(1, 17)
    kv_step(1)
    begin(17, NE)
    for c in loads:
        c.wait()
    stack()
    kv_step(2)
    kv_ready(0)
    forward(0)
    kv_step(3)
    local.wait()
    finish()
    pack()
    product(0)
    kv_step(4)
    product(1)
    y_step(0, 0)
    product(2)
    y_step(0, 1)
    kv_step(5)
    y_step(0, 2)
    kv_ready(1)
    forward(-1)
    forward(1)
    kv_step(6)
    each_y(1)
    kv_ready(2)
    forward(-2)
    forward(2)
    each_y(2)
    kv_ready(3)
    forward(-3)
    forward(3)
    kv_ready(4)
    forward(4)
    normalize()
    each_y(3)
    backward(4)
    backward(-3)
    grad_step(0)
    activate()
    backward(3)
    grad_step(1)
    backward(-2)
    gather_step(1)
    backward(2)
    grad_step(2)
    backward(-1)
    gather_step(2)
    backward(1)
    grad_step(3)
    backward(0)
    gather_step(3)
    grad_step(4)
    gather_ready(0)
    experts_out(0)
    gather_step(4)
    gather_ready(1)
    experts_out(1)
    grad_step(5)
    gather_ready(2)
    experts_out(2)
    gather_ready(3)
    spread()
    experts_out(3)
    gather_ready(4)
    experts_out(4)
    query_grad()
    spread_end()
    ret_finish()
    ret_local.wait()
    for c in sends:
        c.wait_send()
    drain(s_km, kv.at[k])
    drain(s_y, ysend)
    drain(s_g, full.at[k, pl.ds(0, 7)])
    drain(s_gm, full.at[k])
    drain(s_dm, dkv.at[1 - k])

    def drain_zero(start):
        drain(s_kx, kv.at[k, 0, pl.ds(0, 3)])
        drain(s_kz, kv.at[k, pl.ds(0, 7)])
        drain(s_z, zsend)
        drain(s_x, xsend.at[pl.ds(0, 3)])

    def drain_one(start):
        drain(s_kx, kv.at[k, :, pl.ds(0, 3)])
        drain(s_kz, kv.at[k, pl.ds(0, 7), 0])
        drain(s_z, zsend.at[pl.ds(0, 7)])
        drain(s_x, xsend)

    by_core(drain_zero, drain_one)


def vmem():
    return pl.BlockSpec(memory_space=pltpu.VMEM)


def dma(n):
    return pltpu.SemaphoreType.DMA((n,))


def call(kernel, outs, scratch, *args, specs=None, collective=None, name=None, flops=0):
    params = {"vmem_limit_bytes": VMEM_LIMIT}
    if collective is not None:
        params.update(collective_id=collective, has_side_effects=True)
    return pl.pallas_call(
        kernel,
        out_shape=outs,
        in_specs=specs or [vmem()] * len(args),
        out_specs=jax.tree.map(lambda o: vmem(), outs),
        scratch_shapes=scratch,
        compiler_params=pltpu.CompilerParams(**params),
        name=name,
    )(*args)


def shape(*dims, dtype=BF16):
    return jax.ShapeDtypeStruct(dims, dtype)


def body(q, key, val, do, x, g, ids, gain, gate, up, down):
    ids, gain = ids.T, gain.T
    hbm = pl.BlockSpec(memory_space=pl.ANY)
    heads = q.shape[1] // HEAD
    width = heads * TOK
    yslab, zslab, block = (YROWS, HALF), (NX, TOK, HEAD), (TOK, HEAD)

    def f32(*dims):
        return pltpu.VMEM(dims, F32)

    def b16(*dims):
        return pltpu.VMEM(dims, BF16)

    sems = [5, 4, 1, 1, 1, 24, 1, 32, 1, 8, 3, 3, 1, 21, 1, 21, 1, 8]
    sems += [1, 8, 1, 14, 1, 24, 1, 1, 3, 3, 4, 4, 1, 1]
    attn_out, dq, returned, kvg = call(
        layer_kernel,
        (shape(*q.shape), shape(*q.shape), shape(NE, SLAB, 128), shape(2, TOK, 4 * HEAD)),
        [
            b16(*q.shape), b16(*do.shape), b16(*gate.shape), b16(*up.shape), b16(*down.shape),
            b16(NE, SLAB, 128), b16(NE, SLAB, 128), b16(2, ROWS, 256),
            b16(2, NY, 3, *yslab), b16(NY, 3, *yslab), b16(21, *yslab), b16(21, *yslab),
            b16(2, NY, 3, *yslab),
            b16(2, NZ, *zslab), b16(width, HEAD), b16(width, HEAD), b16(NZ, KEYS, width),
            f32(NZ, 1, width), f32(1, width), f32(1, width), f32(HEAD, width), f32(1, width),
            f32(HEAD, width),
            b16(2, NZ, *zslab), b16(NZ, *zslab), b16(28, *block), b16(28, *block), f32(8, *block),
            b16(24, *block), b16(24, *block), b16(*block), b16(*block), b16(*block),
            b16(NE, SLAB, 128),
        ]
        + [dma(n) for n in sems],
        ids, gain, x, g, key, val, q, do, gate, up, down,
        specs=[vmem()] * 4 + [hbm] * 7, collective=0, name="layer",
    )
    moe_out, input_grad, key_grad, value_grad, attn_out, dq = call(
        combine_kernel,
        (shape(TOK, 256), shape(TOK, 256), shape(TOK, 512), shape(TOK, 512),
         shape(*q.shape), shape(*q.shape)), [],
        ids, gain, returned.reshape(NE * SLAB, 128), kvg, attn_out, dq, name="combine",
    )
    return attn_out, dq, key_grad, value_grad, moe_out, input_grad


def solution(mesh):
    rows, both = P("exp", None), P("exp", "ctx")
    return jax.shard_map(
        body,
        mesh=mesh,
        in_specs=(
            both, rows, rows, both, both, both, rows, rows,
            P("exp", "ctx", None), P("exp", "ctx", None), P("exp", None, "ctx"),
        ),
        out_specs=(both, both, rows, rows, both, both),
        check_vma=False,
    )
```

```python
import functools

import jax
import jax.numpy as jnp
from jax import lax
from jax.experimental import pallas as pl
from jax.experimental.pallas import tpu as pltpu
from jax.sharding import PartitionSpec as P

MESH = pl.DeviceIdType.MESH
F32 = jnp.float32
BF16 = jnp.bfloat16
HEAD = 128
NX, NZ, NY = 4, 8, 8
NE = NX * NZ
TOK = 128
LOCAL = 2
EXPERTS = LOCAL * NE
SLOT = 6
GROUP = LOCAL * SLOT
SLAB = 4 * GROUP
ROWS = NE * GROUP
FF = 768
HALF = FF // 2
YROWS = ROWS // NY
SCALE = HEAD ** (-0.5)
VMEM_LIMIT = 60 * 1024 * 1024


def dot(a, b):
    return jnp.dot(a, b, preferred_element_type=F32)


def dot_t(a, b):
    return lax.dot_general(a, b, (((1,), (1,)), ((), ())), preferred_element_type=F32)


def t_dot(a, b):
    return lax.dot_general(a, b, (((0,), (0,)), ((), ())), preferred_element_type=F32)


def fdiv(a, n):
    return jnp.floor((a + 0.5) * (1.0 / n))


def fiota(shape, dim):
    return lax.broadcasted_iota(jnp.int32, shape, dim).astype(F32)


def column(row):
    return jnp.broadcast_to(row, (TOK, TOK)).T


def route_tables(ids):
    lane = fiota((TOK, EXPERTS), 1)
    ids = ids.astype(F32)
    first = jnp.where(column(ids[0:1])[:, :EXPERTS] == lane, 1.0, 0.0)
    second = jnp.where(column(ids[1:2])[:, :EXPERTS] == lane, 1.0, 0.0)
    row = lax.broadcasted_iota(jnp.int32, (TOK, TOK), 0)
    col = lax.broadcasted_iota(jnp.int32, (TOK, TOK), 1)
    before = jnp.where(col < row, 1.0, 0.0).astype(BF16)
    place = dot(before, (first + second).astype(BF16)) + 1.0
    return (first * place).astype(BF16), (second * place).astype(BF16)


def slab_index(p):
    dest = fdiv(p, SLAB)
    inner = p - dest * SLAB
    quarter = fdiv(inner, GROUP)
    inner = inner - quarter * GROUP
    local = fdiv(inner, SLOT)
    slot = inner - local * SLOT
    return dest * LOCAL + local, quarter, slot


def prepare(ids_ref, gain_ref, x_ref, g_ref, out_ref):
    v0, v1 = route_tables(ids_ref[...])
    total = NE * SLAB
    expert, quarter, slot = slab_index(fiota((total, 1), 0))
    pick = jnp.where(expert == fiota((total, EXPERTS), 1), 1.0, 0.0).astype(BF16)
    y0 = dot_t(pick, v0)
    y1 = dot_t(pick, v1)
    want = slot + 1.0
    hit0 = jnp.where(y0 == want, 1.0, 0.0)
    hit1 = jnp.where(y1 == want, 1.0, 0.0)
    both = hit0 + hit1
    x = x_ref[...]
    g = g_ref[...].astype(F32)
    gain = gain_ref[...]
    w0, w1 = column(gain[0:1]), column(gain[1:2])
    lo, hi = g[:, :128], g[:, 128:]
    s0 = jnp.concatenate([lo * w0, hi * w0], axis=1).astype(BF16)
    s1 = jnp.concatenate([lo * w1, hi * w1], axis=1).astype(BF16)
    rows = dot(both.astype(BF16), x)
    hits = jnp.concatenate([hit0, hit1], axis=1).astype(BF16)
    scaled = dot(hits, jnp.concatenate([s0, s1], axis=0))
    out = jnp.where(
        quarter < 2.0,
        jnp.where(quarter < 1.0, rows[:, :128], rows[:, 128:]),
        jnp.where(quarter < 3.0, scaled[:, :128], scaled[:, 128:]),
    )
    out_ref[...] = out.astype(BF16).reshape(NE, SLAB, 128)


def combine_tables(ids_ref, tab_ref):
    v0, v1 = route_tables(ids_ref[...])
    total = NE * SLAB
    expert, quarter, slot = slab_index(fiota((1, total), 1))
    pick = jnp.where(expert == fiota((EXPERTS, total), 0), 1.0, 0.0).astype(BF16)
    y0 = dot(v0, pick)
    y1 = dot(v1, pick)
    want = slot + 1.0
    hit0 = jnp.where(y0 == want, 1.0, 0.0)
    hit1 = jnp.where(y1 == want, 1.0, 0.0)
    q = [jnp.where(quarter == float(i), 1.0, 0.0) for i in range(4)]
    for i in range(2):
        tab_ref[i] = (hit0 * q[i]).astype(BF16)
        tab_ref[2 + i] = (hit1 * q[i]).astype(BF16)
        tab_ref[4 + i] = ((hit0 + hit1) * q[2 + i]).astype(BF16)


def combine(gain_ref, tab_ref, ret_ref, out_ref, in_ref):
    back = ret_ref[...].reshape(NE * SLAB, 128)
    gain = gain_ref[...]
    w0, w1 = column(gain[0:1]), column(gain[1:2])
    for i in range(2):
        lanes = slice(i * 128, (i + 1) * 128)
        mixed = dot(tab_ref[i], back) * w0 + dot(tab_ref[2 + i], back) * w1
        out_ref[:, lanes] = mixed.astype(BF16)
        in_ref[:, lanes] = dot(tab_ref[4 + i], back).astype(BF16)


def close_kernel(mo_ref, ig_ref, kvg_ref, ao_ref, dq_ref, mo_out, ig_out, kg_ref, vg_ref, ao_out, dq_out):
    kg_ref[...] = kvg_ref[0]
    vg_ref[...] = kvg_ref[1]
    mo_out[...] = mo_ref[...]
    ig_out[...] = ig_ref[...]
    ao_out[...] = ao_ref[...]
    dq_out[...] = dq_ref[...]


PACK = 8 * GROUP


def pack_table(transposed, rows):
    n = 4 * rows
    r = fiota((1, n) if transposed else (n, 1), 1 if transposed else 0)
    quarter = fdiv(r, rows)
    inner = r - quarter * rows
    source = fdiv(inner, GROUP)
    p = source * SLAB + quarter * GROUP + (inner - source * GROUP)
    return jnp.where(p == fiota((n, n), 0 if transposed else 1), 1.0, 0.0).astype(BF16)


def first_local(rows):
    r = fiota((rows, 1), 0)
    inner = r - fdiv(r, GROUP) * GROUP
    return inner < float(SLOT)


def source(y, i):
    return ((y - 2 * i + 2 * NZ) % NZ) * NX + i


class Place:
    def __init__(self):
        self.e = lax.axis_index("exp")
        self.c = lax.axis_index("ctx")
        self.z, self.x = self.e // NX, self.e % NX
        self.y, self.k = self.c // 2, self.c % 2
        self.sgn = 1 - 2 * self.k
        self.mate = {"exp": self.e, "ctx": self.y * 2 + 1 - self.k}
        self.twin = {"exp": self.e, "ctx": (self.y + 1 - 2 * (self.y % 2)) * 2 + self.k}

    def at_z(self, step):
        return (self.z + self.sgn * step + 2 * NZ) % NZ

    def at_x(self, step):
        return (self.x + self.sgn * step + 2 * NX) % NX

    def at_y(self, step):
        return (self.y + self.sgn * step + 2 * NY) % NY

    def dev_z(self, step):
        return {"exp": self.at_z(step) * NX + self.x, "ctx": self.c}

    def dev_x(self, step):
        return {"exp": self.z * NX + self.at_x(step), "ctx": self.c}

    def dev_y(self, step):
        return {"exp": self.e, "ctx": self.at_y(step) * 2 + self.k}


def remote(src, dst, send, recv, device):
    return pltpu.make_async_remote_copy(
        src_ref=src, dst_ref=dst, send_sem=send, recv_sem=recv, device_id=device,
        device_id_type=MESH,
    )


def remote(src, dst, send, recv, device):
    return pltpu.make_async_remote_copy(
        src_ref=src, dst_ref=dst, send_sem=send, recv_sem=recv, device_id=device,
        device_id_type=MESH,
    )


def exchange(here, send_ref, recv_ref, send_sem, recv_sem, single=False):
    def one(o):
        dest = (here.e + o) % NE
        return remote(
            send_ref.at[dest], recv_ref.at[here.e], send_sem.at[0], recv_sem.at[0],
            {"exp": dest, "ctx": here.c},
        )

    def begin(first, last):
        def go(o, carry):
            one(o).start()
            return carry

        lax.fori_loop(first, last, go, 0)

    def finish():
        rest = pl.ds(0, NE - 1)
        every = remote(send_ref.at[rest], recv_ref.at[rest], send_sem.at[0], recv_sem.at[0], here.mate)
        every.wait_send()
        every.wait_recv()

    return one, begin, finish


def add16(*refs):
    total = refs[0].astype(F32)
    for r in refs[1:]:
        total = total + r.astype(F32)
    return total


ORDER = [4, -3, 3, -2, 2, -1, 1, 0]
STEPS = [0, -1, 1, -2, 2, -3, 3, 4]
LANES = [0, -1, 1, -2]
PEERS = [2, 1, -1]
DEEP = NZ // 2
KEYS = NX * TOK


def around(s):
    return [s] if s in (0, DEEP) else [-s, s]


def opposite(step):
    return step if step == DEEP else -step


def layer_kernel(
    ids_ref, gain_ref, x_ref, g_ref, key_ref, val_ref, q_hbm, do_hbm, gate_hbm, up_hbm, down_hbm,
    ao_ref, dq_ref, mo_ref, ig_ref, kvg_ref,
    ret_ref, tab_ref, q_ref, do_ref, gate_ref, up_ref, down_ref,
    send, recv, rows_ref, part, pmate, ysend, yrecv, full,
    kv, qs, dos, e_ref, mj, m_ref, l_ref, o_ref, d_ref, dq_acc,
    dkv, dmate, zsend, zrecv, sums, xsend, xrecv, tsend, trecv, kg, back,
    s_in, s_l, s_far, r_far, s_kx, r_kx, s_kz, r_kz, s_km, r_km,
    s_pm, r_pm, s_y, r_y, s_g, r_g, s_gm, r_gm,
    s_dm, r_dm, s_z, r_z, s_x, r_x, s_t, r_t, s_c, r_c, s_cm, r_cm, s_ret, r_ret,
):
    here = Place()
    k, z, x, e = here.k, here.z, here.x, here.e
    barrier = pltpu.get_barrier_semaphore()

    def greet(device):
        pl.semaphore_signal(barrier, inc=1, device_id=device, device_id_type=MESH)

    near = [here.mate] + [here.dev_y(s) for s in (1, -1, 2, -2, 4)]
    for device in near:
        greet(device)

    def greet_far(o, carry):
        greet({"exp": (e + o) % NE, "ctx": here.c})
        return carry

    lax.fori_loop(1, NE, greet_far, 0)

    loads = [
        pltpu.make_async_copy(a, b, s_in.at[i])
        for i, (a, b) in enumerate(
            [(gate_hbm, gate_ref), (up_hbm, up_ref), (down_hbm, down_ref), (q_hbm, q_ref), (do_hbm, do_ref)]
        )
    ]
    for c in loads:
        c.start()
    cols = pl.ds(pl.multiple_of((here.y // 2) * HEAD, HEAD), HEAD)
    own = kv.at[k, z, x]

    @pl.when(k == 0)
    def _():
        pltpu.make_async_copy(key_ref.at[:, cols], own, s_l.at[0]).start()

    @pl.when(k == 1)
    def _():
        pltpu.make_async_copy(val_ref.at[:, cols], own, s_l.at[0]).start()

    prepare(ids_ref, gain_ref, x_ref, g_ref, send)
    pltpu.make_async_copy(key_ref.at[:, cols], own, s_l.at[0]).wait()
    pl.semaphore_wait(barrier, len(near) + NE - 1)

    sends = []

    def go(c):
        c.start()
        sends.append(c)

    def by_core(zero, one):
        for core, f in enumerate((zero, one)):

            def start(make, *args):
                make(*args).start()

            @pl.when(k == core)
            def _(f=f, start=start):
                f(start)

    far_one, begin, finish = exchange(here, send, recv, s_far, r_far)
    local = pltpu.make_async_copy(send.at[e], recv.at[e], s_l.at[1])
    local.start()

    def kz(j, zs, xs, to):
        spot = kv.at[k, here.at_z(zs), here.at_x(xs)]
        return remote(spot, spot, s_kz.at[0], r_kz.at[j], here.dev_z(to))

    def kx(j, zs, xs, to):
        spot = kv.at[k, here.at_z(zs), here.at_x(xs)]
        return remote(spot, spot, s_kx.at[0], r_kx.at[j], here.dev_x(to))

    def kv_mate(step):
        i, spot = STEPS.index(step), kv.at[k, here.at_z(step)]
        return remote(spot, spot, s_km.at[0], r_km.at[i], here.mate)

    def lane_start(start, xs):
        i = LANES.index(xs) * 8
        start(kz, i, 0, xs, 1)
        start(kz, i + DEEP, 0, xs, -1)

    def lane_step(start, s):
        for i, xs in enumerate(LANES):
            kz(i * 8 + s - 1, -s, xs, 1).wait_recv()
            if s < DEEP:
                start(kz, i * 8 + s, -s, xs, 1)
                kz(i * 8 + DEEP + s - 1, s, xs, -1).wait_recv()
                if s < DEEP - 1:
                    start(kz, i * 8 + DEEP + s, s, xs, -1)
        for step in around(s):
            start(kv_mate, step)

    def cross_start(start, s):
        for step in around(s):
            i = STEPS.index(step) * 3
            start(kx, i, step, 0, 1)
            start(kx, i + 2, step, 0, -1)

    def cross_mid(start, s):
        for step in around(s):
            i = STEPS.index(step) * 3
            kx(i, step, -1, 1).wait_recv()
            start(kx, i + 1, step, -1, 1)
            kx(i + 2, step, 1, -1).wait_recv()

    def cross_end(start, s):
        for step in around(s):
            kx(STEPS.index(step) * 3 + 1, step, -2, 1).wait_recv()
            start(kv_mate, step)

    def kv_step(t):
        def zero(start):
            if t == 0:
                start(kx, 0, 0, 0, 1)
                start(kx, 2, 0, 0, -1)
                lane_start(start, 0)
            elif t == 1:
                kx(0, 0, -1, 1).wait_recv()
                start(kx, 1, 0, -1, 1)
                lane_start(start, -1)
                kx(2, 0, 1, -1).wait_recv()
                lane_start(start, 1)
            elif t == 2:
                kx(1, 0, -2, 1).wait_recv()
                lane_start(start, -2)
                start(kv_mate, 0)
            else:
                lane_step(start, t - 2)

        def one(start):
            if t == 0:
                start(kz, 0, 0, 0, 1)
                start(kz, DEEP, 0, 0, -1)
                cross_start(start, 0)
                return
            if t <= DEEP:
                kz(t - 1, -t, 0, 1).wait_recv()
                if t < DEEP:
                    start(kz, t, -t, 0, 1)
                    kz(DEEP + t - 1, t, 0, -1).wait_recv()
                    if t < DEEP - 1:
                        start(kz, DEEP + t, t, 0, -1)
                cross_start(start, t)
            if t <= DEEP + 1:
                cross_mid(start, t - 1)
            if t >= 2:
                cross_end(start, t - 2)

        by_core(zero, one)

    def kv_ready(s):
        for step in around(s):
            i, spot = STEPS.index(opposite(step)), kv.at[1 - k, here.at_z(step)]
            remote(spot, spot, s_km.at[0], r_km.at[i], here.mate).wait_recv()

    def pack():
        table = pack_table(False, PACK)
        for g in range(NE // 8):
            slabs = [recv[source(y, i)] for y in (2 * g, 2 * g + 1) for i in range(NX)]
            packed = dot(table, jnp.concatenate(slabs, axis=0)).astype(BF16)
            for i in range(4):
                lanes = slice((i % 2) * 128, (i % 2 + 1) * 128)
                rows_ref[i // 2, g * PACK : (g + 1) * PACK, lanes] = packed[
                    i * PACK : (i + 1) * PACK, :
                ]

    first = first_local(ROWS)

    def product(m):
        if m < 2:
            w_ref = (gate_ref, up_ref)[m]
            rows = rows_ref[0]
            whole = jnp.where(first, dot(rows, w_ref[0]), dot(rows, w_ref[1]))
        else:
            rows = rows_ref[1]
            whole = jnp.where(first, dot_t(rows, down_ref[0]), dot_t(rows, down_ref[1]))
        whole = whole.astype(BF16)
        for c in range(2):
            for y in range(NY):
                part[c, y, m] = whole[y * YROWS : (y + 1) * YROWS, c * HALF : (c + 1) * HALF]
        go(part_mate(m))

    def part_mate(m):
        return remote(part.at[1 - k, :, m], pmate.at[:, m], s_pm.at[m], r_pm.at[m], here.mate)

    def yslot(i, m, to):
        j = m * 7 + i
        return remote(ysend.at[j], yrecv.at[j], s_y.at[0], r_y.at[j], here.dev_y(to))

    def y_step(s, m):
        d = here.at_y(DEEP - s)
        if s == 0:
            part_mate(m).wait_recv()
        j = m * 7 + s
        if s == 0:
            ysend[j] = add16(part[k, d, m], pmate[d, m]).astype(BF16)
        else:
            yslot(s - 1, m, 1).wait_recv()
            ysend[j] = add16(part[k, d, m], pmate[d, m], yrecv[j - 1]).astype(BF16)
        yslot(s, m, 1).start()
        if s < DEEP - 1:
            d = here.at_y(s + 1 - DEEP)
            j = m * 7 + DEEP + s
            if s == 0:
                ysend[j] = add16(part[k, d, m], pmate[d, m]).astype(BF16)
            else:
                yslot(DEEP + s - 1, m, -1).wait_recv()
                ysend[j] = add16(part[k, d, m], pmate[d, m], yrecv[j - 1]).astype(BF16)
            yslot(DEEP + s, m, -1).start()

    def gcopy(i, m, origin, to):
        spot = full.at[k, here.at_y(origin), m]
        j = m * 7 + i
        return remote(spot, spot, s_g.at[0], r_g.at[j], here.dev_y(to))

    def g_mate(i, origin):
        spot = full.at[k, here.at_y(origin)]
        return remote(spot, spot, s_gm.at[0], r_gm.at[i], here.mate)

    def activate():
        total = []
        for m in range(3):
            d = here.y
            yslot(2 * DEEP - 2, m, -1).wait_recv()
            yslot(DEEP - 1, m, 1).wait_recv()
            total.append(
                add16(part[k, d, m], pmate[d, m], yrecv[m * 7 + 2 * DEEP - 2], yrecv[m * 7 + DEEP - 1])
            )
        gate, up, hidden_grad = total
        sig = 1.0 / (1.0 + jnp.exp(-gate))
        act = gate * sig
        full[k, here.y, 0] = (act * up).astype(BF16)
        full[k, here.y, 1] = (hidden_grad * up * sig * (1.0 + gate * (1.0 - sig))).astype(BF16)
        full[k, here.y, 2] = (hidden_grad * act).astype(BF16)
        for m in range(3):
            gcopy(0, m, 0, 1).start()
            gcopy(DEEP, m, 0, -1).start()
        g_mate(0, 0).start()

    def gather_step(s):
        for m in range(3):
            gcopy(s - 1, m, -s, 1).wait_recv()
            if s < DEEP:
                gcopy(s, m, -s, 1).start()
                gcopy(DEEP + s - 1, m, s, -1).wait_recv()
                if s < DEEP - 1:
                    gcopy(DEEP + s, m, s, -1).start()
        g_mate(s, -s).start()
        if s < DEEP:
            g_mate(DEEP + s, s).start()

    def gather_ready(s):
        for step in around(s):
            i = s if step != -s or s == 0 else DEEP + s
            spot = full.at[1 - k, here.at_y(step)]
            remote(spot, spot, s_gm.at[0], r_gm.at[i], here.mate).wait_recv()

    heads = q_ref.shape[1] // HEAD
    width = heads * TOK

    def stack():
        for h in range(heads):
            qs[h * TOK : (h + 1) * TOK, :] = q_ref[:, h * HEAD : (h + 1) * HEAD]
            dos[h * TOK : (h + 1) * TOK, :] = do_ref[:, h * HEAD : (h + 1) * HEAD]
        m_ref[...] = jnp.full((1, width), -jnp.inf, F32)
        l_ref[...] = jnp.zeros((1, width), F32)
        o_ref[...] = jnp.zeros((HEAD, width), F32)
        dq_acc[...] = jnp.zeros((HEAD, width), F32)

    def forward(step):
        j = here.at_z(step)
        lane = lax.broadcasted_iota(jnp.int32, (1, width), 1)
        q_pos = e * TOK + jnp.bitwise_and(lane, TOK - 1)
        row = lax.broadcasted_iota(jnp.int32, (KEYS, 1), 0) + j * KEYS
        s = dot_t(kv[0, j].reshape(KEYS, HEAD), qs[...]) * SCALE
        s = jnp.where(row <= q_pos, s, -jnp.inf)
        old = m_ref[...]
        m = jnp.maximum(old, jnp.max(s, axis=0, keepdims=True))
        p = jnp.exp(s - m)
        p16 = p.astype(BF16)
        e_ref[j] = p16
        mj[j] = m
        m_ref[...] = m
        fade = jnp.exp(old - m)
        l_ref[...] = l_ref[...] * fade + jnp.sum(p, axis=0, keepdims=True)
        o_ref[...] = o_ref[...] * fade + t_dot(kv[1, j].reshape(KEYS, HEAD), p16)

    def normalize():
        inv = 1.0 / l_ref[...]
        l_ref[...] = inv
        o16 = (o_ref[...] * inv).astype(BF16)
        turned = o16.astype(F32).T
        for h in range(heads):
            ao_ref[:, h * HEAD : (h + 1) * HEAD] = turned[h * TOK : (h + 1) * TOK, :].astype(BF16)
        do_t = dos[...].astype(F32).T
        d_ref[...] = jnp.sum(do_t * o16.astype(F32), axis=0, keepdims=True)

    def backward(step):
        j = here.at_z(step)
        keys = kv[0, j].reshape(KEYS, HEAD)
        dp = dot_t(kv[1, j].reshape(KEYS, HEAD), dos[...])
        p = e_ref[j].astype(F32) * (jnp.exp(mj[j] - m_ref[...]) * l_ref[...])
        ds = (p * (dp - d_ref[...])).astype(BF16)
        dkv[0, j] = (dot(ds, qs[...]) * SCALE).astype(BF16).reshape(NX, TOK, HEAD)
        dkv[1, j] = dot(p.astype(BF16), dos[...]).astype(BF16).reshape(NX, TOK, HEAD)
        dq_acc[...] += t_dot(keys, ds)
        i = ORDER.index(opposite(step))
        remote(dkv.at[1 - k, j], dmate.at[j], s_dm.at[0], r_dm.at[i], here.mate).start()

    def query_grad():
        turned = (dq_acc[...] * SCALE).T
        for h in range(heads):
            dq_ref[:, h * HEAD : (h + 1) * HEAD] = turned[h * TOK : (h + 1) * TOK, :].astype(BF16)

    def dkv_in(step):
        i, d = ORDER.index(step), here.at_z(step)
        remote(dkv.at[k, d], dmate.at[d], s_dm.at[0], r_dm.at[i], here.mate).wait_recv()
        return d

    def zslot(i, n, to):
        spot = pl.ds(i * n, n)
        return remote(zsend.at[spot], zrecv.at[spot], s_z.at[0], r_z.at[i], here.dev_z(to))

    def xslot(i, to):
        return remote(xsend.at[i], xrecv.at[i], s_x.at[0], r_x.at[i], here.dev_x(to))

    def wide_step(start, s, to):
        d = dkv_in(DEEP - s if to > 0 else s + 1 - DEEP)
        for h in range(2):
            i = (s if to > 0 else DEEP + s) * 2 + h
            blocks = pl.ds(2 * h, 2)
            terms = [dkv[k, d, blocks], dmate[d, blocks]]
            if s:
                zslot(i - 2, 2, to).wait_recv()
                terms.append(zrecv[2 * i - 4 : 2 * i - 2])
            zsend[2 * i : 2 * i + 2] = add16(*terms).astype(BF16)
            start(zslot, i, 2, to)

    def thin_step(start, s, to):
        i = s if to > 0 else DEEP + s
        total = sums[STEPS.index(DEEP - s if to > 0 else s + 1 - DEEP)]
        if s:
            zslot(i - 1, 1, to).wait_recv()
            total = total + zrecv[i - 1].astype(F32)
        zsend[i] = total.astype(BF16)
        start(zslot, i, 1, to)

    def x_start(start, s):
        for step in around(s):
            d, i = dkv_in(step), STEPS.index(step) * 3
            for slot, xs in enumerate(PEERS):
                j = here.at_x(xs)
                xsend[i + slot] = add16(dkv[k, d, j], dmate[d, j]).astype(BF16)
                start(xslot, i + slot, xs)

    def x_end(s):
        for step in around(s):
            d, i = here.at_z(step), STEPS.index(step) * 3
            for slot, xs in enumerate(PEERS):
                xslot(i + slot, xs).wait_recv()
            sums[i // 3] = add16(
                dkv[k, d, x], dmate[d, x], xrecv[i], xrecv[i + 1], xrecv[i + 2]
            )

    def grad_step(t):
        def zero(start):
            if t < DEEP:
                if t:
                    wide_step(start, t - 1, -1)
                wide_step(start, t, 1)
            elif t == DEEP:
                d = dkv_in(0)
                for i in (3, 2 * DEEP - 2):
                    for h in range(2):
                        zslot(2 * i + h, 2, 1 if i == 3 else -1).wait_recv()
                last = pl.ds(4 * (2 * DEEP - 2), 4)
                sums[0:4] = add16(dkv[k, d], dmate[d], zrecv[12:16], zrecv[last])
                for slot, xs in enumerate(PEERS):
                    xsend[slot] = sums[here.at_x(xs)].astype(BF16)
                    start(xslot, slot, xs)
            else:
                for slot, xs in enumerate(PEERS):
                    xslot(slot, xs).wait_recv()
                tsend[...] = (sums[x] + add16(xrecv[0], xrecv[1], xrecv[2])).astype(BF16)

        def one(start):
            if t <= DEEP:
                x_start(start, DEEP - t)
            if t >= 1:
                x_end(DEEP + 1 - t)
                if t <= DEEP:
                    thin_step(start, t - 1, 1)
                    if t > 1:
                        thin_step(start, t - 2, -1)
                else:
                    zslot(DEEP - 1, 1, 1).wait_recv()
                    zslot(2 * DEEP - 2, 1, -1).wait_recv()
                    total = sums[0] + add16(zrecv[DEEP - 1], zrecv[2 * DEEP - 2])
                    tsend[...] = total.astype(BF16)

        by_core(zero, one)
        if t == DEEP + 1:
            go(twin)

    twin = remote(tsend, trecv, s_t.at[0], r_t.at[0], here.twin)

    def spot(which, step):
        head = here.at_y(step) // 2
        return kvg_ref.at[which, :, pl.ds(pl.multiple_of(head * HEAD, HEAD), HEAD)]

    mine = pltpu.make_async_copy(kg, spot(k, 0), s_l.at[2])

    def spread():
        twin.wait_recv()
        kg[...] = add16(tsend[...], trecv[...]).astype(BF16)
        for i, step in enumerate((4, 2, 6)):
            go(remote(kg, spot(k, 0), s_c.at[i], r_c.at[i], here.dev_y(step)))
        go(remote(kg, spot(k, 0), s_cm.at[3], r_cm.at[3], here.mate))
        mine.start()

    def spread_end():
        order = (4, 2, 6)
        for i in (1, 2, 0):
            there = spot(k, -order[i])
            remote(kg, there, s_c.at[i], r_c.at[i], here.dev_y(-order[i])).wait_recv()
            go(remote(there, there, s_cm.at[i], r_cm.at[i], here.mate))
        remote(kg, spot(1 - k, 0), s_cm.at[3], r_cm.at[3], here.mate).wait_recv()
        for i in (1, 2, 0):
            there = spot(1 - k, order[i])
            remote(there, there, s_cm.at[i], r_cm.at[i], here.mate).wait_recv()
        mine.wait()

    ret_one, ret_begin, ret_finish = exchange(here, back, ret_ref, s_ret, r_ret)
    ret_local = pltpu.make_async_copy(back.at[e], ret_ref.at[e], s_l.at[3])

    def experts_out(s):
        blocks = [here.at_y(step) for step in around(s)]
        rows = len(blocks) * YROWS
        near = first_local(rows)

        def both(m, weight, transposed):
            parts = [
                jnp.concatenate([full[0, y, m], full[1, y, m]], axis=1) for y in blocks
            ]
            whole = jnp.concatenate(parts, axis=0)
            f = dot_t if transposed else dot
            return jnp.where(near, f(whole, weight[0]), f(whole, weight[1]))

        route_out = both(0, down_ref, False).astype(BF16)
        route_in = (both(1, gate_ref, True) + both(2, up_ref, True)).astype(BF16)
        quarters = [route_out[:, :128], route_out[:, 128:], route_in[:, :128], route_in[:, 128:]]
        out = dot(pack_table(True, rows), jnp.concatenate(quarters, axis=0)).astype(BF16)
        for b, y in enumerate(blocks):
            for i in range(NX):
                dest = source(y, i)
                r = (b * NX + i) * SLAB
                back[dest] = out[r : r + SLAB]
                offset = (dest + NE - e) % NE

                @pl.when(offset != 0)
                def _():
                    ret_one(offset).start()

                @pl.when(offset == 0)
                def _():
                    ret_local.start()

    def each_y(s):
        for m in range(3):
            y_step(s, m)

    def drain(sem, ref):
        remote(ref, ref, sem.at[0], sem.at[0], here.mate).wait_send()

    kv_step(0)
    begin(1, 17)
    kv_step(1)
    begin(17, NE)
    for c in loads:
        c.wait()
    stack()
    kv_step(2)
    kv_ready(0)
    forward(0)
    kv_step(3)
    local.wait()
    finish()
    pack()
    product(0)
    kv_step(4)
    product(1)
    y_step(0, 0)
    product(2)
    y_step(0, 1)
    kv_step(5)
    y_step(0, 2)
    kv_ready(1)
    forward(-1)
    forward(1)
    kv_step(6)
    each_y(1)
    kv_ready(2)
    forward(-2)
    forward(2)
    each_y(2)
    kv_ready(3)
    forward(-3)
    forward(3)
    kv_ready(4)
    forward(4)
    normalize()
    each_y(3)
    backward(4)
    backward(-3)
    grad_step(0)
    activate()
    backward(3)
    grad_step(1)
    backward(-2)
    gather_step(1)
    backward(2)
    grad_step(2)
    backward(-1)
    gather_step(2)
    backward(1)
    grad_step(3)
    backward(0)
    gather_step(3)
    grad_step(4)
    gather_ready(0)
    experts_out(0)
    gather_step(4)
    gather_ready(1)
    experts_out(1)
    grad_step(5)
    gather_ready(2)
    experts_out(2)
    gather_ready(3)
    spread()
    experts_out(3)
    gather_ready(4)
    experts_out(4)
    query_grad()
    combine_tables(ids_ref, tab_ref)
    spread_end()
    ret_finish()
    ret_local.wait()
    combine(gain_ref, tab_ref, ret_ref, mo_ref, ig_ref)
    for c in sends:
        c.wait_send()
    drain(s_km, kv.at[k])
    drain(s_y, ysend)
    drain(s_g, full.at[k, pl.ds(0, 7)])
    drain(s_gm, full.at[k])
    drain(s_dm, dkv.at[1 - k])

    def drain_zero(start):
        drain(s_kx, kv.at[k, 0, pl.ds(0, 3)])
        drain(s_kz, kv.at[k, pl.ds(0, 7)])
        drain(s_z, zsend)
        drain(s_x, xsend.at[pl.ds(0, 3)])

    def drain_one(start):
        drain(s_kx, kv.at[k, :, pl.ds(0, 3)])
        drain(s_kz, kv.at[k, pl.ds(0, 7), 0])
        drain(s_z, zsend.at[pl.ds(0, 7)])
        drain(s_x, xsend)

    by_core(drain_zero, drain_one)


def vmem():
    return pl.BlockSpec(memory_space=pltpu.VMEM)


def dma(n):
    return pltpu.SemaphoreType.DMA((n,))


def call(kernel, outs, scratch, *args, specs=None, collective=None, name=None, flops=0):
    params = {"vmem_limit_bytes": VMEM_LIMIT}
    if collective is not None:
        params.update(collective_id=collective, has_side_effects=True)
    return pl.pallas_call(
        kernel,
        out_shape=outs,
        in_specs=specs or [vmem()] * len(args),
        out_specs=jax.tree.map(lambda o: vmem(), outs),
        scratch_shapes=scratch,
        compiler_params=pltpu.CompilerParams(**params),
        name=name,
    )(*args)


def shape(*dims, dtype=BF16):
    return jax.ShapeDtypeStruct(dims, dtype)


def body(q, key, val, do, x, g, ids, gain, gate, up, down):
    ids, gain = ids.T, gain.T
    hbm = pl.BlockSpec(memory_space=pl.ANY)
    heads = q.shape[1] // HEAD
    width = heads * TOK
    yslab, zslab, block = (YROWS, HALF), (NX, TOK, HEAD), (TOK, HEAD)

    def f32(*dims):
        return pltpu.VMEM(dims, F32)

    def b16(*dims):
        return pltpu.VMEM(dims, BF16)

    sems = [5, 4, 1, 1, 1, 24, 1, 32, 1, 8, 3, 3, 1, 21, 1, 21, 1, 8]
    sems += [1, 8, 1, 14, 1, 24, 1, 1, 3, 3, 4, 4, 1, 1]
    attn_out, dq, moe_out, input_grad, kvg = call(
        layer_kernel,
        (shape(*q.shape), shape(*q.shape), shape(*x.shape), shape(*x.shape),
         shape(2, TOK, 4 * HEAD)),
        [
            b16(NE, SLAB, 128), b16(6, TOK, NE * SLAB),
            b16(*q.shape), b16(*do.shape), b16(*gate.shape), b16(*up.shape), b16(*down.shape),
            b16(NE, SLAB, 128), b16(NE, SLAB, 128), b16(2, ROWS, 256),
            b16(2, NY, 3, *yslab), b16(NY, 3, *yslab), b16(21, *yslab), b16(21, *yslab),
            b16(2, NY, 3, *yslab),
            b16(2, NZ, *zslab), b16(width, HEAD), b16(width, HEAD), b16(NZ, KEYS, width),
            f32(NZ, 1, width), f32(1, width), f32(1, width), f32(HEAD, width), f32(1, width),
            f32(HEAD, width),
            b16(2, NZ, *zslab), b16(NZ, *zslab), b16(28, *block), b16(28, *block), f32(8, *block),
            b16(24, *block), b16(24, *block), b16(*block), b16(*block), b16(*block),
            b16(NE, SLAB, 128),
        ]
        + [dma(n) for n in sems],
        ids, gain, x, g, key, val, q, do, gate, up, down,
        specs=[vmem()] * 4 + [hbm] * 7, collective=0, name="layer",
    )
    moe_out, input_grad, key_grad, value_grad, attn_out, dq = call(
        close_kernel,
        (shape(TOK, 256), shape(TOK, 256), shape(TOK, 512), shape(TOK, 512),
         shape(*q.shape), shape(*q.shape)), [],
        moe_out, input_grad, kvg, attn_out, dq, name="close",
    )
    return attn_out, dq, key_grad, value_grad, moe_out, input_grad


def solution(mesh):
    rows, both = P("exp", None), P("exp", "ctx")
    return jax.shard_map(
        body,
        mesh=mesh,
        in_specs=(
            both, rows, rows, both, both, both, rows, rows,
            P("exp", "ctx", None), P("exp", "ctx", None), P("exp", None, "ctx"),
        ),
        out_specs=(both, both, rows, rows, both, both),
        check_vma=False,
    )
```
